128 devices in a mesh: out: 8 (over y_lo, z), in: 16 (over y_hi, x, core).
Axes of the slice: x: 4, y: 4 (y_hi: 2, y_lo: 2; y = y_hi * 2 + y_lo), z: 4, core: 2. Of those that a mesh axis runs over, the one named last changes fastest.
Arguments:
- markov: bfloat16 [63, 2048, 2048], P(None, 'out', 'in'), may hold values from -0.03125 to 0.03125
- probes: bfloat16 [128, 32, 2048], P('out', None, 'in'), may hold values from -6 to 6
- pattern: int32 [32, 16], P('out', 'in'), may hold values 0 or 1
Outputs:
- sketch: bfloat16 [32, 2048, 128], P(None, 'out')
- corange: float32 [128, 32, 2048], P('out', None, 'in')
- gram_matrix: float32 [128, 128], replicated
The draws below stay inside these ranges and needn't reach their ends.
All inputs are finite; a program needn't handle non-finite values. No bound on the sum of `pattern` on one device may be relied on, other than what follows from the above.
Results may differ from the reference program's by a relative error of at most 0.015.
Values may be sent and summed in bfloat16 or wider, within the bound.
A program may use at most 128 MiB of HBM per device.

```python
import jax
import jax.numpy as jnp
from jax import lax

OUTPUT_CHANNELS = 2048
M = 2048
S = 128
BO = 64
BI = 128
R = 32
C = 32
LAGS = 63


def set_ends(array, own_key, least, high):
    spot = [jax.random.randint(jax.random.fold_in(own_key, axis), (), 0, length) for axis, length in enumerate(array.shape)]
    widest = array.shape.index(max(array.shape))
    next_to = spot[:widest] + [(spot[widest] + 1) % array.shape[widest]] + spot[widest + 1:]
    return array.at[tuple(spot)].set(least).at[tuple(next_to)].set(high)


def levels(rng, extent, cuts, low, largest):
    def one(axis_at, parts):
        draws = jax.random.uniform(jax.random.fold_in(jax.random.fold_in(rng, 6), axis_at), (parts,), jnp.float32, low / len(cuts), largest / len(cuts))
        return jnp.repeat(jnp.exp(draws), extent[axis_at] // parts).reshape((-1,) + (1,) * (len(extent) - axis_at - 1))

    factor_of = one(*cuts[0])
    for cut in cuts[1:]:
        factor_of = factor_of * one(*cut)
    return factor_of


def normal_values(key, dims, deviation, most, cuts=(), kind=jnp.bfloat16):
    gain = levels(key, dims, cuts, -0.22, 0.18) if cuts else 1.0
    array = jax.random.normal(key, dims, jnp.float32) * deviation * gain
    return jnp.minimum(jnp.maximum(array, -most), most).astype(kind)


def setup_inputs(seed: int = 0) -> dict:
    seeds = jax.random.split(jax.random.key(seed), 4)
    return {
        "markov": normal_values(seeds[0], (LAGS, OUTPUT_CHANNELS, M), (C * M // 2) ** -0.5, 0.03125, ((1, 8), (2, 16))),
        "probes": normal_values(seeds[1], (S, C, M), 1.0, 6.0, ((0, 8), (2, 16))),
        "pattern": set_ends((jax.random.randint(seeds[2], (OUTPUT_CHANNELS // BO, M // BI), 0, 2) < 1).astype(jnp.int32), jax.random.fold_in(seeds[2], 1), 0, 1),
    }


def reference(markov, probes, pattern):
    keeper = jnp.repeat(jnp.repeat(pattern, BO, axis=0), BI, axis=1).astype(jnp.bfloat16)
    masked = (markov * keeper[None]).astype(jnp.float32)
    panel_list = probes.astype(jnp.float32)

    def sketch_row(lag_row):
        window_span = lax.dynamic_slice_in_dim(masked, lag_row, C, 0)
        return jnp.einsum("wby,gwy->bg", window_span, panel_list, precision=lax.Precision.HIGHEST)

    raw = lax.map(sketch_row, jnp.arange(R, dtype=jnp.int32))
    sketch = raw.astype(jnp.bfloat16)
    sketch_wide = sketch.astype(jnp.float32)
    gram_matrix = jnp.einsum("ips,ipt->st", sketch_wide, sketch_wide, precision=lax.Precision.HIGHEST) / (R * OUTPUT_CHANNELS)

    def corange_col(lag_col):
        window_span = lax.dynamic_slice_in_dim(masked, lag_col, R, 0)
        return jnp.einsum("ipm,ips->sm", window_span, sketch_wide, precision=lax.Precision.HIGHEST)

    stacked_rows = lax.map(corange_col, jnp.arange(C, dtype=jnp.int32))
    corange = jnp.moveaxis(stacked_rows, 0, 1)
    return sketch, corange, gram_matrix
```

```python
import functools

import jax
import jax.numpy as jnp
from jax import lax
from jax.experimental import pallas as pl
from jax.experimental.pallas import tpu as pltpu
from jax.sharding import PartitionSpec as P

OUTPUT_CHANNELS = 2048
BO = 64
BI = 128
R = 32
C = 32

MESH = pl.DeviceIdType.MESH


def forward_panel(slab, panel_fragment):
    results = []
    for lag_row in range(R):
        window_span = slab[lag_row : lag_row + C]
        results.append(
            jnp.einsum(
                "wby,gwy->bg", window_span, panel_fragment, preferred_element_type=jnp.float32
            )
        )
    return jnp.stack(results, axis=0)


def backward_panel(slab, panel):
    results = []
    for lag_col in range(C):
        window_span = slab[lag_col : lag_col + R]
        results.append(
            jnp.einsum("ipm,ips->sm", window_span, panel, preferred_element_type=jnp.float32)
        )
    return jnp.stack(results, axis=1)


def exchange_kernel(axis, n, stride, gather, x_ref, y_ref, send_sem, recv_sem, local_sem):
    me = lax.axis_index(axis)
    pos = lax.rem(me // stride, n)
    base = me - pos * stride

    def member(k):
        return base + k * stride

    barrier = pltpu.get_barrier_semaphore()
    for d in range(1, n):
        peer = lax.rem(pos + d, n)
        pl.semaphore_signal(barrier, inc=1, device_id={axis: member(peer)}, device_id_type=MESH)
    pl.semaphore_wait(barrier, n - 1)

    own_src = x_ref if gather else x_ref.at[pos]
    local = pltpu.make_async_copy(own_src, y_ref.at[pos], local_sem)
    local.start()
    copies = []
    for d in range(1, n):
        peer = lax.rem(pos + d, n)
        src = x_ref if gather else x_ref.at[peer]
        copy = pltpu.make_async_remote_copy(
            src_ref=src,
            dst_ref=y_ref.at[pos],
            send_sem=send_sem.at[d],
            recv_sem=recv_sem.at[d],
            device_id={axis: member(peer)},
            device_id_type=MESH,
        )
        copy.start()
        copies.append(copy)
    local.wait()
    for copy in copies:
        copy.wait()


def exchange(x, axis, n, stride, gather, cid):
    out_shape = (n,) + (x.shape if gather else x.shape[1:])
    return pl.pallas_call(
        functools.partial(exchange_kernel, axis, n, stride, gather),
        out_shape=jax.ShapeDtypeStruct(out_shape, x.dtype),
        in_specs=[pl.BlockSpec(memory_space=pl.ANY)],
        out_specs=pl.BlockSpec(memory_space=pl.ANY),
        scratch_shapes=[
            pltpu.SemaphoreType.DMA((n,)),
            pltpu.SemaphoreType.DMA((n,)),
            pltpu.SemaphoreType.DMA(()),
        ],
        compiler_params=pltpu.CompilerParams(collective_id=cid, has_side_effects=True),
    )(x)


def shards(n_out, n_in, markov, probes, pattern):
    keeper = jnp.repeat(jnp.repeat(pattern, BO, axis=0), BI, axis=1).astype(jnp.bfloat16)
    masked = markov * keeper[None]
    gathered = exchange(probes, "out", n_out, 1, True, 0)
    panel = gathered.reshape((-1,) + probes.shape[1:])
    raw_part = forward_panel(masked, panel)
    rows, width, sk = raw_part.shape
    pieces = exchange(
        raw_part.astype(jnp.bfloat16).reshape(n_in, rows // n_in, width, sk), "in", n_in, 1, False, 1
    )
    mine = jnp.sum(pieces.astype(jnp.float32), axis=0).astype(jnp.bfloat16)
    sketch = exchange(mine, "in", n_in, 1, True, 2).reshape(rows, width, sk)
    local_gram = jnp.einsum("ips,ipt->st", sketch, sketch, preferred_element_type=jnp.float32)
    gram_parts = exchange(local_gram, "out", n_out, 1, True, 3)
    gram_matrix = jnp.sum(gram_parts, axis=0) / (R * OUTPUT_CHANNELS)
    co_part = backward_panel(masked, sketch).astype(jnp.bfloat16)
    s_all = co_part.shape[0]
    co_pieces = exchange(
        co_part.reshape((n_out, s_all // n_out) + co_part.shape[1:]), "out", n_out, 1, False, 4
    )
    corange = jnp.sum(co_pieces.astype(jnp.float32), axis=0)
    return (sketch, corange, gram_matrix)


def solution(mesh):
    return jax.shard_map(
        functools.partial(shards, mesh.shape["out"], mesh.shape["in"]),
        mesh=mesh,
        in_specs=(P(None, "out", "in"), P("out", None, "in"), P("out", "in")),
        out_specs=(P(None, "out", None), P("out", None, "in"), P()),
        check_vma=False,
    )
```

```python
import functools

import jax
import jax.numpy as jnp
from jax import lax
from jax.experimental import pallas as pl
from jax.experimental.pallas import tpu as pltpu
from jax.sharding import PartitionSpec as P

OUTPUT_CHANNELS = 2048
BO = 64
BI = 128
R = 32
C = 32

MESH = pl.DeviceIdType.MESH


def forward_kernel(pair_ref, probe_ref, out_ref):
    rows, width, sk = out_ref.shape
    steps = probe_ref.shape[0]
    block = 2

    def body(b, carry):
        i0 = b * block
        acc = jnp.zeros((block * width, sk), jnp.float32)
        for t in range(steps):
            lhs = pair_ref[pl.ds(i0 + 2 * t, block)].reshape(block * width, pair_ref.shape[2])
            acc = acc + jnp.dot(lhs, probe_ref[t], preferred_element_type=jnp.float32)
        out_ref[pl.ds(i0, block)] = acc.reshape(block, width, sk)
        return carry

    lax.fori_loop(0, rows // block, body, 0)


def forward_panel(pair, probe_pairs, rows):
    width = pair.shape[1]
    sk = probe_pairs.shape[2]
    return pl.pallas_call(
        forward_kernel,
        out_shape=jax.ShapeDtypeStruct((rows, width, sk), jnp.float32),
        in_specs=[pl.BlockSpec(memory_space=pltpu.VMEM)] * 2,
        out_specs=pl.BlockSpec(memory_space=pltpu.VMEM),
        compiler_params=pltpu.CompilerParams(vmem_limit_bytes=60 * 1024 * 1024),
    )(pair, probe_pairs)


def backward_kernel(mt_ref, sketch_ref, out_ref):
    cols, m_width, sk = out_ref.shape
    rows = sketch_ref.shape[0]
    block = 8
    for jb in range(cols // block):
        def body(i, acc):
            lhs = mt_ref[pl.ds(jb * block + i, block)].reshape(block * m_width, mt_ref.shape[2])
            return acc + jnp.dot(lhs, sketch_ref[i], preferred_element_type=jnp.float32)

        acc = lax.fori_loop(0, rows, body, jnp.zeros((block * m_width, sk), jnp.float32))
        out_ref[jb * block : (jb + 1) * block] = acc.reshape(block, m_width, sk)


def backward_panel(mt, sketch, cols):
    m_width = mt.shape[1]
    sk = sketch.shape[2]
    return pl.pallas_call(
        backward_kernel,
        out_shape=jax.ShapeDtypeStruct((cols, m_width, sk), jnp.float32),
        in_specs=[pl.BlockSpec(memory_space=pltpu.VMEM)] * 2,
        out_specs=pl.BlockSpec(memory_space=pltpu.VMEM),
        compiler_params=pltpu.CompilerParams(vmem_limit_bytes=60 * 1024 * 1024),
    )(mt, sketch)


def exchange_kernel(axis, n, stride, gather, x_ref, y_ref, send_sem, recv_sem, local_sem):
    me = lax.axis_index(axis)
    pos = lax.rem(me // stride, n)
    base = me - pos * stride

    def member(k):
        return base + k * stride

    barrier = pltpu.get_barrier_semaphore()
    for d in range(1, n):
        peer = lax.rem(pos + d, n)
        pl.semaphore_signal(barrier, inc=1, device_id={axis: member(peer)}, device_id_type=MESH)
    pl.semaphore_wait(barrier, n - 1)

    own_src = x_ref if gather else x_ref.at[pos]
    local = pltpu.make_async_copy(own_src, y_ref.at[pos], local_sem)
    local.start()
    copies = []
    for d in range(1, n):
        peer = lax.rem(pos + d, n)
        src = x_ref if gather else x_ref.at[peer]
        copy = pltpu.make_async_remote_copy(
            src_ref=src,
            dst_ref=y_ref.at[pos],
            send_sem=send_sem.at[d],
            recv_sem=recv_sem.at[d],
            device_id={axis: member(peer)},
            device_id_type=MESH,
        )
        copy.start()
        copies.append(copy)
    local.wait()
    for copy in copies:
        copy.wait()


def exchange(x, axis, n, stride, gather, cid):
    out_shape = (n,) + (x.shape if gather else x.shape[1:])
    return pl.pallas_call(
        functools.partial(exchange_kernel, axis, n, stride, gather),
        out_shape=jax.ShapeDtypeStruct(out_shape, x.dtype),
        in_specs=[pl.BlockSpec(memory_space=pl.ANY)],
        out_specs=pl.BlockSpec(memory_space=pl.ANY),
        scratch_shapes=[
            pltpu.SemaphoreType.DMA((n,)),
            pltpu.SemaphoreType.DMA((n,)),
            pltpu.SemaphoreType.DMA(()),
        ],
        compiler_params=pltpu.CompilerParams(collective_id=cid, has_side_effects=True),
    )(x)


def shards(n_out, n_in, markov, probes, pattern):
    keeper = jnp.repeat(jnp.repeat(pattern, BO, axis=0), BI, axis=1).astype(jnp.bfloat16)
    masked = markov * keeper[None]
    pair = jnp.concatenate([masked[:-1], masked[1:]], axis=2)
    mt = jnp.swapaxes(masked, 1, 2)
    gathered = exchange(probes, "out", n_out, 1, True, 0)
    panel = gathered.reshape((-1,) + probes.shape[1:])
    s_all, cols, m_width = panel.shape
    probe_pairs = jnp.swapaxes(panel.reshape(s_all, cols // 2, 2 * m_width), 0, 1).swapaxes(1, 2)
    raw_part = forward_panel(pair, probe_pairs, R)
    rows, width, sk = raw_part.shape
    pieces = exchange(
        raw_part.astype(jnp.bfloat16).reshape(n_in, rows // n_in, width, sk), "in", n_in, 1, False, 1
    )
    mine = jnp.sum(pieces.astype(jnp.float32), axis=0).astype(jnp.bfloat16)
    sketch = exchange(mine, "in", n_in, 1, True, 2).reshape(rows, width, sk)
    local_gram = jnp.einsum("ips,ipt->st", sketch, sketch, preferred_element_type=jnp.float32)
    gram_parts = exchange(local_gram, "out", n_out, 1, True, 3)
    gram_matrix = jnp.sum(gram_parts, axis=0) / (R * OUTPUT_CHANNELS)
    co_t = backward_panel(mt, sketch, cols)
    co_part = jnp.transpose(co_t.astype(jnp.bfloat16), (2, 0, 1))
    co_pieces = exchange(
        co_part.reshape((n_out, s_all // n_out) + co_part.shape[1:]), "out", n_out, 1, False, 4
    )
    corange = jnp.sum(co_pieces.astype(jnp.float32), axis=0)
    return (sketch, corange, gram_matrix)


def solution(mesh):
    return jax.shard_map(
        functools.partial(shards, mesh.shape["out"], mesh.shape["in"]),
        mesh=mesh,
        in_specs=(P(None, "out", "in"), P("out", None, "in"), P("out", "in")),
        out_specs=(P(None, "out", None), P("out", None, "in"), P()),
        check_vma=False,
    )
```

```python
import functools

import jax
import jax.numpy as jnp
from jax import lax
from jax.experimental import pallas as pl
from jax.experimental.pallas import tpu as pltpu
from jax.sharding import PartitionSpec as P

OUTPUT_CHANNELS = 2048
BO = 64
BI = 128
R = 32
C = 32

MESH = pl.DeviceIdType.MESH


def forward_kernel(m_ref, probe_ref, out_ref):
    rows, width, sk = out_ref.shape
    steps = probe_ref.shape[0]
    m_width = m_ref.shape[2]
    block = 2

    def body(b, carry):
        i0 = b * block
        acc = jnp.zeros((block * width, sk), jnp.float32)
        for t in range(steps):
            lo = m_ref[pl.ds(i0 + 2 * t, block)].reshape(block * width, m_width)
            hi = m_ref[pl.ds(i0 + 2 * t + 1, block)].reshape(block * width, m_width)
            lhs = jnp.concatenate([lo, hi], axis=1)
            acc = acc + jnp.dot(lhs, probe_ref[t], preferred_element_type=jnp.float32)
        out_ref[pl.ds(i0, block)] = acc.reshape(block, width, sk)
        return carry

    lax.fori_loop(0, rows // block, body, 0)


def forward_panel(pair, probe_pairs, rows):
    width = pair.shape[1]
    sk = probe_pairs.shape[2]
    return pl.pallas_call(
        forward_kernel,
        out_shape=jax.ShapeDtypeStruct((rows, width, sk), jnp.float32),
        in_specs=[pl.BlockSpec(memory_space=pltpu.VMEM)] * 2,
        out_specs=pl.BlockSpec(memory_space=pltpu.VMEM),
        compiler_params=pltpu.CompilerParams(vmem_limit_bytes=60 * 1024 * 1024),
    )(pair, probe_pairs)


def backward_kernel(mt_ref, sketch_ref, out_ref):
    cols, m_width, sk = out_ref.shape
    rows = sketch_ref.shape[0]
    block = 2
    for jb in range(cols // block):
        def body(i, acc):
            lhs = mt_ref[pl.ds(jb * block + i, block)].reshape(block * m_width, mt_ref.shape[2])
            return acc + jnp.dot(lhs, sketch_ref[i], preferred_element_type=jnp.float32)

        acc = lax.fori_loop(0, rows, body, jnp.zeros((block * m_width, sk), jnp.float32))
        out_ref[jb * block : (jb + 1) * block] = acc.reshape(block, m_width, sk)


def backward_panel(mt, sketch, cols):
    m_width = mt.shape[1]
    sk = sketch.shape[2]
    return pl.pallas_call(
        backward_kernel,
        out_shape=jax.ShapeDtypeStruct((cols, m_width, sk), jnp.float32),
        in_specs=[pl.BlockSpec(memory_space=pltpu.VMEM)] * 2,
        out_specs=pl.BlockSpec(memory_space=pltpu.VMEM),
        compiler_params=pltpu.CompilerParams(vmem_limit_bytes=60 * 1024 * 1024),
    )(mt, sketch)


def exchange_kernel(axis, n, stride, gather, x_ref, y_ref, send_sem, recv_sem, local_sem):
    me = lax.axis_index(axis)
    pos = lax.rem(me // stride, n)
    base = me - pos * stride

    def member(k):
        return base + k * stride

    barrier = pltpu.get_barrier_semaphore()
    for d in range(1, n):
        peer = lax.rem(pos + d, n)
        pl.semaphore_signal(barrier, inc=1, device_id={axis: member(peer)}, device_id_type=MESH)
    pl.semaphore_wait(barrier, n - 1)

    own_src = x_ref if gather else x_ref.at[pos]
    local = pltpu.make_async_copy(own_src, y_ref.at[pos], local_sem)
    local.start()
    copies = []
    for d in range(1, n):
        peer = lax.rem(pos + d, n)
        src = x_ref if gather else x_ref.at[peer]
        copy = pltpu.make_async_remote_copy(
            src_ref=src,
            dst_ref=y_ref.at[pos],
            send_sem=send_sem.at[d],
            recv_sem=recv_sem.at[d],
            device_id={axis: member(peer)},
            device_id_type=MESH,
        )
        copy.start()
        copies.append(copy)
    local.wait()
    for copy in copies:
        copy.wait()


def exchange(x, axis, n, stride, gather, cid):
    out_shape = (n,) + (x.shape if gather else x.shape[1:])
    return pl.pallas_call(
        functools.partial(exchange_kernel, axis, n, stride, gather),
        out_shape=jax.ShapeDtypeStruct(out_shape, x.dtype),
        in_specs=[pl.BlockSpec(memory_space=pl.ANY)],
        out_specs=pl.BlockSpec(memory_space=pl.ANY),
        scratch_shapes=[
            pltpu.SemaphoreType.DMA((n,)),
            pltpu.SemaphoreType.DMA((n,)),
            pltpu.SemaphoreType.DMA(()),
        ],
        compiler_params=pltpu.CompilerParams(collective_id=cid, has_side_effects=True),
    )(x)


def shards(n_out, n_in, markov, probes, pattern):
    keeper = jnp.repeat(jnp.repeat(pattern, BO, axis=0), BI, axis=1).astype(jnp.bfloat16)
    masked = markov * keeper[None]
    mt = jnp.swapaxes(masked, 1, 2)
    gathered = exchange(probes, "out", n_out, 1, True, 0)
    panel = gathered.reshape((-1,) + probes.shape[1:])
    s_all, cols, m_width = panel.shape
    probe_pairs = jnp.swapaxes(panel.reshape(s_all, cols // 2, 2 * m_width), 0, 1).swapaxes(1, 2)
    raw_part = forward_panel(masked, probe_pairs, R)
    rows, width, sk = raw_part.shape
    half = exchange(
        raw_part.astype(jnp.bfloat16).reshape(2, rows // 2, width, sk), "in", 2, 1, False, 1
    )
    half = jnp.sum(half.astype(jnp.float32), axis=0).astype(jnp.bfloat16)
    chips = n_in // 2
    pieces = exchange(half.reshape(chips, rows // n_in, width, sk), "in", chips, 2, False, 2)
    mine = jnp.sum(pieces.astype(jnp.float32), axis=0).astype(jnp.bfloat16)
    half_sketch = exchange(mine, "in", chips, 2, True, 3).reshape(rows // 2, width, sk)
    sketch = exchange(half_sketch, "in", 2, 1, True, 5).reshape(rows, width, sk)
    local_gram = jnp.einsum("ips,ipt->st", sketch, sketch, preferred_element_type=jnp.float32)
    gram_parts = exchange(local_gram, "out", n_out, 1, True, 6)
    gram_matrix = jnp.sum(gram_parts, axis=0) / (R * OUTPUT_CHANNELS)
    co_t = backward_panel(mt, sketch, cols)
    co_part = jnp.transpose(co_t.astype(jnp.bfloat16), (2, 0, 1))
    co_pieces = exchange(
        co_part.reshape((n_out, s_all // n_out) + co_part.shape[1:]), "out", n_out, 1, False, 4
    )
    corange = jnp.sum(co_pieces.astype(jnp.float32), axis=0)
    return (sketch, corange, gram_matrix)


def solution(mesh):
    return jax.shard_map(
        functools.partial(shards, mesh.shape["out"], mesh.shape["in"]),
        mesh=mesh,
        in_specs=(P(None, "out", "in"), P("out", None, "in"), P("out", "in")),
        out_specs=(P(None, "out", None), P("out", None, "in"), P()),
        check_vma=False,
    )
```

```python
import functools

import jax
import jax.numpy as jnp
from jax import lax
from jax.experimental import pallas as pl
from jax.experimental.pallas import tpu as pltpu
from jax.sharding import PartitionSpec as P

OUTPUT_CHANNELS = 2048
BO = 64
BI = 128
R = 32
C = 32

MESH = pl.DeviceIdType.MESH


def forward_kernel(m_ref, probe_ref, out_ref):
    rows, width, sk = out_ref.shape
    steps = probe_ref.shape[0]
    m_width = m_ref.shape[2]
    block = 2

    def body(b, carry):
        i0 = b * block
        acc = jnp.zeros((block * width, sk), jnp.float32)
        for t in range(steps):
            lo = m_ref[pl.ds(i0 + 2 * t, block)].reshape(block * width, m_width)
            hi = m_ref[pl.ds(i0 + 2 * t + 1, block)].reshape(block * width, m_width)
            lhs = jnp.concatenate([lo, hi], axis=1)
            acc = acc + jnp.dot(lhs, probe_ref[t], preferred_element_type=jnp.float32)
        out_ref[pl.ds(i0, block)] = acc.reshape(block, width, sk)
        return carry

    lax.fori_loop(0, rows // block, body, 0)


def forward_panel(pair, probe_pairs, rows):
    width = pair.shape[1]
    sk = probe_pairs.shape[2]
    return pl.pallas_call(
        forward_kernel,
        out_shape=jax.ShapeDtypeStruct((rows, width, sk), jnp.float32),
        in_specs=[pl.BlockSpec(memory_space=pltpu.VMEM)] * 2,
        out_specs=pl.BlockSpec(memory_space=pltpu.VMEM),
        compiler_params=pltpu.CompilerParams(vmem_limit_bytes=60 * 1024 * 1024),
    )(pair, probe_pairs)


def backward_kernel(mt_ref, sketch_ref, out_ref):
    cols, m_width, sk = out_ref.shape
    rows = sketch_ref.shape[0]
    block = 4

    def body(b, carry):
        j0 = b * block
        acc = jnp.zeros((block * m_width, sk), jnp.float32)
        for i in range(rows):
            lhs = mt_ref[pl.ds(j0 + i, block)].reshape(block * m_width, mt_ref.shape[2])
            acc = acc + jnp.dot(lhs, sketch_ref[i], preferred_element_type=jnp.float32)
        out_ref[pl.ds(j0, block)] = acc.reshape(block, m_width, sk)
        return carry

    lax.fori_loop(0, cols // block, body, 0)


def prep_kernel(markov_ref, keeper_ref, masked_ref, mt_ref):
    keeper = keeper_ref[...]

    def body(k, carry):
        value = markov_ref[k] * keeper
        masked_ref[k] = value
        mt_ref[k] = value.astype(jnp.float32).T.astype(mt_ref.dtype)
        return carry

    lax.fori_loop(0, markov_ref.shape[0], body, 0)


def prep(markov, keeper):
    lags, width, m_width = markov.shape
    return pl.pallas_call(
        prep_kernel,
        out_shape=(
            jax.ShapeDtypeStruct((lags, width, m_width), markov.dtype),
            jax.ShapeDtypeStruct((lags, m_width, width), markov.dtype),
        ),
        in_specs=[pl.BlockSpec(memory_space=pltpu.VMEM)] * 2,
        out_specs=(pl.BlockSpec(memory_space=pltpu.VMEM),) * 2,
        compiler_params=pltpu.CompilerParams(vmem_limit_bytes=60 * 1024 * 1024),
    )(markov, keeper)


def backward_panel(mt, sketch, cols):
    m_width = mt.shape[1]
    sk = sketch.shape[2]
    return pl.pallas_call(
        backward_kernel,
        out_shape=jax.ShapeDtypeStruct((cols, m_width, sk), jnp.float32),
        in_specs=[pl.BlockSpec(memory_space=pltpu.VMEM)] * 2,
        out_specs=pl.BlockSpec(memory_space=pltpu.VMEM),
        compiler_params=pltpu.CompilerParams(vmem_limit_bytes=60 * 1024 * 1024),
    )(mt, sketch)


def exchange_kernel(axis, n, stride, gather, x_ref, y_ref, send_sem, recv_sem, local_sem):
    me = lax.axis_index(axis)
    pos = lax.rem(me // stride, n)
    base = me - pos * stride

    def member(k):
        return base + k * stride

    barrier = pltpu.get_barrier_semaphore()
    for d in range(1, n):
        peer = lax.rem(pos + d, n)
        pl.semaphore_signal(barrier, inc=1, device_id={axis: member(peer)}, device_id_type=MESH)
    pl.semaphore_wait(barrier, n - 1)

    own_src = x_ref if gather else x_ref.at[pos]
    local = pltpu.make_async_copy(own_src, y_ref.at[pos], local_sem)
    local.start()
    copies = []
    for d in range(1, n):
        peer = lax.rem(pos + d, n)
        src = x_ref if gather else x_ref.at[peer]
        copy = pltpu.make_async_remote_copy(
            src_ref=src,
            dst_ref=y_ref.at[pos],
            send_sem=send_sem.at[d],
            recv_sem=recv_sem.at[d],
            device_id={axis: member(peer)},
            device_id_type=MESH,
        )
        copy.start()
        copies.append(copy)
    local.wait()
    for copy in copies:
        copy.wait()


def exchange(x, axis, n, stride, gather, cid):
    out_shape = (n,) + (x.shape if gather else x.shape[1:])
    return pl.pallas_call(
        functools.partial(exchange_kernel, axis, n, stride, gather),
        out_shape=jax.ShapeDtypeStruct(out_shape, x.dtype),
        in_specs=[pl.BlockSpec(memory_space=pl.ANY)],
        out_specs=pl.BlockSpec(memory_space=pl.ANY),
        scratch_shapes=[
            pltpu.SemaphoreType.DMA((n,)),
            pltpu.SemaphoreType.DMA((n,)),
            pltpu.SemaphoreType.DMA(()),
        ],
        compiler_params=pltpu.CompilerParams(collective_id=cid, has_side_effects=True),
    )(x)


def shards(n_out, n_in, markov, probes, pattern):
    keeper = jnp.repeat(jnp.repeat(pattern, BO, axis=0), BI, axis=1).astype(jnp.bfloat16)
    masked, mt = prep(markov, keeper)
    gathered = exchange(probes, "out", n_out, 1, True, 0)
    panel = gathered.reshape((-1,) + probes.shape[1:])
    s_all, cols, m_width = panel.shape
    probe_pairs = jnp.swapaxes(panel.reshape(s_all, cols // 2, 2 * m_width), 0, 1).swapaxes(1, 2)
    raw_part = forward_panel(masked, probe_pairs, R)
    rows, width, sk = raw_part.shape
    pieces = exchange(
        raw_part.astype(jnp.bfloat16).reshape(n_in, rows // n_in, width, sk), "in", n_in, 1, False, 1
    )
    mine = jnp.sum(pieces.astype(jnp.float32), axis=0).astype(jnp.bfloat16)
    sketch = exchange(mine, "in", n_in, 1, True, 2).reshape(rows, width, sk)
    local_gram = jnp.einsum("ips,ipt->st", sketch, sketch, preferred_element_type=jnp.float32)
    co_t = backward_panel(mt, sketch, cols)
    co_part = jnp.transpose(co_t.astype(jnp.bfloat16), (2, 0, 1))
    per = s_all // n_out
    gram_rows = local_gram.shape[0] * local_gram.shape[1] // (cols * m_width)
    gram_block = local_gram.astype(jnp.bfloat16).reshape(1, gram_rows, cols, m_width)
    send = jnp.concatenate(
        [co_part.reshape(n_out, per, cols, m_width), jnp.broadcast_to(gram_block, (n_out, gram_rows, cols, m_width))],
        axis=1,
    )
    got = exchange(send, "out", n_out, 1, False, 4).astype(jnp.float32)
    corange = jnp.sum(got[:, :per], axis=0)
    gram_matrix = jnp.sum(got[:, per:], axis=0).reshape(local_gram.shape) / (R * OUTPUT_CHANNELS)
    return (sketch, corange, gram_matrix)


def solution(mesh):
    return jax.shard_map(
        functools.partial(shards, mesh.shape["out"], mesh.shape["in"]),
        mesh=mesh,
        in_specs=(P(None, "out", "in"), P("out", None, "in"), P("out", "in")),
        out_specs=(P(None, "out", None), P("out", None, "in"), P()),
        check_vma=False,
    )
```

```python
import functools

import jax
import jax.numpy as jnp
from jax import lax
from jax.experimental import pallas as pl
from jax.experimental.pallas import tpu as pltpu
from jax.sharding import PartitionSpec as P

OUTPUT_CHANNELS = 2048
BO = 64
BI = 128
R = 32
C = 32

MESH = pl.DeviceIdType.MESH


def forward_kernel(m_ref, probe_ref, out_ref):
    rows, width, sk = out_ref.shape
    steps = probe_ref.shape[0]
    m_width = m_ref.shape[2]
    block = 2

    def body(b, carry):
        i0 = b * block
        acc = jnp.zeros((block * width, sk), jnp.float32)
        for t in range(steps):
            lo = m_ref[pl.ds(i0 + 2 * t, block)].reshape(block * width, m_width)
            hi = m_ref[pl.ds(i0 + 2 * t + 1, block)].reshape(block * width, m_width)
            lhs = jnp.concatenate([lo, hi], axis=1)
            acc = acc + jnp.dot(lhs, probe_ref[t], preferred_element_type=jnp.float32)
        out_ref[pl.ds(i0, block)] = acc.reshape(block, width, sk)
        return carry

    lax.fori_loop(0, rows // block, body, 0)


def forward_panel(pair, probe_pairs, rows):
    width = pair.shape[1]
    sk = probe_pairs.shape[2]
    return pl.pallas_call(
        forward_kernel,
        out_shape=jax.ShapeDtypeStruct((rows, width, sk), jnp.float32),
        in_specs=[pl.BlockSpec(memory_space=pltpu.VMEM)] * 2,
        out_specs=pl.BlockSpec(memory_space=pltpu.VMEM),
        compiler_params=pltpu.CompilerParams(vmem_limit_bytes=60 * 1024 * 1024),
    )(pair, probe_pairs)


def backward_kernel(mt_ref, sketch_ref, out_ref):
    cols, m_width, sk = out_ref.shape
    rows = sketch_ref.shape[0]
    block = 4

    def body(b, carry):
        j0 = b * block
        acc = jnp.zeros((block * m_width, sk), jnp.float32)
        for i in range(rows):
            lhs = mt_ref[pl.ds(j0 + i, block)].reshape(block * m_width, mt_ref.shape[2])
            acc = acc + jnp.dot(lhs, sketch_ref[i], preferred_element_type=jnp.float32)
        out_ref[pl.ds(j0, block)] = acc.reshape(block, m_width, sk)
        return carry

    lax.fori_loop(0, cols // block, body, 0)


def prep_kernel(markov_ref, keeper_ref, masked_ref, mt_ref):
    keeper = keeper_ref[...]

    def body(k, carry):
        value = markov_ref[k] * keeper
        masked_ref[k] = value
        mt_ref[k] = value.astype(jnp.float32).T.astype(mt_ref.dtype)
        return carry

    lax.fori_loop(0, markov_ref.shape[0], body, 0)


def prep(markov, keeper):
    lags, width, m_width = markov.shape
    return pl.pallas_call(
        prep_kernel,
        out_shape=(
            jax.ShapeDtypeStruct((lags, width, m_width), markov.dtype),
            jax.ShapeDtypeStruct((lags, m_width, width), markov.dtype),
        ),
        in_specs=[pl.BlockSpec(memory_space=pltpu.VMEM)] * 2,
        out_specs=(pl.BlockSpec(memory_space=pltpu.VMEM),) * 2,
        compiler_params=pltpu.CompilerParams(vmem_limit_bytes=60 * 1024 * 1024),
    )(markov, keeper)


def backward_panel(mt, sketch, cols):
    m_width = mt.shape[1]
    sk = sketch.shape[2]
    return pl.pallas_call(
        backward_kernel,
        out_shape=jax.ShapeDtypeStruct((cols, m_width, sk), jnp.float32),
        in_specs=[pl.BlockSpec(memory_space=pltpu.VMEM)] * 2,
        out_specs=pl.BlockSpec(memory_space=pltpu.VMEM),
        compiler_params=pltpu.CompilerParams(vmem_limit_bytes=60 * 1024 * 1024),
    )(mt, sketch)


def exchange_kernel(axis, n, stride, gather, x_ref, y_ref, send_sem, recv_sem, local_sem):
    me = lax.axis_index(axis)
    pos = lax.rem(me // stride, n)
    base = me - pos * stride

    def member(k):
        return base + k * stride

    barrier = pltpu.get_barrier_semaphore()
    for d in range(1, n):
        peer = lax.rem(pos + d, n)
        pl.semaphore_signal(barrier, inc=1, device_id={axis: member(peer)}, device_id_type=MESH)
    pl.semaphore_wait(barrier, n - 1)

    own_src = x_ref if gather else x_ref.at[pos]
    local = pltpu.make_async_copy(own_src, y_ref.at[pos], local_sem)
    local.start()
    copies = []
    for d in range(1, n):
        peer = lax.rem(pos + d, n)
        src = x_ref if gather else x_ref.at[peer]
        copy = pltpu.make_async_remote_copy(
            src_ref=src,
            dst_ref=y_ref.at[pos],
            send_sem=send_sem.at[d],
            recv_sem=recv_sem.at[d],
            device_id={axis: member(peer)},
            device_id_type=MESH,
        )
        copy.start()
        copies.append(copy)
    local.wait()
    for copy in copies:
        copy.wait()


def exchange(x, axis, n, stride, gather, cid):
    out_shape = (n,) + (x.shape if gather else x.shape[1:])
    return pl.pallas_call(
        functools.partial(exchange_kernel, axis, n, stride, gather),
        out_shape=jax.ShapeDtypeStruct(out_shape, x.dtype),
        in_specs=[pl.BlockSpec(memory_space=pl.ANY)],
        out_specs=pl.BlockSpec(memory_space=pl.ANY),
        scratch_shapes=[
            pltpu.SemaphoreType.DMA((n,)),
            pltpu.SemaphoreType.DMA((n,)),
            pltpu.SemaphoreType.DMA(()),
        ],
        compiler_params=pltpu.CompilerParams(collective_id=cid, has_side_effects=True),
    )(x)


def sketch_sum_kernel(
    n_chips, raw_ref, out_ref, half_send, core_buf, chip_send, chip_recv, core_sems, rs_send, rs_recv, ag_send, ag_recv
):
    me = lax.axis_index("in")
    core = lax.rem(me, 2)
    chip = me // 2
    partner = me + 1 - 2 * core
    rows = raw_ref.shape[0]
    half = rows // 2
    piece = half // n_chips
    my_half = core * half

    def chip_dev(k):
        return k * 2 + core

    barrier = pltpu.get_barrier_semaphore()
    pl.semaphore_signal(barrier, inc=1, device_id={"in": partner}, device_id_type=MESH)
    for d in range(1, n_chips):
        peer = lax.rem(chip + d, n_chips)
        pl.semaphore_signal(barrier, inc=1, device_id={"in": chip_dev(peer)}, device_id_type=MESH)
    pl.semaphore_wait(barrier, n_chips)

    other_half = (1 - core) * half

    def to_send(r, carry):
        half_send[r] = raw_ref[other_half + r].astype(half_send.dtype)
        return carry

    lax.fori_loop(0, half, to_send, 0)
    core_copy = pltpu.make_async_remote_copy(
        src_ref=half_send,
        dst_ref=core_buf,
        send_sem=core_sems.at[0],
        recv_sem=core_sems.at[1],
        device_id={"in": partner},
        device_id_type=MESH,
    )
    core_copy.start()
    core_copy.wait()

    def add_core(r, carry):
        chip_send[r] = (raw_ref[my_half + r] + core_buf[r].astype(jnp.float32)).astype(chip_send.dtype)
        return carry

    lax.fori_loop(0, half, add_core, 0)
    scatter = []
    for d in range(1, n_chips):
        peer = lax.rem(chip + d, n_chips)
        copy = pltpu.make_async_remote_copy(
            src_ref=chip_send.at[pl.ds(peer * piece, piece)],
            dst_ref=chip_recv.at[chip],
            send_sem=rs_send.at[d],
            recv_sem=rs_recv.at[d],
            device_id={"in": chip_dev(peer)},
            device_id_type=MESH,
        )
        copy.start()
        scatter.append(copy)
    for copy in scatter:
        copy.wait()

    base_row = my_half + chip * piece
    for q in range(piece):
        acc = chip_send[chip * piece + q].astype(jnp.float32)
        for d in range(1, n_chips):
            acc = acc + chip_recv[lax.rem(chip + d, n_chips), q].astype(jnp.float32)
        out_ref[base_row + q] = acc.astype(out_ref.dtype)

    gather = []
    for d in range(1, n_chips):
        peer = lax.rem(chip + d, n_chips)
        copy = pltpu.make_async_remote_copy(
            src_ref=out_ref.at[pl.ds(base_row, piece)],
            dst_ref=out_ref.at[pl.ds(base_row, piece)],
            send_sem=ag_send.at[d],
            recv_sem=ag_recv.at[d],
            device_id={"in": chip_dev(peer)},
            device_id_type=MESH,
        )
        copy.start()
        gather.append(copy)
    for copy in gather:
        copy.wait()
    core_back = pltpu.make_async_remote_copy(
        src_ref=out_ref.at[pl.ds(my_half, half)],
        dst_ref=out_ref.at[pl.ds(my_half, half)],
        send_sem=core_sems.at[2],
        recv_sem=core_sems.at[3],
        device_id={"in": partner},
        device_id_type=MESH,
    )
    core_back.start()
    core_back.wait()


def sketch_sum(raw, n_in, cid):
    rows, width, sk = raw.shape
    n_chips = n_in // 2
    half = rows // 2
    return pl.pallas_call(
        functools.partial(sketch_sum_kernel, n_chips),
        out_shape=jax.ShapeDtypeStruct(raw.shape, jnp.bfloat16),
        in_specs=[pl.BlockSpec(memory_space=pltpu.VMEM)],
        out_specs=pl.BlockSpec(memory_space=pltpu.VMEM),
        scratch_shapes=[
            pltpu.VMEM((half, width, sk), jnp.bfloat16),
            pltpu.VMEM((half, width, sk), jnp.bfloat16),
            pltpu.VMEM((half, width, sk), jnp.bfloat16),
            pltpu.VMEM((n_chips, half // n_chips, width, sk), jnp.bfloat16),
            pltpu.SemaphoreType.DMA((4,)),
            pltpu.SemaphoreType.DMA((n_chips,)),
            pltpu.SemaphoreType.DMA((n_chips,)),
            pltpu.SemaphoreType.DMA((n_chips,)),
            pltpu.SemaphoreType.DMA((n_chips,)),
        ],
        compiler_params=pltpu.CompilerParams(
            collective_id=cid, has_side_effects=True, vmem_limit_bytes=60 * 1024 * 1024
        ),
    )(raw)


def shards(n_out, n_in, markov, probes, pattern):
    keeper = jnp.repeat(jnp.repeat(pattern, BO, axis=0), BI, axis=1).astype(jnp.bfloat16)
    masked, mt = prep(markov, keeper)
    gathered = exchange(probes, "out", n_out, 1, True, 0)
    panel = gathered.reshape((-1,) + probes.shape[1:])
    s_all, cols, m_width = panel.shape
    probe_pairs = jnp.swapaxes(panel.reshape(s_all, cols // 2, 2 * m_width), 0, 1).swapaxes(1, 2)
    raw_part = forward_panel(masked, probe_pairs, R)
    rows, width, sk = raw_part.shape
    sketch = sketch_sum(raw_part, n_in, 1)
    local_gram = jnp.einsum("ips,ipt->st", sketch, sketch, preferred_element_type=jnp.float32)
    co_t = backward_panel(mt, sketch, cols)
    co_part = jnp.transpose(co_t.astype(jnp.bfloat16), (2, 0, 1))
    per = s_all // n_out
    gram_rows = local_gram.shape[0] * local_gram.shape[1] // (cols * m_width)
    gram_block = local_gram.astype(jnp.bfloat16).reshape(1, gram_rows, cols, m_width)
    send = jnp.concatenate(
        [co_part.reshape(n_out, per, cols, m_width), jnp.broadcast_to(gram_block, (n_out, gram_rows, cols, m_width))],
        axis=1,
    )
    got = exchange(send, "out", n_out, 1, False, 4).astype(jnp.float32)
    corange = jnp.sum(got[:, :per], axis=0)
    gram_matrix = jnp.sum(got[:, per:], axis=0).reshape(local_gram.shape) / (R * OUTPUT_CHANNELS)
    return (sketch, corange, gram_matrix)


def solution(mesh):
    return jax.shard_map(
        functools.partial(shards, mesh.shape["out"], mesh.shape["in"]),
        mesh=mesh,
        in_specs=(P(None, "out", "in"), P("out", None, "in"), P("out", "in")),
        out_specs=(P(None, "out", None), P("out", None, "in"), P()),
        check_vma=False,
    )
```

```python
import functools

import jax
import jax.numpy as jnp
from jax import lax
from jax.experimental import pallas as pl
from jax.experimental.pallas import tpu as pltpu
from jax.sharding import PartitionSpec as P

OUTPUT_CHANNELS = 2048
BO = 64
BI = 128
R = 32
C = 32

MESH = pl.DeviceIdType.MESH


def forward_kernel(m_ref, probe_ref, out_ref):
    rows, width, sk = out_ref.shape
    steps = probe_ref.shape[0]
    m_width = m_ref.shape[2]
    block = 2

    def body(b, carry):
        i0 = b * block
        acc = jnp.zeros((block * width, sk), jnp.float32)
        for t in range(steps):
            lo = m_ref[pl.ds(i0 + 2 * t, block)].reshape(block * width, m_width)
            hi = m_ref[pl.ds(i0 + 2 * t + 1, block)].reshape(block * width, m_width)
            lhs = jnp.concatenate([lo, hi], axis=1)
            acc = acc + jnp.dot(lhs, probe_ref[t], preferred_element_type=jnp.float32)
        out_ref[pl.ds(i0, block)] = acc.reshape(block, width, sk)
        return carry

    lax.fori_loop(0, rows // block, body, 0)


def forward_panel(pair, probe_pairs, rows):
    width = pair.shape[1]
    sk = probe_pairs.shape[2]
    return pl.pallas_call(
        forward_kernel,
        out_shape=jax.ShapeDtypeStruct((rows, width, sk), jnp.float32),
        in_specs=[pl.BlockSpec(memory_space=pltpu.VMEM)] * 2,
        out_specs=pl.BlockSpec(memory_space=pltpu.VMEM),
        compiler_params=pltpu.CompilerParams(vmem_limit_bytes=60 * 1024 * 1024),
    )(pair, probe_pairs)


def backward_kernel(mt_ref, sketch_ref, out_ref):
    cols, m_width, sk = out_ref.shape
    rows = sketch_ref.shape[0]
    block = 4

    def body(b, carry):
        j0 = b * block
        acc = jnp.zeros((block * m_width, sk), jnp.float32)
        for i in range(rows):
            lhs = mt_ref[pl.ds(j0 + i, block)].reshape(block * m_width, mt_ref.shape[2])
            acc = acc + jnp.dot(lhs, sketch_ref[i], preferred_element_type=jnp.float32)
        out_ref[pl.ds(j0, block)] = acc.reshape(block, m_width, sk)
        return carry

    lax.fori_loop(0, cols // block, body, 0)


def prep_kernel(n_out, markov_ref, keeper_ref, probes_ref, masked_ref, mt_ref, gathered_ref, send_sem, recv_sem, local_sem):
    me = lax.axis_index("out")
    barrier = pltpu.get_barrier_semaphore()
    for d in range(1, n_out):
        pl.semaphore_signal(barrier, inc=1, device_id={"out": lax.rem(me + d, n_out)}, device_id_type=MESH)
    pl.semaphore_wait(barrier, n_out - 1)
    local = pltpu.make_async_copy(probes_ref, gathered_ref.at[me], local_sem)
    local.start()
    copies = []
    for d in range(1, n_out):
        copy = pltpu.make_async_remote_copy(
            src_ref=probes_ref,
            dst_ref=gathered_ref.at[me],
            send_sem=send_sem.at[d],
            recv_sem=recv_sem.at[d],
            device_id={"out": lax.rem(me + d, n_out)},
            device_id_type=MESH,
        )
        copy.start()
        copies.append(copy)

    keeper = keeper_ref[...]

    def body(k, carry):
        value = markov_ref[k] * keeper
        masked_ref[k] = value
        mt_ref[k] = value.astype(jnp.float32).T.astype(mt_ref.dtype)
        return carry

    lax.fori_loop(0, markov_ref.shape[0], body, 0)
    local.wait()
    for copy in copies:
        copy.wait()


def prep(markov, keeper, probes, n_out, cid):
    lags, width, m_width = markov.shape
    return pl.pallas_call(
        functools.partial(prep_kernel, n_out),
        out_shape=(
            jax.ShapeDtypeStruct((lags, width, m_width), markov.dtype),
            jax.ShapeDtypeStruct((lags, m_width, width), markov.dtype),
            jax.ShapeDtypeStruct((n_out,) + probes.shape, probes.dtype),
        ),
        in_specs=[pl.BlockSpec(memory_space=pltpu.VMEM)] * 3,
        out_specs=(pl.BlockSpec(memory_space=pltpu.VMEM),) * 3,
        scratch_shapes=[
            pltpu.SemaphoreType.DMA((n_out,)),
            pltpu.SemaphoreType.DMA((n_out,)),
            pltpu.SemaphoreType.DMA(()),
        ],
        compiler_params=pltpu.CompilerParams(
            collective_id=cid, has_side_effects=True, vmem_limit_bytes=60 * 1024 * 1024
        ),
    )(markov, keeper, probes)


def backward_panel(mt, sketch, cols):
    m_width = mt.shape[1]
    sk = sketch.shape[2]
    return pl.pallas_call(
        backward_kernel,
        out_shape=jax.ShapeDtypeStruct((cols, m_width, sk), jnp.float32),
        in_specs=[pl.BlockSpec(memory_space=pltpu.VMEM)] * 2,
        out_specs=pl.BlockSpec(memory_space=pltpu.VMEM),
        compiler_params=pltpu.CompilerParams(vmem_limit_bytes=60 * 1024 * 1024),
    )(mt, sketch)


def exchange_kernel(axis, n, stride, gather, x_ref, y_ref, send_sem, recv_sem, local_sem):
    me = lax.axis_index(axis)
    pos = lax.rem(me // stride, n)
    base = me - pos * stride

    def member(k):
        return base + k * stride

    barrier = pltpu.get_barrier_semaphore()
    for d in range(1, n):
        peer = lax.rem(pos + d, n)
        pl.semaphore_signal(barrier, inc=1, device_id={axis: member(peer)}, device_id_type=MESH)
    pl.semaphore_wait(barrier, n - 1)

    own_src = x_ref if gather else x_ref.at[pos]
    local = pltpu.make_async_copy(own_src, y_ref.at[pos], local_sem)
    local.start()
    copies = []
    for d in range(1, n):
        peer = lax.rem(pos + d, n)
        src = x_ref if gather else x_ref.at[peer]
        copy = pltpu.make_async_remote_copy(
            src_ref=src,
            dst_ref=y_ref.at[pos],
            send_sem=send_sem.at[d],
            recv_sem=recv_sem.at[d],
            device_id={axis: member(peer)},
            device_id_type=MESH,
        )
        copy.start()
        copies.append(copy)
    local.wait()
    for copy in copies:
        copy.wait()


def exchange(x, axis, n, stride, gather, cid):
    out_shape = (n,) + (x.shape if gather else x.shape[1:])
    return pl.pallas_call(
        functools.partial(exchange_kernel, axis, n, stride, gather),
        out_shape=jax.ShapeDtypeStruct(out_shape, x.dtype),
        in_specs=[pl.BlockSpec(memory_space=pl.ANY)],
        out_specs=pl.BlockSpec(memory_space=pl.ANY),
        scratch_shapes=[
            pltpu.SemaphoreType.DMA((n,)),
            pltpu.SemaphoreType.DMA((n,)),
            pltpu.SemaphoreType.DMA(()),
        ],
        compiler_params=pltpu.CompilerParams(collective_id=cid, has_side_effects=True),
    )(x)


def sketch_sum_kernel(
    n_chips, raw_ref, out_ref, half_send, core_buf, chip_send, chip_recv, core_sems, rs_send, rs_recv, ag_send, ag_recv
):
    me = lax.axis_index("in")
    core = lax.rem(me, 2)
    chip = me // 2
    partner = me + 1 - 2 * core
    rows = raw_ref.shape[0]
    half = rows // 2
    piece = half // n_chips
    my_half = core * half

    def chip_dev(k):
        return k * 2 + core

    barrier = pltpu.get_barrier_semaphore()
    pl.semaphore_signal(barrier, inc=1, device_id={"in": partner}, device_id_type=MESH)
    for d in range(1, n_chips):
        peer = lax.rem(chip + d, n_chips)
        pl.semaphore_signal(barrier, inc=1, device_id={"in": chip_dev(peer)}, device_id_type=MESH)
    pl.semaphore_wait(barrier, n_chips)

    other_half = (1 - core) * half

    def to_send(r, carry):
        half_send[r] = raw_ref[other_half + r].astype(half_send.dtype)
        return carry

    lax.fori_loop(0, half, to_send, 0)
    core_copy = pltpu.make_async_remote_copy(
        src_ref=half_send,
        dst_ref=core_buf,
        send_sem=core_sems.at[0],
        recv_sem=core_sems.at[1],
        device_id={"in": partner},
        device_id_type=MESH,
    )
    core_copy.start()
    core_copy.wait()

    def add_core(r, carry):
        chip_send[r] = (raw_ref[my_half + r] + core_buf[r].astype(jnp.float32)).astype(chip_send.dtype)
        return carry

    lax.fori_loop(0, half, add_core, 0)
    scatter = []
    for d in range(1, n_chips):
        peer = lax.rem(chip + d, n_chips)
        copy = pltpu.make_async_remote_copy(
            src_ref=chip_send.at[pl.ds(peer * piece, piece)],
            dst_ref=chip_recv.at[chip],
            send_sem=rs_send.at[d],
            recv_sem=rs_recv.at[d],
            device_id={"in": chip_dev(peer)},
            device_id_type=MESH,
        )
        copy.start()
        scatter.append(copy)
    for copy in scatter:
        copy.wait()

    base_row = my_half + chip * piece
    for q in range(piece):
        acc = chip_send[chip * piece + q].astype(jnp.float32)
        for d in range(1, n_chips):
            acc = acc + chip_recv[lax.rem(chip + d, n_chips), q].astype(jnp.float32)
        out_ref[base_row + q] = acc.astype(out_ref.dtype)

    gather = []
    for d in range(1, n_chips):
        peer = lax.rem(chip + d, n_chips)
        copy = pltpu.make_async_remote_copy(
            src_ref=out_ref.at[pl.ds(base_row, piece)],
            dst_ref=out_ref.at[pl.ds(base_row, piece)],
            send_sem=ag_send.at[d],
            recv_sem=ag_recv.at[d],
            device_id={"in": chip_dev(peer)},
            device_id_type=MESH,
        )
        copy.start()
        gather.append(copy)
    for copy in gather:
        copy.wait()
    core_back = pltpu.make_async_remote_copy(
        src_ref=out_ref.at[pl.ds(my_half, half)],
        dst_ref=out_ref.at[pl.ds(my_half, half)],
        send_sem=core_sems.at[2],
        recv_sem=core_sems.at[3],
        device_id={"in": partner},
        device_id_type=MESH,
    )
    core_back.start()
    core_back.wait()


def sketch_sum(raw, n_in, cid):
    rows, width, sk = raw.shape
    n_chips = n_in // 2
    half = rows // 2
    return pl.pallas_call(
        functools.partial(sketch_sum_kernel, n_chips),
        out_shape=jax.ShapeDtypeStruct(raw.shape, jnp.bfloat16),
        in_specs=[pl.BlockSpec(memory_space=pltpu.VMEM)],
        out_specs=pl.BlockSpec(memory_space=pltpu.VMEM),
        scratch_shapes=[
            pltpu.VMEM((half, width, sk), jnp.bfloat16),
            pltpu.VMEM((half, width, sk), jnp.bfloat16),
            pltpu.VMEM((half, width, sk), jnp.bfloat16),
            pltpu.VMEM((n_chips, half // n_chips, width, sk), jnp.bfloat16),
            pltpu.SemaphoreType.DMA((4,)),
            pltpu.SemaphoreType.DMA((n_chips,)),
            pltpu.SemaphoreType.DMA((n_chips,)),
            pltpu.SemaphoreType.DMA((n_chips,)),
            pltpu.SemaphoreType.DMA((n_chips,)),
        ],
        compiler_params=pltpu.CompilerParams(
            collective_id=cid, has_side_effects=True, vmem_limit_bytes=60 * 1024 * 1024
        ),
    )(raw)


def forward_rows(m_ref, probe_ref, i0, block):
    width, m_width = m_ref.shape[1], m_ref.shape[2]
    sk = probe_ref.shape[2]
    acc = jnp.zeros((block * width, sk), jnp.float32)
    for t in range(probe_ref.shape[0]):
        lo = m_ref[pl.ds(i0 + 2 * t, block)].reshape(block * width, m_width)
        hi = m_ref[pl.ds(i0 + 2 * t + 1, block)].reshape(block * width, m_width)
        lhs = jnp.concatenate([lo, hi], axis=1)
        acc = acc + jnp.dot(lhs, probe_ref[t], preferred_element_type=jnp.float32)
    return acc.reshape(block, width, sk)


def sketch_kernel(
    n_chips, m_ref, probe_ref, out_ref, half_send, core_buf, chip_send, chip_recv,
    core_send, core_recv, rs_send, rs_recv, ag_send, ag_recv, back_sems,
):
    me = lax.axis_index("in")
    core = lax.rem(me, 2)
    chip = me // 2
    partner = me + 1 - 2 * core
    rows = out_ref.shape[0]
    half = rows // 2
    piece = half // n_chips
    my_half = core * half
    other_half = (1 - core) * half

    def chip_dev(k):
        return k * 2 + core

    def chunk_of(step):
        return lax.rem(chip + step + 1, n_chips)

    def core_copy(step):
        c = chunk_of(step)
        return pltpu.make_async_remote_copy(
            src_ref=half_send.at[pl.ds(c * piece, piece)],
            dst_ref=core_buf.at[pl.ds(c * piece, piece)],
            send_sem=core_send.at[step],
            recv_sem=core_recv.at[step],
            device_id={"in": partner},
            device_id_type=MESH,
        )

    def rs_copy(step):
        c = chunk_of(step)
        return pltpu.make_async_remote_copy(
            src_ref=chip_send.at[pl.ds(c * piece, piece)],
            dst_ref=chip_recv.at[chip],
            send_sem=rs_send.at[step],
            recv_sem=rs_recv.at[step],
            device_id={"in": chip_dev(c)},
            device_id_type=MESH,
        )

    barrier = pltpu.get_barrier_semaphore()
    pl.semaphore_signal(barrier, inc=1, device_id={"in": partner}, device_id_type=MESH)
    for d in range(1, n_chips):
        pl.semaphore_signal(barrier, inc=1, device_id={"in": chip_dev(lax.rem(chip + d, n_chips))}, device_id_type=MESH)
    pl.semaphore_wait(barrier, n_chips)

    def partner_rows(step, carry):
        c = chunk_of(step)
        half_send[pl.ds(c * piece, piece)] = forward_rows(m_ref, probe_ref, other_half + c * piece, piece).astype(
            half_send.dtype
        )
        core_copy(step).start()
        return carry

    lax.fori_loop(0, n_chips, partner_rows, 0)

    def own_rows(step):
        c = chunk_of(step)
        mine = forward_rows(m_ref, probe_ref, my_half + c * piece, piece)
        core_copy(step).wait_recv()
        chip_send[pl.ds(c * piece, piece)] = (mine + core_buf[pl.ds(c * piece, piece)].astype(jnp.float32)).astype(
            chip_send.dtype
        )

    def chip_rows(step, carry):
        own_rows(step)
        rs_copy(step).start()
        return carry

    lax.fori_loop(0, n_chips - 1, chip_rows, 0)
    own_rows(n_chips - 1)

    for step in range(n_chips - 1):
        rs_copy(step).wait_recv()
    base_row = my_half + chip * piece
    for q in range(piece):
        acc = chip_send[chip * piece + q].astype(jnp.float32)
        for d in range(1, n_chips):
            acc = acc + chip_recv[lax.rem(chip + d, n_chips), q].astype(jnp.float32)
        out_ref[base_row + q] = acc.astype(out_ref.dtype)

    gather = []
    for d in range(1, n_chips):
        copy = pltpu.make_async_remote_copy(
            src_ref=out_ref.at[pl.ds(base_row, piece)],
            dst_ref=out_ref.at[pl.ds(base_row, piece)],
            send_sem=ag_send.at[d],
            recv_sem=ag_recv.at[d],
            device_id={"in": chip_dev(lax.rem(chip + d, n_chips))},
            device_id_type=MESH,
        )
        copy.start()
        gather.append(copy)
    for copy in gather:
        copy.wait()
    back = pltpu.make_async_remote_copy(
        src_ref=out_ref.at[pl.ds(my_half, half)],
        dst_ref=out_ref.at[pl.ds(my_half, half)],
        send_sem=back_sems.at[0],
        recv_sem=back_sems.at[1],
        device_id={"in": partner},
        device_id_type=MESH,
    )
    back.start()
    for step in range(n_chips):
        core_copy(step).wait_send()
    for step in range(n_chips - 1):
        rs_copy(step).wait_send()
    back.wait()


def sketch_of(masked, probe_pairs, rows, n_in, cid):
    width = masked.shape[1]
    sk = probe_pairs.shape[2]
    n_chips = n_in // 2
    half = rows // 2
    return pl.pallas_call(
        functools.partial(sketch_kernel, n_chips),
        out_shape=jax.ShapeDtypeStruct((rows, width, sk), jnp.bfloat16),
        in_specs=[pl.BlockSpec(memory_space=pltpu.VMEM)] * 2,
        out_specs=pl.BlockSpec(memory_space=pltpu.VMEM),
        scratch_shapes=[
            pltpu.VMEM((half, width, sk), jnp.bfloat16),
            pltpu.VMEM((half, width, sk), jnp.bfloat16),
            pltpu.VMEM((half, width, sk), jnp.bfloat16),
            pltpu.VMEM((n_chips, half // n_chips, width, sk), jnp.bfloat16),
            pltpu.SemaphoreType.DMA((n_chips,)),
            pltpu.SemaphoreType.DMA((n_chips,)),
            pltpu.SemaphoreType.DMA((n_chips,)),
            pltpu.SemaphoreType.DMA((n_chips,)),
            pltpu.SemaphoreType.DMA((n_chips,)),
            pltpu.SemaphoreType.DMA((n_chips,)),
            pltpu.SemaphoreType.DMA((2,)),
        ],
        compiler_params=pltpu.CompilerParams(
            collective_id=cid, has_side_effects=True, vmem_limit_bytes=60 * 1024 * 1024
        ),
    )(masked, probe_pairs)


def shards(n_out, n_in, markov, probes, pattern):
    keeper = jnp.repeat(jnp.repeat(pattern, BO, axis=0), BI, axis=1).astype(jnp.bfloat16)
    masked, mt, gathered = prep(markov, keeper, probes, n_out, 0)
    panel = gathered.reshape((-1,) + probes.shape[1:])
    s_all, cols, m_width = panel.shape
    probe_pairs = jnp.swapaxes(panel.reshape(s_all, cols // 2, 2 * m_width), 0, 1).swapaxes(1, 2)
    sketch = sketch_of(masked, probe_pairs, R, n_in, 1)
    rows, width, sk = sketch.shape
    local_gram = jnp.einsum("ips,ipt->st", sketch, sketch, preferred_element_type=jnp.float32)
    co_t = backward_panel(mt, sketch, cols)
    co_part = jnp.transpose(co_t.astype(jnp.bfloat16), (2, 0, 1))
    per = s_all // n_out
    gram_rows = local_gram.shape[0] * local_gram.shape[1] // (cols * m_width)
    gram_block = local_gram.astype(jnp.bfloat16).reshape(1, gram_rows, cols, m_width)
    send = jnp.concatenate(
        [co_part.reshape(n_out, per, cols, m_width), jnp.broadcast_to(gram_block, (n_out, gram_rows, cols, m_width))],
        axis=1,
    )
    got = exchange(send, "out", n_out, 1, False, 4).astype(jnp.float32)
    corange = jnp.sum(got[:, :per], axis=0)
    gram_matrix = jnp.sum(got[:, per:], axis=0).reshape(local_gram.shape) / (R * OUTPUT_CHANNELS)
    return (sketch, corange, gram_matrix)


def solution(mesh):
    return jax.shard_map(
        functools.partial(shards, mesh.shape["out"], mesh.shape["in"]),
        mesh=mesh,
        in_specs=(P(None, "out", "in"), P("out", None, "in"), P("out", "in")),
        out_specs=(P(None, "out", None), P("out", None, "in"), P()),
        check_vma=False,
    )
```

```python
import functools

import jax
import jax.numpy as jnp
from jax import lax
from jax.experimental import pallas as pl
from jax.experimental.pallas import tpu as pltpu
from jax.sharding import PartitionSpec as P

OUTPUT_CHANNELS = 2048
BO = 64
BI = 128
R = 32
C = 32

MESH = pl.DeviceIdType.MESH


def forward_kernel(m_ref, probe_ref, out_ref):
    rows, width, sk = out_ref.shape
    steps = probe_ref.shape[0]
    m_width = m_ref.shape[2]
    block = 2

    def body(b, carry):
        i0 = b * block
        acc = jnp.zeros((block * width, sk), jnp.float32)
        for t in range(steps):
            lo = m_ref[pl.ds(i0 + 2 * t, block)].reshape(block * width, m_width)
            hi = m_ref[pl.ds(i0 + 2 * t + 1, block)].reshape(block * width, m_width)
            lhs = jnp.concatenate([lo, hi], axis=1)
            acc = acc + jnp.dot(lhs, probe_ref[t], preferred_element_type=jnp.float32)
        out_ref[pl.ds(i0, block)] = acc.reshape(block, width, sk)
        return carry

    lax.fori_loop(0, rows // block, body, 0)


def forward_panel(pair, probe_pairs, rows):
    width = pair.shape[1]
    sk = probe_pairs.shape[2]
    return pl.pallas_call(
        forward_kernel,
        out_shape=jax.ShapeDtypeStruct((rows, width, sk), jnp.float32),
        in_specs=[pl.BlockSpec(memory_space=pltpu.VMEM)] * 2,
        out_specs=pl.BlockSpec(memory_space=pltpu.VMEM),
        compiler_params=pltpu.CompilerParams(vmem_limit_bytes=60 * 1024 * 1024),
    )(pair, probe_pairs)


def backward_kernel(mt_ref, sketch_ref, out_ref):
    cols, m_width, sk = out_ref.shape
    rows = sketch_ref.shape[0]
    block = 4

    def body(b, carry):
        j0 = b * block
        acc = jnp.zeros((block * m_width, sk), jnp.float32)
        for i in range(rows):
            lhs = mt_ref[pl.ds(j0 + i, block)].reshape(block * m_width, mt_ref.shape[2])
            acc = acc + jnp.dot(lhs, sketch_ref[i], preferred_element_type=jnp.float32)
        out_ref[pl.ds(j0, block)] = acc.reshape(block, m_width, sk)
        return carry

    lax.fori_loop(0, cols // block, body, 0)


def prep_kernel(n_out, markov_ref, keeper_ref, probes_ref, masked_ref, mt_ref, gathered_ref, send_sem, recv_sem, local_sem):
    me = lax.axis_index("out")
    barrier = pltpu.get_barrier_semaphore()
    for d in range(1, n_out):
        pl.semaphore_signal(barrier, inc=1, device_id={"out": lax.rem(me + d, n_out)}, device_id_type=MESH)
    pl.semaphore_wait(barrier, n_out - 1)
    local = pltpu.make_async_copy(probes_ref, gathered_ref.at[me], local_sem)
    local.start()
    copies = []
    for d in range(1, n_out):
        copy = pltpu.make_async_remote_copy(
            src_ref=probes_ref,
            dst_ref=gathered_ref.at[me],
            send_sem=send_sem.at[d],
            recv_sem=recv_sem.at[d],
            device_id={"out": lax.rem(me + d, n_out)},
            device_id_type=MESH,
        )
        copy.start()
        copies.append(copy)

    keeper = keeper_ref[...]

    def body(k, carry):
        value = markov_ref[k] * keeper
        masked_ref[k] = value
        mt_ref[k] = value.astype(jnp.float32).T.astype(mt_ref.dtype)
        return carry

    lax.fori_loop(0, markov_ref.shape[0], body, 0)
    local.wait()
    for copy in copies:
        copy.wait()


def prep(markov, keeper, probes, n_out, cid):
    lags, width, m_width = markov.shape
    return pl.pallas_call(
        functools.partial(prep_kernel, n_out),
        out_shape=(
            jax.ShapeDtypeStruct((lags, width, m_width), markov.dtype),
            jax.ShapeDtypeStruct((lags, m_width, width), markov.dtype),
            jax.ShapeDtypeStruct((n_out,) + probes.shape, probes.dtype),
        ),
        in_specs=[pl.BlockSpec(memory_space=pltpu.VMEM)] * 3,
        out_specs=(pl.BlockSpec(memory_space=pltpu.VMEM),) * 3,
        scratch_shapes=[
            pltpu.SemaphoreType.DMA((n_out,)),
            pltpu.SemaphoreType.DMA((n_out,)),
            pltpu.SemaphoreType.DMA(()),
        ],
        compiler_params=pltpu.CompilerParams(
            collective_id=cid, has_side_effects=True, vmem_limit_bytes=60 * 1024 * 1024
        ),
    )(markov, keeper, probes)


def backward_panel(mt, sketch, cols):
    m_width = mt.shape[1]
    sk = sketch.shape[2]
    return pl.pallas_call(
        backward_kernel,
        out_shape=jax.ShapeDtypeStruct((cols, m_width, sk), jnp.float32),
        in_specs=[pl.BlockSpec(memory_space=pltpu.VMEM)] * 2,
        out_specs=pl.BlockSpec(memory_space=pltpu.VMEM),
        compiler_params=pltpu.CompilerParams(vmem_limit_bytes=60 * 1024 * 1024),
    )(mt, sketch)


def exchange_kernel(axis, n, stride, gather, x_ref, y_ref, send_sem, recv_sem, local_sem):
    me = lax.axis_index(axis)
    pos = lax.rem(me // stride, n)
    base = me - pos * stride

    def member(k):
        return base + k * stride

    barrier = pltpu.get_barrier_semaphore()
    for d in range(1, n):
        peer = lax.rem(pos + d, n)
        pl.semaphore_signal(barrier, inc=1, device_id={axis: member(peer)}, device_id_type=MESH)
    pl.semaphore_wait(barrier, n - 1)

    own_src = x_ref if gather else x_ref.at[pos]
    local = pltpu.make_async_copy(own_src, y_ref.at[pos], local_sem)
    local.start()
    copies = []
    for d in range(1, n):
        peer = lax.rem(pos + d, n)
        src = x_ref if gather else x_ref.at[peer]
        copy = pltpu.make_async_remote_copy(
            src_ref=src,
            dst_ref=y_ref.at[pos],
            send_sem=send_sem.at[d],
            recv_sem=recv_sem.at[d],
            device_id={axis: member(peer)},
            device_id_type=MESH,
        )
        copy.start()
        copies.append(copy)
    local.wait()
    for copy in copies:
        copy.wait()


def exchange(x, axis, n, stride, gather, cid):
    out_shape = (n,) + (x.shape if gather else x.shape[1:])
    return pl.pallas_call(
        functools.partial(exchange_kernel, axis, n, stride, gather),
        out_shape=jax.ShapeDtypeStruct(out_shape, x.dtype),
        in_specs=[pl.BlockSpec(memory_space=pl.ANY)],
        out_specs=pl.BlockSpec(memory_space=pl.ANY),
        scratch_shapes=[
            pltpu.SemaphoreType.DMA((n,)),
            pltpu.SemaphoreType.DMA((n,)),
            pltpu.SemaphoreType.DMA(()),
        ],
        compiler_params=pltpu.CompilerParams(collective_id=cid, has_side_effects=True),
    )(x)


def sketch_sum_kernel(
    n_chips, raw_ref, out_ref, half_send, core_buf, chip_send, chip_recv, core_sems, rs_send, rs_recv, ag_send, ag_recv
):
    me = lax.axis_index("in")
    core = lax.rem(me, 2)
    chip = me // 2
    partner = me + 1 - 2 * core
    rows = raw_ref.shape[0]
    half = rows // 2
    piece = half // n_chips
    my_half = core * half

    def chip_dev(k):
        return k * 2 + core

    barrier = pltpu.get_barrier_semaphore()
    pl.semaphore_signal(barrier, inc=1, device_id={"in": partner}, device_id_type=MESH)
    for d in range(1, n_chips):
        peer = lax.rem(chip + d, n_chips)
        pl.semaphore_signal(barrier, inc=1, device_id={"in": chip_dev(peer)}, device_id_type=MESH)
    pl.semaphore_wait(barrier, n_chips)

    other_half = (1 - core) * half

    def to_send(r, carry):
        half_send[r] = raw_ref[other_half + r].astype(half_send.dtype)
        return carry

    lax.fori_loop(0, half, to_send, 0)
    core_copy = pltpu.make_async_remote_copy(
        src_ref=half_send,
        dst_ref=core_buf,
        send_sem=core_sems.at[0],
        recv_sem=core_sems.at[1],
        device_id={"in": partner},
        device_id_type=MESH,
    )
    core_copy.start()
    core_copy.wait()

    def add_core(r, carry):
        chip_send[r] = (raw_ref[my_half + r] + core_buf[r].astype(jnp.float32)).astype(chip_send.dtype)
        return carry

    lax.fori_loop(0, half, add_core, 0)
    scatter = []
    for d in range(1, n_chips):
        peer = lax.rem(chip + d, n_chips)
        copy = pltpu.make_async_remote_copy(
            src_ref=chip_send.at[pl.ds(peer * piece, piece)],
            dst_ref=chip_recv.at[chip],
            send_sem=rs_send.at[d],
            recv_sem=rs_recv.at[d],
            device_id={"in": chip_dev(peer)},
            device_id_type=MESH,
        )
        copy.start()
        scatter.append(copy)
    for copy in scatter:
        copy.wait()

    base_row = my_half + chip * piece
    for q in range(piece):
        acc = chip_send[chip * piece + q].astype(jnp.float32)
        for d in range(1, n_chips):
            acc = acc + chip_recv[lax.rem(chip + d, n_chips), q].astype(jnp.float32)
        out_ref[base_row + q] = acc.astype(out_ref.dtype)

    gather = []
    for d in range(1, n_chips):
        peer = lax.rem(chip + d, n_chips)
        copy = pltpu.make_async_remote_copy(
            src_ref=out_ref.at[pl.ds(base_row, piece)],
            dst_ref=out_ref.at[pl.ds(base_row, piece)],
            send_sem=ag_send.at[d],
            recv_sem=ag_recv.at[d],
            device_id={"in": chip_dev(peer)},
            device_id_type=MESH,
        )
        copy.start()
        gather.append(copy)
    for copy in gather:
        copy.wait()
    core_back = pltpu.make_async_remote_copy(
        src_ref=out_ref.at[pl.ds(my_half, half)],
        dst_ref=out_ref.at[pl.ds(my_half, half)],
        send_sem=core_sems.at[2],
        recv_sem=core_sems.at[3],
        device_id={"in": partner},
        device_id_type=MESH,
    )
    core_back.start()
    core_back.wait()


def sketch_sum(raw, n_in, cid):
    rows, width, sk = raw.shape
    n_chips = n_in // 2
    half = rows // 2
    return pl.pallas_call(
        functools.partial(sketch_sum_kernel, n_chips),
        out_shape=jax.ShapeDtypeStruct(raw.shape, jnp.bfloat16),
        in_specs=[pl.BlockSpec(memory_space=pltpu.VMEM)],
        out_specs=pl.BlockSpec(memory_space=pltpu.VMEM),
        scratch_shapes=[
            pltpu.VMEM((half, width, sk), jnp.bfloat16),
            pltpu.VMEM((half, width, sk), jnp.bfloat16),
            pltpu.VMEM((half, width, sk), jnp.bfloat16),
            pltpu.VMEM((n_chips, half // n_chips, width, sk), jnp.bfloat16),
            pltpu.SemaphoreType.DMA((4,)),
            pltpu.SemaphoreType.DMA((n_chips,)),
            pltpu.SemaphoreType.DMA((n_chips,)),
            pltpu.SemaphoreType.DMA((n_chips,)),
            pltpu.SemaphoreType.DMA((n_chips,)),
        ],
        compiler_params=pltpu.CompilerParams(
            collective_id=cid, has_side_effects=True, vmem_limit_bytes=60 * 1024 * 1024
        ),
    )(raw)


def forward_rows(m_ref, probe_ref, i0, block):
    width, m_width = m_ref.shape[1], m_ref.shape[2]
    sk = probe_ref.shape[2]
    acc = jnp.zeros((block * width, sk), jnp.float32)
    for t in range(probe_ref.shape[0]):
        lo = m_ref[pl.ds(i0 + 2 * t, block)].reshape(block * width, m_width)
        hi = m_ref[pl.ds(i0 + 2 * t + 1, block)].reshape(block * width, m_width)
        lhs = jnp.concatenate([lo, hi], axis=1)
        acc = acc + jnp.dot(lhs, probe_ref[t], preferred_element_type=jnp.float32)
    return acc.reshape(block, width, sk)


def sketch_kernel(
    n_chips, m_ref, probe_ref, out_ref, half_send, core_buf, chip_send, chip_recv,
    core_send, core_recv, rs_send, rs_recv, ag_send, ag_recv, back_sems,
):
    me = lax.axis_index("in")
    core = lax.rem(me, 2)
    chip = me // 2
    partner = me + 1 - 2 * core
    rows = out_ref.shape[0]
    half = rows // 2
    piece = half // n_chips
    my_half = core * half
    other_half = (1 - core) * half

    def chip_dev(k):
        return k * 2 + core

    def chunk_of(step):
        return lax.rem(chip + step + 1, n_chips)

    def core_copy(step):
        c = chunk_of(step)
        return pltpu.make_async_remote_copy(
            src_ref=half_send.at[pl.ds(c * piece, piece)],
            dst_ref=core_buf.at[pl.ds(c * piece, piece)],
            send_sem=core_send.at[step],
            recv_sem=core_recv.at[step],
            device_id={"in": partner},
            device_id_type=MESH,
        )

    def rs_copy(step):
        c = chunk_of(step)
        return pltpu.make_async_remote_copy(
            src_ref=chip_send.at[pl.ds(c * piece, piece)],
            dst_ref=chip_recv.at[chip],
            send_sem=rs_send.at[step],
            recv_sem=rs_recv.at[step],
            device_id={"in": chip_dev(c)},
            device_id_type=MESH,
        )

    barrier = pltpu.get_barrier_semaphore()
    pl.semaphore_signal(barrier, inc=1, device_id={"in": partner}, device_id_type=MESH)
    for d in range(1, n_chips):
        pl.semaphore_signal(barrier, inc=1, device_id={"in": chip_dev(lax.rem(chip + d, n_chips))}, device_id_type=MESH)
    pl.semaphore_wait(barrier, n_chips)

    def partner_rows(step, carry):
        c = chunk_of(step)
        half_send[pl.ds(c * piece, piece)] = forward_rows(m_ref, probe_ref, other_half + c * piece, piece).astype(
            half_send.dtype
        )
        core_copy(step).start()
        return carry

    lax.fori_loop(0, n_chips, partner_rows, 0)

    def own_rows(step):
        c = chunk_of(step)
        mine = forward_rows(m_ref, probe_ref, my_half + c * piece, piece)
        core_copy(step).wait_recv()
        chip_send[pl.ds(c * piece, piece)] = (mine + core_buf[pl.ds(c * piece, piece)].astype(jnp.float32)).astype(
            chip_send.dtype
        )

    def chip_rows(step, carry):
        own_rows(step)
        rs_copy(step).start()
        return carry

    lax.fori_loop(0, n_chips - 1, chip_rows, 0)
    own_rows(n_chips - 1)

    for step in range(n_chips - 1):
        rs_copy(step).wait_recv()
    base_row = my_half + chip * piece
    for q in range(piece):
        acc = chip_send[chip * piece + q].astype(jnp.float32)
        for d in range(1, n_chips):
            acc = acc + chip_recv[lax.rem(chip + d, n_chips), q].astype(jnp.float32)
        out_ref[base_row + q] = acc.astype(out_ref.dtype)

    gather = []
    for d in range(1, n_chips):
        copy = pltpu.make_async_remote_copy(
            src_ref=out_ref.at[pl.ds(base_row, piece)],
            dst_ref=out_ref.at[pl.ds(base_row, piece)],
            send_sem=ag_send.at[d],
            recv_sem=ag_recv.at[d],
            device_id={"in": chip_dev(lax.rem(chip + d, n_chips))},
            device_id_type=MESH,
        )
        copy.start()
        gather.append(copy)
    for copy in gather:
        copy.wait()
    back = pltpu.make_async_remote_copy(
        src_ref=out_ref.at[pl.ds(my_half, half)],
        dst_ref=out_ref.at[pl.ds(my_half, half)],
        send_sem=back_sems.at[0],
        recv_sem=back_sems.at[1],
        device_id={"in": partner},
        device_id_type=MESH,
    )
    back.start()
    for step in range(n_chips):
        core_copy(step).wait_send()
    for step in range(n_chips - 1):
        rs_copy(step).wait_send()
    back.wait()


def sketch_of(masked, probe_pairs, rows, n_in, cid):
    width = masked.shape[1]
    sk = probe_pairs.shape[2]
    n_chips = n_in // 2
    half = rows // 2
    return pl.pallas_call(
        functools.partial(sketch_kernel, n_chips),
        out_shape=jax.ShapeDtypeStruct((rows, width, sk), jnp.bfloat16),
        in_specs=[pl.BlockSpec(memory_space=pltpu.VMEM)] * 2,
        out_specs=pl.BlockSpec(memory_space=pltpu.VMEM),
        scratch_shapes=[
            pltpu.VMEM((half, width, sk), jnp.bfloat16),
            pltpu.VMEM((half, width, sk), jnp.bfloat16),
            pltpu.VMEM((half, width, sk), jnp.bfloat16),
            pltpu.VMEM((n_chips, half // n_chips, width, sk), jnp.bfloat16),
            pltpu.SemaphoreType.DMA((n_chips,)),
            pltpu.SemaphoreType.DMA((n_chips,)),
            pltpu.SemaphoreType.DMA((n_chips,)),
            pltpu.SemaphoreType.DMA((n_chips,)),
            pltpu.SemaphoreType.DMA((n_chips,)),
            pltpu.SemaphoreType.DMA((n_chips,)),
            pltpu.SemaphoreType.DMA((2,)),
        ],
        compiler_params=pltpu.CompilerParams(
            collective_id=cid, has_side_effects=True, vmem_limit_bytes=60 * 1024 * 1024
        ),
    )(masked, probe_pairs)


def corange_kernel(
    n_out, mt_ref, sketch_ref, gram_ref, recv_ref, gram_recv, send_buf, co_send, co_recv, gram_send, gram_in, local_sems
):
    me = lax.axis_index("out")
    cols_all = send_buf.shape[1]
    m_width = mt_ref.shape[1]
    sk = sketch_ref.shape[2]
    rows = sketch_ref.shape[0]
    block = 4
    n_blocks = cols_all // (block * m_width)
    span = block * m_width
    per = sk // n_out

    barrier = pltpu.get_barrier_semaphore()
    for d in range(1, n_out):
        pl.semaphore_signal(barrier, inc=1, device_id={"out": lax.rem(me + d, n_out)}, device_id_type=MESH)
    pl.semaphore_wait(barrier, n_out - 1)

    def gram_copy(d):
        return pltpu.make_async_remote_copy(
            src_ref=gram_ref,
            dst_ref=gram_recv.at[me],
            send_sem=gram_send.at[d],
            recv_sem=gram_in.at[d],
            device_id={"out": lax.rem(me + d, n_out)},
            device_id_type=MESH,
        )

    gram_local = pltpu.make_async_copy(gram_ref, gram_recv.at[me], local_sems.at[n_blocks])
    gram_local.start()
    for d in range(1, n_out):
        gram_copy(d).start()

    def co_copy(d, b):
        k = lax.rem(me + d, n_out)
        return pltpu.make_async_remote_copy(
            src_ref=send_buf.at[pl.ds(pl.multiple_of(k * per, per), per), pl.ds(pl.multiple_of(b * span, span), span)],
            dst_ref=recv_ref.at[me, :, pl.ds(pl.multiple_of(b * span, span), span)],
            send_sem=co_send.at[d, b],
            recv_sem=co_recv.at[d, b],
            device_id={"out": k},
            device_id_type=MESH,
        )

    def local_copy(b):
        return pltpu.make_async_copy(
            send_buf.at[pl.ds(pl.multiple_of(me * per, per), per), pl.ds(pl.multiple_of(b * span, span), span)],
            recv_ref.at[me, :, pl.ds(pl.multiple_of(b * span, span), span)],
            local_sems.at[b],
        )

    def body(b, carry):
        j0 = b * block
        acc = jnp.zeros((span, sk), jnp.float32)
        for i in range(rows):
            lhs = mt_ref[pl.ds(j0 + i, block)].reshape(span, mt_ref.shape[2])
            acc = acc + jnp.dot(lhs, sketch_ref[i], preferred_element_type=jnp.float32)
        send_buf[:, pl.ds(pl.multiple_of(b * span, span), span)] = acc.T.astype(send_buf.dtype)
        local_copy(b).start()
        for d in range(1, n_out):
            co_copy(d, b).start()
        return carry

    lax.fori_loop(0, n_blocks, body, 0)

    def drain(b, carry):
        local_copy(b).wait()
        for d in range(1, n_out):
            co_copy(d, b).wait()
        return carry

    lax.fori_loop(0, n_blocks, drain, 0)
    gram_local.wait()
    for d in range(1, n_out):
        gram_copy(d).wait()


def corange_of(mt, sketch, gram_part, cols, n_out, cid):
    m_width = mt.shape[1]
    sk = sketch.shape[2]
    n_blocks = cols // 4
    return pl.pallas_call(
        functools.partial(corange_kernel, n_out),
        out_shape=(
            jax.ShapeDtypeStruct((n_out, sk // n_out, cols * m_width), jnp.bfloat16),
            jax.ShapeDtypeStruct((n_out,) + gram_part.shape, jnp.bfloat16),
        ),
        in_specs=[pl.BlockSpec(memory_space=pltpu.VMEM)] * 3,
        out_specs=(pl.BlockSpec(memory_space=pltpu.VMEM),) * 2,
        scratch_shapes=[
            pltpu.VMEM((sk, cols * m_width), jnp.bfloat16),
            pltpu.SemaphoreType.DMA((n_out, n_blocks)),
            pltpu.SemaphoreType.DMA((n_out, n_blocks)),
            pltpu.SemaphoreType.DMA((n_out,)),
            pltpu.SemaphoreType.DMA((n_out,)),
            pltpu.SemaphoreType.DMA((n_blocks + 1,)),
        ],
        compiler_params=pltpu.CompilerParams(
            collective_id=cid, has_side_effects=True, vmem_limit_bytes=60 * 1024 * 1024
        ),
    )(mt, sketch, gram_part)


def shards(n_out, n_in, markov, probes, pattern):
    keeper = jnp.repeat(jnp.repeat(pattern, BO, axis=0), BI, axis=1).astype(jnp.bfloat16)
    masked, mt, gathered = prep(markov, keeper, probes, n_out, 0)
    panel = gathered.reshape((-1,) + probes.shape[1:])
    s_all, cols, m_width = panel.shape
    probe_pairs = jnp.swapaxes(panel.reshape(s_all, cols // 2, 2 * m_width), 0, 1).swapaxes(1, 2)
    sketch = sketch_of(masked, probe_pairs, R, n_in, 1)
    rows, width, sk = sketch.shape
    local_gram = jnp.einsum("ips,ipt->st", sketch, sketch, preferred_element_type=jnp.float32)
    got, gram_got = corange_of(mt, sketch, local_gram.astype(jnp.bfloat16), cols, n_out, 4)
    corange = jnp.sum(got.astype(jnp.float32), axis=0).reshape(s_all // n_out, cols, m_width)
    gram_matrix = jnp.sum(gram_got.astype(jnp.float32), axis=0) / (R * OUTPUT_CHANNELS)
    return (sketch, corange, gram_matrix)


def solution(mesh):
    return jax.shard_map(
        functools.partial(shards, mesh.shape["out"], mesh.shape["in"]),
        mesh=mesh,
        in_specs=(P(None, "out", "in"), P("out", None, "in"), P("out", "in")),
        out_specs=(P(None, "out", None), P("out", None, "in"), P()),
        check_vma=False,
    )
```

```python
import functools

import jax
import jax.numpy as jnp
from jax import lax
from jax.experimental import pallas as pl
from jax.experimental.pallas import tpu as pltpu
from jax.sharding import PartitionSpec as P

OUTPUT_CHANNELS = 2048
BO = 64
BI = 128
R = 32
C = 32

MESH = pl.DeviceIdType.MESH


def forward_kernel(m_ref, probe_ref, out_ref):
    rows, width, sk = out_ref.shape
    steps = probe_ref.shape[0]
    m_width = m_ref.shape[2]
    block = 2

    def body(b, carry):
        i0 = b * block
        acc = jnp.zeros((block * width, sk), jnp.float32)
        for t in range(steps):
            lo = m_ref[pl.ds(i0 + 2 * t, block)].reshape(block * width, m_width)
            hi = m_ref[pl.ds(i0 + 2 * t + 1, block)].reshape(block * width, m_width)
            lhs = jnp.concatenate([lo, hi], axis=1)
            acc = acc + jnp.dot(lhs, probe_ref[t], preferred_element_type=jnp.float32)
        out_ref[pl.ds(i0, block)] = acc.reshape(block, width, sk)
        return carry

    lax.fori_loop(0, rows // block, body, 0)


def forward_panel(pair, probe_pairs, rows):
    width = pair.shape[1]
    sk = probe_pairs.shape[2]
    return pl.pallas_call(
        forward_kernel,
        out_shape=jax.ShapeDtypeStruct((rows, width, sk), jnp.float32),
        in_specs=[pl.BlockSpec(memory_space=pltpu.VMEM)] * 2,
        out_specs=pl.BlockSpec(memory_space=pltpu.VMEM),
        compiler_params=pltpu.CompilerParams(vmem_limit_bytes=60 * 1024 * 1024),
    )(pair, probe_pairs)


def backward_kernel(mt_ref, sketch_ref, out_ref):
    cols, m_width, sk = out_ref.shape
    rows = sketch_ref.shape[0]
    block = 4

    def body(b, carry):
        j0 = b * block
        acc = jnp.zeros((block * m_width, sk), jnp.float32)
        for i in range(rows):
            lhs = mt_ref[pl.ds(j0 + i, block)].reshape(block * m_width, mt_ref.shape[2])
            acc = acc + jnp.dot(lhs, sketch_ref[i], preferred_element_type=jnp.float32)
        out_ref[pl.ds(j0, block)] = acc.reshape(block, m_width, sk)
        return carry

    lax.fori_loop(0, cols // block, body, 0)


def prep_kernel(n_out, markov_ref, keeper_ref, probes_ref, masked_ref, gathered_ref, send_sem, recv_sem, local_sem):
    me = lax.axis_index("out")
    barrier = pltpu.get_barrier_semaphore()
    for d in range(1, n_out):
        pl.semaphore_signal(barrier, inc=1, device_id={"out": lax.rem(me + d, n_out)}, device_id_type=MESH)
    pl.semaphore_wait(barrier, n_out - 1)
    local = pltpu.make_async_copy(probes_ref, gathered_ref.at[me], local_sem)
    local.start()
    copies = []
    for d in range(1, n_out):
        copy = pltpu.make_async_remote_copy(
            src_ref=probes_ref,
            dst_ref=gathered_ref.at[me],
            send_sem=send_sem.at[d],
            recv_sem=recv_sem.at[d],
            device_id={"out": lax.rem(me + d, n_out)},
            device_id_type=MESH,
        )
        copy.start()
        copies.append(copy)

    keeper = keeper_ref[...]

    def body(k, carry):
        masked_ref[k] = markov_ref[k] * keeper
        return carry

    lax.fori_loop(0, markov_ref.shape[0], body, 0)
    local.wait()
    for copy in copies:
        copy.wait()


def prep(markov, keeper, probes, n_out, cid):
    lags, width, m_width = markov.shape
    return pl.pallas_call(
        functools.partial(prep_kernel, n_out),
        out_shape=(
            jax.ShapeDtypeStruct((lags, width, m_width), markov.dtype),
            jax.ShapeDtypeStruct((n_out,) + probes.shape, probes.dtype),
        ),
        in_specs=[pl.BlockSpec(memory_space=pltpu.VMEM)] * 3,
        out_specs=(pl.BlockSpec(memory_space=pltpu.VMEM),) * 2,
        scratch_shapes=[
            pltpu.SemaphoreType.DMA((n_out,)),
            pltpu.SemaphoreType.DMA((n_out,)),
            pltpu.SemaphoreType.DMA(()),
        ],
        compiler_params=pltpu.CompilerParams(
            collective_id=cid, has_side_effects=True, vmem_limit_bytes=60 * 1024 * 1024
        ),
    )(markov, keeper, probes)


def backward_panel(mt, sketch, cols):
    m_width = mt.shape[1]
    sk = sketch.shape[2]
    return pl.pallas_call(
        backward_kernel,
        out_shape=jax.ShapeDtypeStruct((cols, m_width, sk), jnp.float32),
        in_specs=[pl.BlockSpec(memory_space=pltpu.VMEM)] * 2,
        out_specs=pl.BlockSpec(memory_space=pltpu.VMEM),
        compiler_params=pltpu.CompilerParams(vmem_limit_bytes=60 * 1024 * 1024),
    )(mt, sketch)


def exchange_kernel(axis, n, stride, gather, x_ref, y_ref, send_sem, recv_sem, local_sem):
    me = lax.axis_index(axis)
    pos = lax.rem(me // stride, n)
    base = me - pos * stride

    def member(k):
        return base + k * stride

    barrier = pltpu.get_barrier_semaphore()
    for d in range(1, n):
        peer = lax.rem(pos + d, n)
        pl.semaphore_signal(barrier, inc=1, device_id={axis: member(peer)}, device_id_type=MESH)
    pl.semaphore_wait(barrier, n - 1)

    own_src = x_ref if gather else x_ref.at[pos]
    local = pltpu.make_async_copy(own_src, y_ref.at[pos], local_sem)
    local.start()
    copies = []
    for d in range(1, n):
        peer = lax.rem(pos + d, n)
        src = x_ref if gather else x_ref.at[peer]
        copy = pltpu.make_async_remote_copy(
            src_ref=src,
            dst_ref=y_ref.at[pos],
            send_sem=send_sem.at[d],
            recv_sem=recv_sem.at[d],
            device_id={axis: member(peer)},
            device_id_type=MESH,
        )
        copy.start()
        copies.append(copy)
    local.wait()
    for copy in copies:
        copy.wait()


def exchange(x, axis, n, stride, gather, cid):
    out_shape = (n,) + (x.shape if gather else x.shape[1:])
    return pl.pallas_call(
        functools.partial(exchange_kernel, axis, n, stride, gather),
        out_shape=jax.ShapeDtypeStruct(out_shape, x.dtype),
        in_specs=[pl.BlockSpec(memory_space=pl.ANY)],
        out_specs=pl.BlockSpec(memory_space=pl.ANY),
        scratch_shapes=[
            pltpu.SemaphoreType.DMA((n,)),
            pltpu.SemaphoreType.DMA((n,)),
            pltpu.SemaphoreType.DMA(()),
        ],
        compiler_params=pltpu.CompilerParams(collective_id=cid, has_side_effects=True),
    )(x)


def sketch_sum_kernel(
    n_chips, raw_ref, out_ref, half_send, core_buf, chip_send, chip_recv, core_sems, rs_send, rs_recv, ag_send, ag_recv
):
    me = lax.axis_index("in")
    core = lax.rem(me, 2)
    chip = me // 2
    partner = me + 1 - 2 * core
    rows = raw_ref.shape[0]
    half = rows // 2
    piece = half // n_chips
    my_half = core * half

    def chip_dev(k):
        return k * 2 + core

    barrier = pltpu.get_barrier_semaphore()
    pl.semaphore_signal(barrier, inc=1, device_id={"in": partner}, device_id_type=MESH)
    for d in range(1, n_chips):
        peer = lax.rem(chip + d, n_chips)
        pl.semaphore_signal(barrier, inc=1, device_id={"in": chip_dev(peer)}, device_id_type=MESH)
    pl.semaphore_wait(barrier, n_chips)

    other_half = (1 - core) * half

    def to_send(r, carry):
        half_send[r] = raw_ref[other_half + r].astype(half_send.dtype)
        return carry

    lax.fori_loop(0, half, to_send, 0)
    core_copy = pltpu.make_async_remote_copy(
        src_ref=half_send,
        dst_ref=core_buf,
        send_sem=core_sems.at[0],
        recv_sem=core_sems.at[1],
        device_id={"in": partner},
        device_id_type=MESH,
    )
    core_copy.start()
    core_copy.wait()

    def add_core(r, carry):
        chip_send[r] = (raw_ref[my_half + r] + core_buf[r].astype(jnp.float32)).astype(chip_send.dtype)
        return carry

    lax.fori_loop(0, half, add_core, 0)
    scatter = []
    for d in range(1, n_chips):
        peer = lax.rem(chip + d, n_chips)
        copy = pltpu.make_async_remote_copy(
            src_ref=chip_send.at[pl.ds(peer * piece, piece)],
            dst_ref=chip_recv.at[chip],
            send_sem=rs_send.at[d],
            recv_sem=rs_recv.at[d],
            device_id={"in": chip_dev(peer)},
            device_id_type=MESH,
        )
        copy.start()
        scatter.append(copy)
    for copy in scatter:
        copy.wait()

    base_row = my_half + chip * piece
    for q in range(piece):
        acc = chip_send[chip * piece + q].astype(jnp.float32)
        for d in range(1, n_chips):
            acc = acc + chip_recv[lax.rem(chip + d, n_chips), q].astype(jnp.float32)
        out_ref[base_row + q] = acc.astype(out_ref.dtype)

    gather = []
    for d in range(1, n_chips):
        peer = lax.rem(chip + d, n_chips)
        copy = pltpu.make_async_remote_copy(
            src_ref=out_ref.at[pl.ds(base_row, piece)],
            dst_ref=out_ref.at[pl.ds(base_row, piece)],
            send_sem=ag_send.at[d],
            recv_sem=ag_recv.at[d],
            device_id={"in": chip_dev(peer)},
            device_id_type=MESH,
        )
        copy.start()
        gather.append(copy)
    for copy in gather:
        copy.wait()
    core_back = pltpu.make_async_remote_copy(
        src_ref=out_ref.at[pl.ds(my_half, half)],
        dst_ref=out_ref.at[pl.ds(my_half, half)],
        send_sem=core_sems.at[2],
        recv_sem=core_sems.at[3],
        device_id={"in": partner},
        device_id_type=MESH,
    )
    core_back.start()
    core_back.wait()


def sketch_sum(raw, n_in, cid):
    rows, width, sk = raw.shape
    n_chips = n_in // 2
    half = rows // 2
    return pl.pallas_call(
        functools.partial(sketch_sum_kernel, n_chips),
        out_shape=jax.ShapeDtypeStruct(raw.shape, jnp.bfloat16),
        in_specs=[pl.BlockSpec(memory_space=pltpu.VMEM)],
        out_specs=pl.BlockSpec(memory_space=pltpu.VMEM),
        scratch_shapes=[
            pltpu.VMEM((half, width, sk), jnp.bfloat16),
            pltpu.VMEM((half, width, sk), jnp.bfloat16),
            pltpu.VMEM((half, width, sk), jnp.bfloat16),
            pltpu.VMEM((n_chips, half // n_chips, width, sk), jnp.bfloat16),
            pltpu.SemaphoreType.DMA((4,)),
            pltpu.SemaphoreType.DMA((n_chips,)),
            pltpu.SemaphoreType.DMA((n_chips,)),
            pltpu.SemaphoreType.DMA((n_chips,)),
            pltpu.SemaphoreType.DMA((n_chips,)),
        ],
        compiler_params=pltpu.CompilerParams(
            collective_id=cid, has_side_effects=True, vmem_limit_bytes=60 * 1024 * 1024
        ),
    )(raw)


def forward_rows(m_ref, probe_ref, i0, block):
    width, m_width = m_ref.shape[1], m_ref.shape[2]
    sk = probe_ref.shape[2]
    acc = jnp.zeros((block * width, sk), jnp.float32)
    for t in range(probe_ref.shape[0]):
        lo = m_ref[pl.ds(i0 + 2 * t, block)].reshape(block * width, m_width)
        hi = m_ref[pl.ds(i0 + 2 * t + 1, block)].reshape(block * width, m_width)
        lhs = jnp.concatenate([lo, hi], axis=1)
        acc = acc + jnp.dot(lhs, probe_ref[t], preferred_element_type=jnp.float32)
    return acc.reshape(block, width, sk)


def sketch_kernel(
    n_chips, m_ref, probe_ref, out_ref, mt_ref, half_send, core_buf, chip_send, chip_recv,
    core_send, core_recv, rs_send, rs_recv, ag_send, ag_recv, back_sems,
):
    me = lax.axis_index("in")
    core = lax.rem(me, 2)
    chip = me // 2
    partner = me + 1 - 2 * core
    rows = out_ref.shape[0]
    half = rows // 2
    piece = half // n_chips
    my_half = core * half
    other_half = (1 - core) * half

    def chip_dev(k):
        return k * 2 + core

    def chunk_of(step):
        return lax.rem(chip + step + 1, n_chips)

    def core_copy(step):
        c = chunk_of(step)
        return pltpu.make_async_remote_copy(
            src_ref=half_send.at[pl.ds(c * piece, piece)],
            dst_ref=core_buf.at[pl.ds(c * piece, piece)],
            send_sem=core_send.at[step],
            recv_sem=core_recv.at[step],
            device_id={"in": partner},
            device_id_type=MESH,
        )

    def rs_copy(step):
        c = chunk_of(step)
        return pltpu.make_async_remote_copy(
            src_ref=chip_send.at[pl.ds(c * piece, piece)],
            dst_ref=chip_recv.at[chip],
            send_sem=rs_send.at[step],
            recv_sem=rs_recv.at[step],
            device_id={"in": chip_dev(c)},
            device_id_type=MESH,
        )

    barrier = pltpu.get_barrier_semaphore()
    pl.semaphore_signal(barrier, inc=1, device_id={"in": partner}, device_id_type=MESH)
    for d in range(1, n_chips):
        pl.semaphore_signal(barrier, inc=1, device_id={"in": chip_dev(lax.rem(chip + d, n_chips))}, device_id_type=MESH)
    pl.semaphore_wait(barrier, n_chips)

    def partner_rows(step, carry):
        c = chunk_of(step)
        half_send[pl.ds(c * piece, piece)] = forward_rows(m_ref, probe_ref, other_half + c * piece, piece).astype(
            half_send.dtype
        )
        core_copy(step).start()
        return carry

    lax.fori_loop(0, n_chips, partner_rows, 0)

    def own_rows(step):
        c = chunk_of(step)
        mine = forward_rows(m_ref, probe_ref, my_half + c * piece, piece)
        core_copy(step).wait_recv()
        chip_send[pl.ds(c * piece, piece)] = (mine + core_buf[pl.ds(c * piece, piece)].astype(jnp.float32)).astype(
            chip_send.dtype
        )

    def chip_rows(step, carry):
        own_rows(step)
        rs_copy(step).start()
        return carry

    lax.fori_loop(0, n_chips - 1, chip_rows, 0)
    own_rows(n_chips - 1)

    for step in range(n_chips - 1):
        rs_copy(step).wait_recv()
    base_row = my_half + chip * piece
    for q in range(piece):
        acc = chip_send[chip * piece + q].astype(jnp.float32)
        for d in range(1, n_chips):
            acc = acc + chip_recv[lax.rem(chip + d, n_chips), q].astype(jnp.float32)
        out_ref[base_row + q] = acc.astype(out_ref.dtype)

    gather = []
    for d in range(1, n_chips):
        copy = pltpu.make_async_remote_copy(
            src_ref=out_ref.at[pl.ds(base_row, piece)],
            dst_ref=out_ref.at[pl.ds(base_row, piece)],
            send_sem=ag_send.at[d],
            recv_sem=ag_recv.at[d],
            device_id={"in": chip_dev(lax.rem(chip + d, n_chips))},
            device_id_type=MESH,
        )
        copy.start()
        gather.append(copy)

    def transpose_lag(k, carry):
        mt_ref[k] = m_ref[k].astype(jnp.float32).T.astype(mt_ref.dtype)
        return carry

    lax.fori_loop(0, m_ref.shape[0], transpose_lag, 0)
    for copy in gather:
        copy.wait()
    back = pltpu.make_async_remote_copy(
        src_ref=out_ref.at[pl.ds(my_half, half)],
        dst_ref=out_ref.at[pl.ds(my_half, half)],
        send_sem=back_sems.at[0],
        recv_sem=back_sems.at[1],
        device_id={"in": partner},
        device_id_type=MESH,
    )
    back.start()
    for step in range(n_chips):
        core_copy(step).wait_send()
    for step in range(n_chips - 1):
        rs_copy(step).wait_send()
    back.wait()


def sketch_of(masked, probe_pairs, rows, n_in, cid):
    lags, width, m_width = masked.shape
    sk = probe_pairs.shape[2]
    n_chips = n_in // 2
    half = rows // 2
    return pl.pallas_call(
        functools.partial(sketch_kernel, n_chips),
        out_shape=(
            jax.ShapeDtypeStruct((rows, width, sk), jnp.bfloat16),
            jax.ShapeDtypeStruct((lags, m_width, width), masked.dtype),
        ),
        in_specs=[pl.BlockSpec(memory_space=pltpu.VMEM)] * 2,
        out_specs=(pl.BlockSpec(memory_space=pltpu.VMEM),) * 2,
        scratch_shapes=[
            pltpu.VMEM((half, width, sk), jnp.bfloat16),
            pltpu.VMEM((half, width, sk), jnp.bfloat16),
            pltpu.VMEM((half, width, sk), jnp.bfloat16),
            pltpu.VMEM((n_chips, half // n_chips, width, sk), jnp.bfloat16),
            pltpu.SemaphoreType.DMA((n_chips,)),
            pltpu.SemaphoreType.DMA((n_chips,)),
            pltpu.SemaphoreType.DMA((n_chips,)),
            pltpu.SemaphoreType.DMA((n_chips,)),
            pltpu.SemaphoreType.DMA((n_chips,)),
            pltpu.SemaphoreType.DMA((n_chips,)),
            pltpu.SemaphoreType.DMA((2,)),
        ],
        compiler_params=pltpu.CompilerParams(
            collective_id=cid, has_side_effects=True, vmem_limit_bytes=60 * 1024 * 1024
        ),
    )(masked, probe_pairs)


def corange_kernel(
    n_out, mt_ref, sketch_ref, recv_ref, gram_recv, send_buf, gram_ref, co_send, co_recv, gram_send, gram_in, local_sems
):
    me = lax.axis_index("out")
    cols_all = send_buf.shape[1]
    m_width = mt_ref.shape[1]
    sk = sketch_ref.shape[2]
    rows = sketch_ref.shape[0]
    block = 4
    n_blocks = cols_all // (block * m_width)
    span = block * m_width
    per = sk // n_out

    barrier = pltpu.get_barrier_semaphore()
    for d in range(1, n_out):
        pl.semaphore_signal(barrier, inc=1, device_id={"out": lax.rem(me + d, n_out)}, device_id_type=MESH)
    pl.semaphore_wait(barrier, n_out - 1)

    def gram_copy(d):
        return pltpu.make_async_remote_copy(
            src_ref=gram_ref,
            dst_ref=gram_recv.at[me],
            send_sem=gram_send.at[d],
            recv_sem=gram_in.at[d],
            device_id={"out": lax.rem(me + d, n_out)},
            device_id_type=MESH,
        )

    gram_local = pltpu.make_async_copy(gram_ref, gram_recv.at[me], local_sems.at[n_blocks])

    def co_copy(d, b):
        k = lax.rem(me + d, n_out)
        return pltpu.make_async_remote_copy(
            src_ref=send_buf.at[pl.ds(pl.multiple_of(k * per, per), per), pl.ds(pl.multiple_of(b * span, span), span)],
            dst_ref=recv_ref.at[me, :, pl.ds(pl.multiple_of(b * span, span), span)],
            send_sem=co_send.at[d, b],
            recv_sem=co_recv.at[d, b],
            device_id={"out": k},
            device_id_type=MESH,
        )

    def local_copy(b):
        return pltpu.make_async_copy(
            send_buf.at[pl.ds(pl.multiple_of(me * per, per), per), pl.ds(pl.multiple_of(b * span, span), span)],
            recv_ref.at[me, :, pl.ds(pl.multiple_of(b * span, span), span)],
            local_sems.at[b],
        )

    def body(b, carry):
        j0 = b * block
        acc = jnp.zeros((span, sk), jnp.float32)
        for i in range(rows):
            lhs = mt_ref[pl.ds(j0 + i, block)].reshape(span, mt_ref.shape[2])
            acc = acc + jnp.dot(lhs, sketch_ref[i], preferred_element_type=jnp.float32)
        send_buf[:, pl.ds(pl.multiple_of(b * span, span), span)] = acc.T.astype(send_buf.dtype)
        local_copy(b).start()
        for d in range(1, n_out):
            co_copy(d, b).start()
        return carry

    lax.fori_loop(0, n_blocks, body, 0)

    def gram_rows(i, acc):
        value = sketch_ref[i]
        return acc + jnp.dot(value.astype(jnp.float32).T.astype(value.dtype), value, preferred_element_type=jnp.float32)

    gram = lax.fori_loop(0, rows, gram_rows, jnp.zeros((sk, sk), jnp.float32))
    gram_ref[...] = gram.astype(gram_ref.dtype)
    gram_local.start()
    for d in range(1, n_out):
        gram_copy(d).start()

    def drain(b, carry):
        local_copy(b).wait()
        for d in range(1, n_out):
            co_copy(d, b).wait()
        return carry

    lax.fori_loop(0, n_blocks, drain, 0)
    gram_local.wait()
    for d in range(1, n_out):
        gram_copy(d).wait()


def corange_of(mt, sketch, cols, n_out, cid):
    m_width = mt.shape[1]
    sk = sketch.shape[2]
    n_blocks = cols // 4
    return pl.pallas_call(
        functools.partial(corange_kernel, n_out),
        out_shape=(
            jax.ShapeDtypeStruct((n_out, sk // n_out, cols * m_width), jnp.bfloat16),
            jax.ShapeDtypeStruct((n_out, sk, sk), jnp.bfloat16),
        ),
        in_specs=[pl.BlockSpec(memory_space=pltpu.VMEM)] * 2,
        out_specs=(pl.BlockSpec(memory_space=pltpu.VMEM),) * 2,
        scratch_shapes=[
            pltpu.VMEM((sk, cols * m_width), jnp.bfloat16),
            pltpu.VMEM((sk, sk), jnp.bfloat16),
            pltpu.SemaphoreType.DMA((n_out, n_blocks)),
            pltpu.SemaphoreType.DMA((n_out, n_blocks)),
            pltpu.SemaphoreType.DMA((n_out,)),
            pltpu.SemaphoreType.DMA((n_out,)),
            pltpu.SemaphoreType.DMA((n_blocks + 1,)),
        ],
        compiler_params=pltpu.CompilerParams(
            collective_id=cid, has_side_effects=True, vmem_limit_bytes=60 * 1024 * 1024
        ),
    )(mt, sketch)


def shards(n_out, n_in, markov, probes, pattern):
    keeper = jnp.repeat(jnp.repeat(pattern, BO, axis=0), BI, axis=1).astype(jnp.bfloat16)
    masked, gathered = prep(markov, keeper, probes, n_out, 0)
    panel = gathered.reshape((-1,) + probes.shape[1:])
    s_all, cols, m_width = panel.shape
    probe_pairs = jnp.swapaxes(panel.reshape(s_all, cols // 2, 2 * m_width), 0, 1).swapaxes(1, 2)
    sketch, mt = sketch_of(masked, probe_pairs, R, n_in, 1)
    got, gram_got = corange_of(mt, sketch, cols, n_out, 4)
    corange = jnp.sum(got.astype(jnp.float32), axis=0).reshape(s_all // n_out, cols, m_width)
    gram_matrix = jnp.sum(gram_got.astype(jnp.float32), axis=0) / (R * OUTPUT_CHANNELS)
    return (sketch, corange, gram_matrix)


def solution(mesh):
    return jax.shard_map(
        functools.partial(shards, mesh.shape["out"], mesh.shape["in"]),
        mesh=mesh,
        in_specs=(P(None, "out", "in"), P("out", None, "in"), P("out", "in")),
        out_specs=(P(None, "out", None), P("out", None, "in"), P()),
        check_vma=False,
    )
```

```python
import functools

import jax
import jax.numpy as jnp
from jax import lax
from jax.experimental import pallas as pl
from jax.experimental.pallas import tpu as pltpu
from jax.sharding import PartitionSpec as P

OUTPUT_CHANNELS = 2048
BO = 64
BI = 128
R = 32
C = 32

MESH = pl.DeviceIdType.MESH


def forward_kernel(m_ref, probe_ref, out_ref):
    rows, width, sk = out_ref.shape
    steps = probe_ref.shape[0]
    m_width = m_ref.shape[2]
    block = 2

    def body(b, carry):
        i0 = b * block
        acc = jnp.zeros((block * width, sk), jnp.float32)
        for t in range(steps):
            lo = m_ref[pl.ds(i0 + 2 * t, block)].reshape(block * width, m_width)
            hi = m_ref[pl.ds(i0 + 2 * t + 1, block)].reshape(block * width, m_width)
            lhs = jnp.concatenate([lo, hi], axis=1)
            acc = acc + jnp.dot(lhs, probe_ref[t], preferred_element_type=jnp.float32)
        out_ref[pl.ds(i0, block)] = acc.reshape(block, width, sk)
        return carry

    lax.fori_loop(0, rows // block, body, 0)


def forward_panel(pair, probe_pairs, rows):
    width = pair.shape[1]
    sk = probe_pairs.shape[2]
    return pl.pallas_call(
        forward_kernel,
        out_shape=jax.ShapeDtypeStruct((rows, width, sk), jnp.float32),
        in_specs=[pl.BlockSpec(memory_space=pltpu.VMEM)] * 2,
        out_specs=pl.BlockSpec(memory_space=pltpu.VMEM),
        compiler_params=pltpu.CompilerParams(vmem_limit_bytes=60 * 1024 * 1024),
    )(pair, probe_pairs)


def backward_kernel(mt_ref, sketch_ref, out_ref):
    cols, m_width, sk = out_ref.shape
    rows = sketch_ref.shape[0]
    block = 4

    def body(b, carry):
        j0 = b * block
        acc = jnp.zeros((block * m_width, sk), jnp.float32)
        for i in range(rows):
            lhs = mt_ref[pl.ds(j0 + i, block)].reshape(block * m_width, mt_ref.shape[2])
            acc = acc + jnp.dot(lhs, sketch_ref[i], preferred_element_type=jnp.float32)
        out_ref[pl.ds(j0, block)] = acc.reshape(block, m_width, sk)
        return carry

    lax.fori_loop(0, cols // block, body, 0)


def prep_kernel(n_out, markov_ref, keeper_ref, probes_ref, masked_ref, mt_ref, gathered_ref, send_sem, recv_sem, local_sem):
    me = lax.axis_index("out")
    barrier = pltpu.get_barrier_semaphore()
    for d in range(1, n_out):
        pl.semaphore_signal(barrier, inc=1, device_id={"out": lax.rem(me + d, n_out)}, device_id_type=MESH)
    pl.semaphore_wait(barrier, n_out - 1)
    local = pltpu.make_async_copy(probes_ref, gathered_ref.at[me], local_sem)
    local.start()
    copies = []
    for d in range(1, n_out):
        copy = pltpu.make_async_remote_copy(
            src_ref=probes_ref,
            dst_ref=gathered_ref.at[me],
            send_sem=send_sem.at[d],
            recv_sem=recv_sem.at[d],
            device_id={"out": lax.rem(me + d, n_out)},
            device_id_type=MESH,
        )
        copy.start()
        copies.append(copy)

    keeper = keeper_ref[...]

    def body(k, carry):
        value = markov_ref[k] * keeper
        masked_ref[k] = value
        mt_ref[k] = value.astype(jnp.float32).T.astype(mt_ref.dtype)
        return carry

    lax.fori_loop(0, markov_ref.shape[0], body, 0)
    local.wait()
    for copy in copies:
        copy.wait()


def prep(markov, keeper, probes, n_out, cid):
    lags, width, m_width = markov.shape
    return pl.pallas_call(
        functools.partial(prep_kernel, n_out),
        out_shape=(
            jax.ShapeDtypeStruct((lags, width, m_width), markov.dtype),
            jax.ShapeDtypeStruct((lags, m_width, width), markov.dtype),
            jax.ShapeDtypeStruct((n_out,) + probes.shape, probes.dtype),
        ),
        in_specs=[pl.BlockSpec(memory_space=pltpu.VMEM)] * 3,
        out_specs=(pl.BlockSpec(memory_space=pltpu.VMEM),) * 3,
        scratch_shapes=[
            pltpu.SemaphoreType.DMA((n_out,)),
            pltpu.SemaphoreType.DMA((n_out,)),
            pltpu.SemaphoreType.DMA(()),
        ],
        compiler_params=pltpu.CompilerParams(
            collective_id=cid, has_side_effects=True, vmem_limit_bytes=60 * 1024 * 1024
        ),
    )(markov, keeper, probes)


def backward_panel(mt, sketch, cols):
    m_width = mt.shape[1]
    sk = sketch.shape[2]
    return pl.pallas_call(
        backward_kernel,
        out_shape=jax.ShapeDtypeStruct((cols, m_width, sk), jnp.float32),
        in_specs=[pl.BlockSpec(memory_space=pltpu.VMEM)] * 2,
        out_specs=pl.BlockSpec(memory_space=pltpu.VMEM),
        compiler_params=pltpu.CompilerParams(vmem_limit_bytes=60 * 1024 * 1024),
    )(mt, sketch)


def exchange_kernel(axis, n, stride, gather, x_ref, y_ref, send_sem, recv_sem, local_sem):
    me = lax.axis_index(axis)
    pos = lax.rem(me // stride, n)
    base = me - pos * stride

    def member(k):
        return base + k * stride

    barrier = pltpu.get_barrier_semaphore()
    for d in range(1, n):
        peer = lax.rem(pos + d, n)
        pl.semaphore_signal(barrier, inc=1, device_id={axis: member(peer)}, device_id_type=MESH)
    pl.semaphore_wait(barrier, n - 1)

    own_src = x_ref if gather else x_ref.at[pos]
    local = pltpu.make_async_copy(own_src, y_ref.at[pos], local_sem)
    local.start()
    copies = []
    for d in range(1, n):
        peer = lax.rem(pos + d, n)
        src = x_ref if gather else x_ref.at[peer]
        copy = pltpu.make_async_remote_copy(
            src_ref=src,
            dst_ref=y_ref.at[pos],
            send_sem=send_sem.at[d],
            recv_sem=recv_sem.at[d],
            device_id={axis: member(peer)},
            device_id_type=MESH,
        )
        copy.start()
        copies.append(copy)
    local.wait()
    for copy in copies:
        copy.wait()


def exchange(x, axis, n, stride, gather, cid):
    out_shape = (n,) + (x.shape if gather else x.shape[1:])
    return pl.pallas_call(
        functools.partial(exchange_kernel, axis, n, stride, gather),
        out_shape=jax.ShapeDtypeStruct(out_shape, x.dtype),
        in_specs=[pl.BlockSpec(memory_space=pl.ANY)],
        out_specs=pl.BlockSpec(memory_space=pl.ANY),
        scratch_shapes=[
            pltpu.SemaphoreType.DMA((n,)),
            pltpu.SemaphoreType.DMA((n,)),
            pltpu.SemaphoreType.DMA(()),
        ],
        compiler_params=pltpu.CompilerParams(collective_id=cid, has_side_effects=True),
    )(x)


def sketch_sum_kernel(
    n_chips, raw_ref, out_ref, half_send, core_buf, chip_send, chip_recv, core_sems, rs_send, rs_recv, ag_send, ag_recv
):
    me = lax.axis_index("in")
    core = lax.rem(me, 2)
    chip = me // 2
    partner = me + 1 - 2 * core
    rows = raw_ref.shape[0]
    half = rows // 2
    piece = half // n_chips
    my_half = core * half

    def chip_dev(k):
        return k * 2 + core

    barrier = pltpu.get_barrier_semaphore()
    pl.semaphore_signal(barrier, inc=1, device_id={"in": partner}, device_id_type=MESH)
    for d in range(1, n_chips):
        peer = lax.rem(chip + d, n_chips)
        pl.semaphore_signal(barrier, inc=1, device_id={"in": chip_dev(peer)}, device_id_type=MESH)
    pl.semaphore_wait(barrier, n_chips)

    other_half = (1 - core) * half

    def to_send(r, carry):
        half_send[r] = raw_ref[other_half + r].astype(half_send.dtype)
        return carry

    lax.fori_loop(0, half, to_send, 0)
    core_copy = pltpu.make_async_remote_copy(
        src_ref=half_send,
        dst_ref=core_buf,
        send_sem=core_sems.at[0],
        recv_sem=core_sems.at[1],
        device_id={"in": partner},
        device_id_type=MESH,
    )
    core_copy.start()
    core_copy.wait()

    def add_core(r, carry):
        chip_send[r] = (raw_ref[my_half + r] + core_buf[r].astype(jnp.float32)).astype(chip_send.dtype)
        return carry

    lax.fori_loop(0, half, add_core, 0)
    scatter = []
    for d in range(1, n_chips):
        peer = lax.rem(chip + d, n_chips)
        copy = pltpu.make_async_remote_copy(
            src_ref=chip_send.at[pl.ds(peer * piece, piece)],
            dst_ref=chip_recv.at[chip],
            send_sem=rs_send.at[d],
            recv_sem=rs_recv.at[d],
            device_id={"in": chip_dev(peer)},
            device_id_type=MESH,
        )
        copy.start()
        scatter.append(copy)
    for copy in scatter:
        copy.wait()

    base_row = my_half + chip * piece
    for q in range(piece):
        acc = chip_send[chip * piece + q].astype(jnp.float32)
        for d in range(1, n_chips):
            acc = acc + chip_recv[lax.rem(chip + d, n_chips), q].astype(jnp.float32)
        out_ref[base_row + q] = acc.astype(out_ref.dtype)

    gather = []
    for d in range(1, n_chips):
        peer = lax.rem(chip + d, n_chips)
        copy = pltpu.make_async_remote_copy(
            src_ref=out_ref.at[pl.ds(base_row, piece)],
            dst_ref=out_ref.at[pl.ds(base_row, piece)],
            send_sem=ag_send.at[d],
            recv_sem=ag_recv.at[d],
            device_id={"in": chip_dev(peer)},
            device_id_type=MESH,
        )
        copy.start()
        gather.append(copy)
    for copy in gather:
        copy.wait()
    core_back = pltpu.make_async_remote_copy(
        src_ref=out_ref.at[pl.ds(my_half, half)],
        dst_ref=out_ref.at[pl.ds(my_half, half)],
        send_sem=core_sems.at[2],
        recv_sem=core_sems.at[3],
        device_id={"in": partner},
        device_id_type=MESH,
    )
    core_back.start()
    core_back.wait()


def sketch_sum(raw, n_in, cid):
    rows, width, sk = raw.shape
    n_chips = n_in // 2
    half = rows // 2
    return pl.pallas_call(
        functools.partial(sketch_sum_kernel, n_chips),
        out_shape=jax.ShapeDtypeStruct(raw.shape, jnp.bfloat16),
        in_specs=[pl.BlockSpec(memory_space=pltpu.VMEM)],
        out_specs=pl.BlockSpec(memory_space=pltpu.VMEM),
        scratch_shapes=[
            pltpu.VMEM((half, width, sk), jnp.bfloat16),
            pltpu.VMEM((half, width, sk), jnp.bfloat16),
            pltpu.VMEM((half, width, sk), jnp.bfloat16),
            pltpu.VMEM((n_chips, half // n_chips, width, sk), jnp.bfloat16),
            pltpu.SemaphoreType.DMA((4,)),
            pltpu.SemaphoreType.DMA((n_chips,)),
            pltpu.SemaphoreType.DMA((n_chips,)),
            pltpu.SemaphoreType.DMA((n_chips,)),
            pltpu.SemaphoreType.DMA((n_chips,)),
        ],
        compiler_params=pltpu.CompilerParams(
            collective_id=cid, has_side_effects=True, vmem_limit_bytes=60 * 1024 * 1024
        ),
    )(raw)


def forward_rows(m_ref, probe_ref, i0, block):
    width, m_width = m_ref.shape[1], m_ref.shape[2]
    sk = probe_ref.shape[2]
    acc = jnp.zeros((block * width, sk), jnp.float32)
    for t in range(probe_ref.shape[0]):
        lo = m_ref[pl.ds(i0 + 2 * t, block)].reshape(block * width, m_width)
        hi = m_ref[pl.ds(i0 + 2 * t + 1, block)].reshape(block * width, m_width)
        lhs = jnp.concatenate([lo, hi], axis=1)
        acc = acc + jnp.dot(lhs, probe_ref[t], preferred_element_type=jnp.float32)
    return acc.reshape(block, width, sk)


def sketch_kernel(
    n_chips, m_ref, probe_ref, out_ref, half_send, core_buf, chip_send, chip_recv,
    core_send, core_recv, rs_send, rs_recv, ag_send, ag_recv, back_sems,
):
    me = lax.axis_index("in")
    core = lax.rem(me, 2)
    chip = me // 2
    partner = me + 1 - 2 * core
    rows = out_ref.shape[0]
    half = rows // 2
    piece = half // n_chips
    my_half = core * half
    other_half = (1 - core) * half

    def chip_dev(k):
        return k * 2 + core

    def chunk_of(step):
        return lax.rem(chip + step + 1, n_chips)

    def core_copy(step):
        c = chunk_of(step)
        return pltpu.make_async_remote_copy(
            src_ref=half_send.at[pl.ds(c * piece, piece)],
            dst_ref=core_buf.at[pl.ds(c * piece, piece)],
            send_sem=core_send.at[step],
            recv_sem=core_recv.at[step],
            device_id={"in": partner},
            device_id_type=MESH,
        )

    def rs_copy(step):
        c = chunk_of(step)
        return pltpu.make_async_remote_copy(
            src_ref=chip_send.at[pl.ds(c * piece, piece)],
            dst_ref=chip_recv.at[chip],
            send_sem=rs_send.at[step],
            recv_sem=rs_recv.at[step],
            device_id={"in": chip_dev(c)},
            device_id_type=MESH,
        )

    barrier = pltpu.get_barrier_semaphore()
    pl.semaphore_signal(barrier, inc=1, device_id={"in": partner}, device_id_type=MESH)
    for d in range(1, n_chips):
        pl.semaphore_signal(barrier, inc=1, device_id={"in": chip_dev(lax.rem(chip + d, n_chips))}, device_id_type=MESH)
    pl.semaphore_wait(barrier, n_chips)

    def partner_rows(step, carry):
        c = chunk_of(step)
        half_send[pl.ds(c * piece, piece)] = forward_rows(m_ref, probe_ref, other_half + c * piece, piece).astype(
            half_send.dtype
        )
        core_copy(step).start()
        return carry

    lax.fori_loop(0, n_chips, partner_rows, 0)

    def own_rows(step):
        c = chunk_of(step)
        mine = forward_rows(m_ref, probe_ref, my_half + c * piece, piece)
        core_copy(step).wait_recv()
        chip_send[pl.ds(c * piece, piece)] = (mine + core_buf[pl.ds(c * piece, piece)].astype(jnp.float32)).astype(
            chip_send.dtype
        )

    def chip_rows(step, carry):
        own_rows(step)
        rs_copy(step).start()
        return carry

    lax.fori_loop(0, n_chips - 1, chip_rows, 0)
    own_rows(n_chips - 1)

    for step in range(n_chips - 1):
        rs_copy(step).wait_recv()
    base_row = my_half + chip * piece
    for q in range(piece):
        acc = chip_send[chip * piece + q].astype(jnp.float32)
        for d in range(1, n_chips):
            acc = acc + chip_recv[lax.rem(chip + d, n_chips), q].astype(jnp.float32)
        out_ref[base_row + q] = acc.astype(out_ref.dtype)

    gather = []
    for d in range(1, n_chips):
        copy = pltpu.make_async_remote_copy(
            src_ref=out_ref.at[pl.ds(base_row, piece)],
            dst_ref=out_ref.at[pl.ds(base_row, piece)],
            send_sem=ag_send.at[d],
            recv_sem=ag_recv.at[d],
            device_id={"in": chip_dev(lax.rem(chip + d, n_chips))},
            device_id_type=MESH,
        )
        copy.start()
        gather.append(copy)
    for copy in gather:
        copy.wait()
    back = pltpu.make_async_remote_copy(
        src_ref=out_ref.at[pl.ds(my_half, half)],
        dst_ref=out_ref.at[pl.ds(my_half, half)],
        send_sem=back_sems.at[0],
        recv_sem=back_sems.at[1],
        device_id={"in": partner},
        device_id_type=MESH,
    )
    back.start()
    for step in range(n_chips):
        core_copy(step).wait_send()
    for step in range(n_chips - 1):
        rs_copy(step).wait_send()
    back.wait()


def sketch_of(masked, probe_pairs, rows, n_in, cid):
    width = masked.shape[1]
    sk = probe_pairs.shape[2]
    n_chips = n_in // 2
    half = rows // 2
    return pl.pallas_call(
        functools.partial(sketch_kernel, n_chips),
        out_shape=jax.ShapeDtypeStruct((rows, width, sk), jnp.bfloat16),
        in_specs=[pl.BlockSpec(memory_space=pltpu.VMEM)] * 2,
        out_specs=pl.BlockSpec(memory_space=pltpu.VMEM),
        scratch_shapes=[
            pltpu.VMEM((half, width, sk), jnp.bfloat16),
            pltpu.VMEM((half, width, sk), jnp.bfloat16),
            pltpu.VMEM((half, width, sk), jnp.bfloat16),
            pltpu.VMEM((n_chips, half // n_chips, width, sk), jnp.bfloat16),
            pltpu.SemaphoreType.DMA((n_chips,)),
            pltpu.SemaphoreType.DMA((n_chips,)),
            pltpu.SemaphoreType.DMA((n_chips,)),
            pltpu.SemaphoreType.DMA((n_chips,)),
            pltpu.SemaphoreType.DMA((n_chips,)),
            pltpu.SemaphoreType.DMA((n_chips,)),
            pltpu.SemaphoreType.DMA((2,)),
        ],
        compiler_params=pltpu.CompilerParams(
            collective_id=cid, has_side_effects=True, vmem_limit_bytes=60 * 1024 * 1024
        ),
    )(masked, probe_pairs)


def corange_kernel(
    n_out, scale, mt_ref, sketch_ref, gram_ref, co_out, gram_out, recv_ref, gram_recv, send_buf,
    co_send, co_recv, gram_send, gram_in, local_sems
):
    me = lax.axis_index("out")
    cols_all = send_buf.shape[1]
    m_width = mt_ref.shape[1]
    sk = sketch_ref.shape[2]
    rows = sketch_ref.shape[0]
    block = 4
    n_blocks = cols_all // (block * m_width)
    span = block * m_width
    per = sk // n_out

    barrier = pltpu.get_barrier_semaphore()
    for d in range(1, n_out):
        pl.semaphore_signal(barrier, inc=1, device_id={"out": lax.rem(me + d, n_out)}, device_id_type=MESH)
    pl.semaphore_wait(barrier, n_out - 1)

    def gram_copy(d):
        return pltpu.make_async_remote_copy(
            src_ref=gram_ref,
            dst_ref=gram_recv.at[me],
            send_sem=gram_send.at[d],
            recv_sem=gram_in.at[d],
            device_id={"out": lax.rem(me + d, n_out)},
            device_id_type=MESH,
        )

    gram_local = pltpu.make_async_copy(gram_ref, gram_recv.at[me], local_sems.at[n_blocks])
    gram_local.start()
    for d in range(1, n_out):
        gram_copy(d).start()

    def co_copy(d, b):
        k = lax.rem(me + d, n_out)
        return pltpu.make_async_remote_copy(
            src_ref=send_buf.at[pl.ds(pl.multiple_of(k * per, per), per), pl.ds(pl.multiple_of(b * span, span), span)],
            dst_ref=recv_ref.at[me, :, pl.ds(pl.multiple_of(b * span, span), span)],
            send_sem=co_send.at[d, b],
            recv_sem=co_recv.at[d, b],
            device_id={"out": k},
            device_id_type=MESH,
        )

    def local_copy(b):
        return pltpu.make_async_copy(
            send_buf.at[pl.ds(pl.multiple_of(me * per, per), per), pl.ds(pl.multiple_of(b * span, span), span)],
            recv_ref.at[me, :, pl.ds(pl.multiple_of(b * span, span), span)],
            local_sems.at[b],
        )

    def body(b, carry):
        j0 = b * block
        acc = jnp.zeros((span, sk), jnp.float32)
        for i in range(rows):
            lhs = mt_ref[pl.ds(j0 + i, block)].reshape(span, mt_ref.shape[2])
            acc = acc + jnp.dot(lhs, sketch_ref[i], preferred_element_type=jnp.float32)
        send_buf[:, pl.ds(pl.multiple_of(b * span, span), span)] = acc.T.astype(send_buf.dtype)
        local_copy(b).start()
        for d in range(1, n_out):
            co_copy(d, b).start()
        return carry

    lax.fori_loop(0, n_blocks, body, 0)

    def drain(b, carry):
        local_copy(b).wait()
        for d in range(1, n_out):
            co_copy(d, b).wait()
        return carry

    lax.fori_loop(0, n_blocks, drain, 0)
    gram_local.wait()
    for d in range(1, n_out):
        gram_copy(d).wait()
    co_total = recv_ref[0].astype(jnp.float32)
    gram_total = gram_recv[0].astype(jnp.float32)
    for k in range(1, n_out):
        co_total = co_total + recv_ref[k].astype(jnp.float32)
        gram_total = gram_total + gram_recv[k].astype(jnp.float32)
    co_out[...] = co_total
    gram_out[...] = gram_total * scale


def corange_of(mt, sketch, gram_part, cols, n_out, cid):
    m_width = mt.shape[1]
    sk = sketch.shape[2]
    n_blocks = cols // 4
    return pl.pallas_call(
        functools.partial(corange_kernel, n_out, 1.0 / (R * OUTPUT_CHANNELS)),
        out_shape=(
            jax.ShapeDtypeStruct((sk // n_out, cols * m_width), jnp.float32),
            jax.ShapeDtypeStruct(gram_part.shape, jnp.float32),
        ),
        in_specs=[pl.BlockSpec(memory_space=pltpu.VMEM)] * 3,
        out_specs=(pl.BlockSpec(memory_space=pltpu.VMEM),) * 2,
        scratch_shapes=[
            pltpu.VMEM((n_out, sk // n_out, cols * m_width), jnp.bfloat16),
            pltpu.VMEM((n_out,) + gram_part.shape, jnp.bfloat16),
            pltpu.VMEM((sk, cols * m_width), jnp.bfloat16),
            pltpu.SemaphoreType.DMA((n_out, n_blocks)),
            pltpu.SemaphoreType.DMA((n_out, n_blocks)),
            pltpu.SemaphoreType.DMA((n_out,)),
            pltpu.SemaphoreType.DMA((n_out,)),
            pltpu.SemaphoreType.DMA((n_blocks + 1,)),
        ],
        compiler_params=pltpu.CompilerParams(
            collective_id=cid, has_side_effects=True, vmem_limit_bytes=60 * 1024 * 1024
        ),
    )(mt, sketch, gram_part)


def shards(n_out, n_in, markov, probes, pattern):
    keeper = jnp.repeat(jnp.repeat(pattern, BO, axis=0), BI, axis=1).astype(jnp.bfloat16)
    masked, mt, gathered = prep(markov, keeper, probes, n_out, 0)
    panel = gathered.reshape((-1,) + probes.shape[1:])
    s_all, cols, m_width = panel.shape
    probe_pairs = jnp.swapaxes(panel.reshape(s_all, cols // 2, 2 * m_width), 0, 1).swapaxes(1, 2)
    sketch = sketch_of(masked, probe_pairs, R, n_in, 1)
    rows, width, sk = sketch.shape
    local_gram = jnp.einsum("ips,ipt->st", sketch, sketch, preferred_element_type=jnp.float32)
    co_sum, gram_matrix = corange_of(mt, sketch, local_gram.astype(jnp.bfloat16), cols, n_out, 4)
    corange = co_sum.reshape(s_all // n_out, cols, m_width)
    return (sketch, corange, gram_matrix)


def solution(mesh):
    return jax.shard_map(
        functools.partial(shards, mesh.shape["out"], mesh.shape["in"]),
        mesh=mesh,
        in_specs=(P(None, "out", "in"), P("out", None, "in"), P("out", "in")),
        out_specs=(P(None, "out", None), P("out", None, "in"), P()),
        check_vma=False,
    )
```

```python
import functools

import jax
import jax.numpy as jnp
from jax import lax
from jax.experimental import pallas as pl
from jax.experimental.pallas import tpu as pltpu
from jax.sharding import PartitionSpec as P

OUTPUT_CHANNELS = 2048
BO = 64
BI = 128
R = 32
C = 32

MESH = pl.DeviceIdType.MESH


def forward_kernel(m_ref, probe_ref, out_ref):
    rows, width, sk = out_ref.shape
    steps = probe_ref.shape[0]
    m_width = m_ref.shape[2]
    block = 2

    def body(b, carry):
        i0 = b * block
        acc = jnp.zeros((block * width, sk), jnp.float32)
        for t in range(steps):
            lo = m_ref[pl.ds(i0 + 2 * t, block)].reshape(block * width, m_width)
            hi = m_ref[pl.ds(i0 + 2 * t + 1, block)].reshape(block * width, m_width)
            lhs = jnp.concatenate([lo, hi], axis=1)
            acc = acc + jnp.dot(lhs, probe_ref[t], preferred_element_type=jnp.float32)
        out_ref[pl.ds(i0, block)] = acc.reshape(block, width, sk)
        return carry

    lax.fori_loop(0, rows // block, body, 0)


def forward_panel(pair, probe_pairs, rows):
    width = pair.shape[1]
    sk = probe_pairs.shape[2]
    return pl.pallas_call(
        forward_kernel,
        out_shape=jax.ShapeDtypeStruct((rows, width, sk), jnp.float32),
        in_specs=[pl.BlockSpec(memory_space=pltpu.VMEM)] * 2,
        out_specs=pl.BlockSpec(memory_space=pltpu.VMEM),
        compiler_params=pltpu.CompilerParams(vmem_limit_bytes=60 * 1024 * 1024),
    )(pair, probe_pairs)


def backward_kernel(mt_ref, sketch_ref, out_ref):
    cols, m_width, sk = out_ref.shape
    rows = sketch_ref.shape[0]
    block = 4

    def body(b, carry):
        j0 = b * block
        acc = jnp.zeros((block * m_width, sk), jnp.float32)
        for i in range(rows):
            lhs = mt_ref[pl.ds(j0 + i, block)].reshape(block * m_width, mt_ref.shape[2])
            acc = acc + jnp.dot(lhs, sketch_ref[i], preferred_element_type=jnp.float32)
        out_ref[pl.ds(j0, block)] = acc.reshape(block, m_width, sk)
        return carry

    lax.fori_loop(0, cols // block, body, 0)


def prep_kernel(n_out, markov_ref, keeper_ref, probes_ref, masked_ref, mt_ref, gathered_ref, send_sem, recv_sem, local_sem):
    me = lax.axis_index("out")
    barrier = pltpu.get_barrier_semaphore()
    for d in range(1, n_out):
        pl.semaphore_signal(barrier, inc=1, device_id={"out": lax.rem(me + d, n_out)}, device_id_type=MESH)
    pl.semaphore_wait(barrier, n_out - 1)
    local = pltpu.make_async_copy(probes_ref, gathered_ref.at[me], local_sem)
    local.start()
    copies = []
    for d in range(1, n_out):
        copy = pltpu.make_async_remote_copy(
            src_ref=probes_ref,
            dst_ref=gathered_ref.at[me],
            send_sem=send_sem.at[d],
            recv_sem=recv_sem.at[d],
            device_id={"out": lax.rem(me + d, n_out)},
            device_id_type=MESH,
        )
        copy.start()
        copies.append(copy)

    keeper = keeper_ref[...]

    def body(k, carry):
        value = markov_ref[k] * keeper
        masked_ref[k] = value
        mt_ref[k] = value.astype(jnp.float32).T.astype(mt_ref.dtype)
        return carry

    lax.fori_loop(0, markov_ref.shape[0], body, 0)
    local.wait()
    for copy in copies:
        copy.wait()


def prep(markov, keeper, probes, n_out, cid):
    lags, width, m_width = markov.shape
    return pl.pallas_call(
        functools.partial(prep_kernel, n_out),
        out_shape=(
            jax.ShapeDtypeStruct((lags, width, m_width), markov.dtype),
            jax.ShapeDtypeStruct((lags, m_width, width), markov.dtype),
            jax.ShapeDtypeStruct((n_out,) + probes.shape, probes.dtype),
        ),
        in_specs=[pl.BlockSpec(memory_space=pltpu.VMEM)] * 3,
        out_specs=(pl.BlockSpec(memory_space=pltpu.VMEM),) * 3,
        scratch_shapes=[
            pltpu.SemaphoreType.DMA((n_out,)),
            pltpu.SemaphoreType.DMA((n_out,)),
            pltpu.SemaphoreType.DMA(()),
        ],
        compiler_params=pltpu.CompilerParams(
            collective_id=cid, has_side_effects=True, vmem_limit_bytes=60 * 1024 * 1024
        ),
    )(markov, keeper, probes)


def backward_panel(mt, sketch, cols):
    m_width = mt.shape[1]
    sk = sketch.shape[2]
    return pl.pallas_call(
        backward_kernel,
        out_shape=jax.ShapeDtypeStruct((cols, m_width, sk), jnp.float32),
        in_specs=[pl.BlockSpec(memory_space=pltpu.VMEM)] * 2,
        out_specs=pl.BlockSpec(memory_space=pltpu.VMEM),
        compiler_params=pltpu.CompilerParams(vmem_limit_bytes=60 * 1024 * 1024),
    )(mt, sketch)


def exchange_kernel(axis, n, stride, gather, x_ref, y_ref, send_sem, recv_sem, local_sem):
    me = lax.axis_index(axis)
    pos = lax.rem(me // stride, n)
    base = me - pos * stride

    def member(k):
        return base + k * stride

    barrier = pltpu.get_barrier_semaphore()
    for d in range(1, n):
        peer = lax.rem(pos + d, n)
        pl.semaphore_signal(barrier, inc=1, device_id={axis: member(peer)}, device_id_type=MESH)
    pl.semaphore_wait(barrier, n - 1)

    own_src = x_ref if gather else x_ref.at[pos]
    local = pltpu.make_async_copy(own_src, y_ref.at[pos], local_sem)
    local.start()
    copies = []
    for d in range(1, n):
        peer = lax.rem(pos + d, n)
        src = x_ref if gather else x_ref.at[peer]
        copy = pltpu.make_async_remote_copy(
            src_ref=src,
            dst_ref=y_ref.at[pos],
            send_sem=send_sem.at[d],
            recv_sem=recv_sem.at[d],
            device_id={axis: member(peer)},
            device_id_type=MESH,
        )
        copy.start()
        copies.append(copy)
    local.wait()
    for copy in copies:
        copy.wait()


def exchange(x, axis, n, stride, gather, cid):
    out_shape = (n,) + (x.shape if gather else x.shape[1:])
    return pl.pallas_call(
        functools.partial(exchange_kernel, axis, n, stride, gather),
        out_shape=jax.ShapeDtypeStruct(out_shape, x.dtype),
        in_specs=[pl.BlockSpec(memory_space=pl.ANY)],
        out_specs=pl.BlockSpec(memory_space=pl.ANY),
        scratch_shapes=[
            pltpu.SemaphoreType.DMA((n,)),
            pltpu.SemaphoreType.DMA((n,)),
            pltpu.SemaphoreType.DMA(()),
        ],
        compiler_params=pltpu.CompilerParams(collective_id=cid, has_side_effects=True),
    )(x)


def sketch_sum_kernel(
    n_chips, raw_ref, out_ref, half_send, core_buf, chip_send, chip_recv, core_sems, rs_send, rs_recv, ag_send, ag_recv
):
    me = lax.axis_index("in")
    core = lax.rem(me, 2)
    chip = me // 2
    partner = me + 1 - 2 * core
    rows = raw_ref.shape[0]
    half = rows // 2
    piece = half // n_chips
    my_half = core * half

    def chip_dev(k):
        return k * 2 + core

    barrier = pltpu.get_barrier_semaphore()
    pl.semaphore_signal(barrier, inc=1, device_id={"in": partner}, device_id_type=MESH)
    for d in range(1, n_chips):
        peer = lax.rem(chip + d, n_chips)
        pl.semaphore_signal(barrier, inc=1, device_id={"in": chip_dev(peer)}, device_id_type=MESH)
    pl.semaphore_wait(barrier, n_chips)

    other_half = (1 - core) * half

    def to_send(r, carry):
        half_send[r] = raw_ref[other_half + r].astype(half_send.dtype)
        return carry

    lax.fori_loop(0, half, to_send, 0)
    core_copy = pltpu.make_async_remote_copy(
        src_ref=half_send,
        dst_ref=core_buf,
        send_sem=core_sems.at[0],
        recv_sem=core_sems.at[1],
        device_id={"in": partner},
        device_id_type=MESH,
    )
    core_copy.start()
    core_copy.wait()

    def add_core(r, carry):
        chip_send[r] = (raw_ref[my_half + r] + core_buf[r].astype(jnp.float32)).astype(chip_send.dtype)
        return carry

    lax.fori_loop(0, half, add_core, 0)
    scatter = []
    for d in range(1, n_chips):
        peer = lax.rem(chip + d, n_chips)
        copy = pltpu.make_async_remote_copy(
            src_ref=chip_send.at[pl.ds(peer * piece, piece)],
            dst_ref=chip_recv.at[chip],
            send_sem=rs_send.at[d],
            recv_sem=rs_recv.at[d],
            device_id={"in": chip_dev(peer)},
            device_id_type=MESH,
        )
        copy.start()
        scatter.append(copy)
    for copy in scatter:
        copy.wait()

    base_row = my_half + chip * piece
    for q in range(piece):
        acc = chip_send[chip * piece + q].astype(jnp.float32)
        for d in range(1, n_chips):
            acc = acc + chip_recv[lax.rem(chip + d, n_chips), q].astype(jnp.float32)
        out_ref[base_row + q] = acc.astype(out_ref.dtype)

    gather = []
    for d in range(1, n_chips):
        peer = lax.rem(chip + d, n_chips)
        copy = pltpu.make_async_remote_copy(
            src_ref=out_ref.at[pl.ds(base_row, piece)],
            dst_ref=out_ref.at[pl.ds(base_row, piece)],
            send_sem=ag_send.at[d],
            recv_sem=ag_recv.at[d],
            device_id={"in": chip_dev(peer)},
            device_id_type=MESH,
        )
        copy.start()
        gather.append(copy)
    for copy in gather:
        copy.wait()
    core_back = pltpu.make_async_remote_copy(
        src_ref=out_ref.at[pl.ds(my_half, half)],
        dst_ref=out_ref.at[pl.ds(my_half, half)],
        send_sem=core_sems.at[2],
        recv_sem=core_sems.at[3],
        device_id={"in": partner},
        device_id_type=MESH,
    )
    core_back.start()
    core_back.wait()


def sketch_sum(raw, n_in, cid):
    rows, width, sk = raw.shape
    n_chips = n_in // 2
    half = rows // 2
    return pl.pallas_call(
        functools.partial(sketch_sum_kernel, n_chips),
        out_shape=jax.ShapeDtypeStruct(raw.shape, jnp.bfloat16),
        in_specs=[pl.BlockSpec(memory_space=pltpu.VMEM)],
        out_specs=pl.BlockSpec(memory_space=pltpu.VMEM),
        scratch_shapes=[
            pltpu.VMEM((half, width, sk), jnp.bfloat16),
            pltpu.VMEM((half, width, sk), jnp.bfloat16),
            pltpu.VMEM((half, width, sk), jnp.bfloat16),
            pltpu.VMEM((n_chips, half // n_chips, width, sk), jnp.bfloat16),
            pltpu.SemaphoreType.DMA((4,)),
            pltpu.SemaphoreType.DMA((n_chips,)),
            pltpu.SemaphoreType.DMA((n_chips,)),
            pltpu.SemaphoreType.DMA((n_chips,)),
            pltpu.SemaphoreType.DMA((n_chips,)),
        ],
        compiler_params=pltpu.CompilerParams(
            collective_id=cid, has_side_effects=True, vmem_limit_bytes=60 * 1024 * 1024
        ),
    )(raw)


def forward_rows(m_ref, probe_ref, i0, block):
    width, m_width = m_ref.shape[1], m_ref.shape[2]
    sk = probe_ref.shape[2]
    acc = jnp.zeros((block * width, sk), jnp.float32)
    for t in range(probe_ref.shape[0]):
        lo = m_ref[pl.ds(i0 + 2 * t, block)].reshape(block * width, m_width)
        hi = m_ref[pl.ds(i0 + 2 * t + 1, block)].reshape(block * width, m_width)
        lhs = jnp.concatenate([lo, hi], axis=1)
        acc = acc + jnp.dot(lhs, probe_ref[t], preferred_element_type=jnp.float32)
    return acc.reshape(block, width, sk)


def sketch_kernel(
    n_chips, m_ref, probe_ref, out_ref, half_send, core_buf, chip_send, chip_recv,
    core_send, core_recv, rs_send, rs_recv, ag_send, ag_recv, back_sems, back_recv,
):
    me = lax.axis_index("in")
    core = lax.rem(me, 2)
    chip = me // 2
    partner = me + 1 - 2 * core
    rows = out_ref.shape[0]
    half = rows // 2
    piece = half // n_chips
    my_half = core * half
    other_half = (1 - core) * half

    def chip_dev(k):
        return k * 2 + core

    def chunk_of(step):
        return lax.rem(chip + step + 1, n_chips)

    def core_copy(step):
        c = chunk_of(step)
        return pltpu.make_async_remote_copy(
            src_ref=half_send.at[pl.ds(c * piece, piece)],
            dst_ref=core_buf.at[pl.ds(c * piece, piece)],
            send_sem=core_send.at[step],
            recv_sem=core_recv.at[step],
            device_id={"in": partner},
            device_id_type=MESH,
        )

    def rs_copy(step):
        c = chunk_of(step)
        return pltpu.make_async_remote_copy(
            src_ref=chip_send.at[pl.ds(c * piece, piece)],
            dst_ref=chip_recv.at[chip],
            send_sem=rs_send.at[step],
            recv_sem=rs_recv.at[step],
            device_id={"in": chip_dev(c)},
            device_id_type=MESH,
        )

    barrier = pltpu.get_barrier_semaphore()
    pl.semaphore_signal(barrier, inc=1, device_id={"in": partner}, device_id_type=MESH)
    for d in range(1, n_chips):
        pl.semaphore_signal(barrier, inc=1, device_id={"in": chip_dev(lax.rem(chip + d, n_chips))}, device_id_type=MESH)
    pl.semaphore_wait(barrier, n_chips)

    def partner_rows(step, carry):
        c = chunk_of(step)
        half_send[pl.ds(c * piece, piece)] = forward_rows(m_ref, probe_ref, other_half + c * piece, piece).astype(
            half_send.dtype
        )
        core_copy(step).start()
        return carry

    lax.fori_loop(0, n_chips, partner_rows, 0)

    def own_rows(step):
        c = chunk_of(step)
        mine = forward_rows(m_ref, probe_ref, my_half + c * piece, piece)
        core_copy(step).wait_recv()
        chip_send[pl.ds(c * piece, piece)] = (mine + core_buf[pl.ds(c * piece, piece)].astype(jnp.float32)).astype(
            chip_send.dtype
        )

    def chip_rows(step, carry):
        own_rows(step)
        rs_copy(step).start()
        return carry

    lax.fori_loop(0, n_chips - 1, chip_rows, 0)
    own_rows(n_chips - 1)

    for step in range(n_chips - 1):
        rs_copy(step).wait_recv()
    base_row = my_half + chip * piece
    for q in range(piece):
        acc = chip_send[chip * piece + q].astype(jnp.float32)
        for d in range(1, n_chips):
            acc = acc + chip_recv[lax.rem(chip + d, n_chips), q].astype(jnp.float32)
        out_ref[base_row + q] = acc.astype(out_ref.dtype)

    def ag_copy(d):
        return pltpu.make_async_remote_copy(
            src_ref=out_ref.at[pl.ds(base_row, piece)],
            dst_ref=out_ref.at[pl.ds(base_row, piece)],
            send_sem=ag_send.at[d],
            recv_sem=ag_recv.at[d],
            device_id={"in": chip_dev(lax.rem(chip + d, n_chips))},
            device_id_type=MESH,
        )

    def forward_copy(d):
        start = my_half + lax.rem(chip + n_chips - d, n_chips) * piece
        return pltpu.make_async_remote_copy(
            src_ref=out_ref.at[pl.ds(start, piece)],
            dst_ref=out_ref.at[pl.ds(start, piece)],
            send_sem=back_sems.at[d],
            recv_sem=back_recv.at[d],
            device_id={"in": partner},
            device_id_type=MESH,
        )

    forward_copy(0).start()
    for d in range(1, n_chips):
        ag_copy(d).start()
    for d in range(1, n_chips):
        ag_copy(d).wait_recv()
        forward_copy(d).start()
    for step in range(n_chips):
        core_copy(step).wait_send()
    for step in range(n_chips - 1):
        rs_copy(step).wait_send()
    for d in range(1, n_chips):
        ag_copy(d).wait_send()
    for d in range(n_chips):
        forward_copy(d).wait()


def sketch_of(masked, probe_pairs, rows, n_in, cid):
    width = masked.shape[1]
    sk = probe_pairs.shape[2]
    n_chips = n_in // 2
    half = rows // 2
    return pl.pallas_call(
        functools.partial(sketch_kernel, n_chips),
        out_shape=jax.ShapeDtypeStruct((rows, width, sk), jnp.bfloat16),
        in_specs=[pl.BlockSpec(memory_space=pltpu.VMEM)] * 2,
        out_specs=pl.BlockSpec(memory_space=pltpu.VMEM),
        scratch_shapes=[
            pltpu.VMEM((half, width, sk), jnp.bfloat16),
            pltpu.VMEM((half, width, sk), jnp.bfloat16),
            pltpu.VMEM((half, width, sk), jnp.bfloat16),
            pltpu.VMEM((n_chips, half // n_chips, width, sk), jnp.bfloat16),
            pltpu.SemaphoreType.DMA((n_chips,)),
            pltpu.SemaphoreType.DMA((n_chips,)),
            pltpu.SemaphoreType.DMA((n_chips,)),
            pltpu.SemaphoreType.DMA((n_chips,)),
            pltpu.SemaphoreType.DMA((n_chips,)),
            pltpu.SemaphoreType.DMA((n_chips,)),
            pltpu.SemaphoreType.DMA((n_chips,)),
            pltpu.SemaphoreType.DMA((n_chips,)),
        ],
        compiler_params=pltpu.CompilerParams(
            collective_id=cid, has_side_effects=True, vmem_limit_bytes=60 * 1024 * 1024
        ),
    )(masked, probe_pairs)


def corange_kernel(
    n_out, scale, mt_ref, sketch_ref, gram_ref, co_out, gram_out, recv_ref, gram_recv, send_buf,
    co_send, co_recv, gram_send, gram_in, local_sems
):
    me = lax.axis_index("out")
    cols_all = send_buf.shape[1]
    m_width = mt_ref.shape[1]
    sk = sketch_ref.shape[2]
    rows = sketch_ref.shape[0]
    block = 4
    n_blocks = cols_all // (block * m_width)
    span = block * m_width
    per = sk // n_out

    barrier = pltpu.get_barrier_semaphore()
    for d in range(1, n_out):
        pl.semaphore_signal(barrier, inc=1, device_id={"out": lax.rem(me + d, n_out)}, device_id_type=MESH)
    pl.semaphore_wait(barrier, n_out - 1)

    def gram_copy(d):
        return pltpu.make_async_remote_copy(
            src_ref=gram_ref,
            dst_ref=gram_recv.at[me],
            send_sem=gram_send.at[d],
            recv_sem=gram_in.at[d],
            device_id={"out": lax.rem(me + d, n_out)},
            device_id_type=MESH,
        )

    gram_local = pltpu.make_async_copy(gram_ref, gram_recv.at[me], local_sems.at[n_blocks])
    gram_local.start()
    for d in range(1, n_out):
        gram_copy(d).start()

    def co_copy(d, b):
        k = lax.rem(me + d, n_out)
        return pltpu.make_async_remote_copy(
            src_ref=send_buf.at[pl.ds(pl.multiple_of(k * per, per), per), pl.ds(pl.multiple_of(b * span, span), span)],
            dst_ref=recv_ref.at[me, :, pl.ds(pl.multiple_of(b * span, span), span)],
            send_sem=co_send.at[d, b],
            recv_sem=co_recv.at[d, b],
            device_id={"out": k},
            device_id_type=MESH,
        )

    def local_copy(b):
        return pltpu.make_async_copy(
            send_buf.at[pl.ds(pl.multiple_of(me * per, per), per), pl.ds(pl.multiple_of(b * span, span), span)],
            recv_ref.at[me, :, pl.ds(pl.multiple_of(b * span, span), span)],
            local_sems.at[b],
        )

    def body(b, carry):
        j0 = b * block
        acc = jnp.zeros((span, sk), jnp.float32)
        for i in range(rows):
            lhs = mt_ref[pl.ds(j0 + i, block)].reshape(span, mt_ref.shape[2])
            acc = acc + jnp.dot(lhs, sketch_ref[i], preferred_element_type=jnp.float32)
        send_buf[:, pl.ds(pl.multiple_of(b * span, span), span)] = acc.T.astype(send_buf.dtype)
        local_copy(b).start()
        for d in range(1, n_out):
            co_copy(d, b).start()
        return carry

    lax.fori_loop(0, n_blocks, body, 0)

    def drain(b, carry):
        local_copy(b).wait()
        for d in range(1, n_out):
            co_copy(d, b).wait()
        return carry

    lax.fori_loop(0, n_blocks, drain, 0)
    gram_local.wait()
    for d in range(1, n_out):
        gram_copy(d).wait()
    co_total = recv_ref[0].astype(jnp.float32)
    gram_total = gram_recv[0].astype(jnp.float32)
    for k in range(1, n_out):
        co_total = co_total + recv_ref[k].astype(jnp.float32)
        gram_total = gram_total + gram_recv[k].astype(jnp.float32)
    co_out[...] = co_total
    gram_out[...] = gram_total * scale


def corange_of(mt, sketch, gram_part, cols, n_out, cid):
    m_width = mt.shape[1]
    sk = sketch.shape[2]
    n_blocks = cols // 4
    return pl.pallas_call(
        functools.partial(corange_kernel, n_out, 1.0 / (R * OUTPUT_CHANNELS)),
        out_shape=(
            jax.ShapeDtypeStruct((sk // n_out, cols * m_width), jnp.float32),
            jax.ShapeDtypeStruct(gram_part.shape, jnp.float32),
        ),
        in_specs=[pl.BlockSpec(memory_space=pltpu.VMEM)] * 3,
        out_specs=(pl.BlockSpec(memory_space=pltpu.VMEM),) * 2,
        scratch_shapes=[
            pltpu.VMEM((n_out, sk // n_out, cols * m_width), jnp.bfloat16),
            pltpu.VMEM((n_out,) + gram_part.shape, jnp.bfloat16),
            pltpu.VMEM((sk, cols * m_width), jnp.bfloat16),
            pltpu.SemaphoreType.DMA((n_out, n_blocks)),
            pltpu.SemaphoreType.DMA((n_out, n_blocks)),
            pltpu.SemaphoreType.DMA((n_out,)),
            pltpu.SemaphoreType.DMA((n_out,)),
            pltpu.SemaphoreType.DMA((n_blocks + 1,)),
        ],
        compiler_params=pltpu.CompilerParams(
            collective_id=cid, has_side_effects=True, vmem_limit_bytes=60 * 1024 * 1024
        ),
    )(mt, sketch, gram_part)


def shards(n_out, n_in, markov, probes, pattern):
    keeper = jnp.repeat(jnp.repeat(pattern, BO, axis=0), BI, axis=1).astype(jnp.bfloat16)
    masked, mt, gathered = prep(markov, keeper, probes, n_out, 0)
    panel = gathered.reshape((-1,) + probes.shape[1:])
    s_all, cols, m_width = panel.shape
    probe_pairs = jnp.swapaxes(panel.reshape(s_all, cols // 2, 2 * m_width), 0, 1).swapaxes(1, 2)
    sketch = sketch_of(masked, probe_pairs, R, n_in, 1)
    rows, width, sk = sketch.shape
    local_gram = jnp.einsum("ips,ipt->st", sketch, sketch, preferred_element_type=jnp.float32)
    co_sum, gram_matrix = corange_of(mt, sketch, local_gram.astype(jnp.bfloat16), cols, n_out, 4)
    corange = co_sum.reshape(s_all // n_out, cols, m_width)
    return (sketch, corange, gram_matrix)


def solution(mesh):
    return jax.shard_map(
        functools.partial(shards, mesh.shape["out"], mesh.shape["in"]),
        mesh=mesh,
        in_specs=(P(None, "out", "in"), P("out", None, "in"), P("out", "in")),
        out_specs=(P(None, "out", None), P("out", None, "in"), P()),
        check_vma=False,
    )
```

```python
import functools

import jax
import jax.numpy as jnp
from jax import lax
from jax.experimental import pallas as pl
from jax.experimental.pallas import tpu as pltpu
from jax.sharding import PartitionSpec as P

OUTPUT_CHANNELS = 2048
BO = 64
BI = 128
R = 32
C = 32

MESH = pl.DeviceIdType.MESH


def forward_kernel(m_ref, probe_ref, out_ref):
    rows, width, sk = out_ref.shape
    steps = probe_ref.shape[0]
    m_width = m_ref.shape[2]
    block = 2

    def body(b, carry):
        i0 = b * block
        acc = jnp.zeros((block * width, sk), jnp.float32)
        for t in range(steps):
            lo = m_ref[pl.ds(i0 + 2 * t, block)].reshape(block * width, m_width)
            hi = m_ref[pl.ds(i0 + 2 * t + 1, block)].reshape(block * width, m_width)
            lhs = jnp.concatenate([lo, hi], axis=1)
            acc = acc + jnp.dot(lhs, probe_ref[t], preferred_element_type=jnp.float32)
        out_ref[pl.ds(i0, block)] = acc.reshape(block, width, sk)
        return carry

    lax.fori_loop(0, rows // block, body, 0)


def forward_panel(pair, probe_pairs, rows):
    width = pair.shape[1]
    sk = probe_pairs.shape[2]
    return pl.pallas_call(
        forward_kernel,
        out_shape=jax.ShapeDtypeStruct((rows, width, sk), jnp.float32),
        in_specs=[pl.BlockSpec(memory_space=pltpu.VMEM)] * 2,
        out_specs=pl.BlockSpec(memory_space=pltpu.VMEM),
        compiler_params=pltpu.CompilerParams(vmem_limit_bytes=60 * 1024 * 1024),
    )(pair, probe_pairs)


def backward_kernel(mt_ref, sketch_ref, out_ref):
    cols, m_width, sk = out_ref.shape
    rows = sketch_ref.shape[0]
    block = 4

    def body(b, carry):
        j0 = b * block
        acc = jnp.zeros((block * m_width, sk), jnp.float32)
        for i in range(rows):
            lhs = mt_ref[pl.ds(j0 + i, block)].reshape(block * m_width, mt_ref.shape[2])
            acc = acc + jnp.dot(lhs, sketch_ref[i], preferred_element_type=jnp.float32)
        out_ref[pl.ds(j0, block)] = acc.reshape(block, m_width, sk)
        return carry

    lax.fori_loop(0, cols // block, body, 0)


def prep_kernel(n_out, markov_ref, keeper_ref, probes_ref, masked_ref, mt_ref, gathered_ref, send_sem, recv_sem, local_sem):
    me = lax.axis_index("out")
    barrier = pltpu.get_barrier_semaphore()
    for d in range(1, n_out):
        pl.semaphore_signal(barrier, inc=1, device_id={"out": lax.rem(me + d, n_out)}, device_id_type=MESH)
    pl.semaphore_wait(barrier, n_out - 1)
    local = pltpu.make_async_copy(probes_ref, gathered_ref.at[me], local_sem)
    local.start()
    copies = []
    for d in range(1, n_out):
        copy = pltpu.make_async_remote_copy(
            src_ref=probes_ref,
            dst_ref=gathered_ref.at[me],
            send_sem=send_sem.at[d],
            recv_sem=recv_sem.at[d],
            device_id={"out": lax.rem(me + d, n_out)},
            device_id_type=MESH,
        )
        copy.start()
        copies.append(copy)

    keeper = keeper_ref[...]

    def body(k, carry):
        value = markov_ref[k] * keeper
        masked_ref[k] = value
        mt_ref[k] = value.astype(jnp.float32).T.astype(mt_ref.dtype)
        return carry

    lax.fori_loop(0, markov_ref.shape[0], body, 0)
    local.wait()
    for copy in copies:
        copy.wait()


def prep(markov, keeper, probes, n_out, cid):
    lags, width, m_width = markov.shape
    return pl.pallas_call(
        functools.partial(prep_kernel, n_out),
        out_shape=(
            jax.ShapeDtypeStruct((lags, width, m_width), markov.dtype),
            jax.ShapeDtypeStruct((lags, m_width, width), markov.dtype),
            jax.ShapeDtypeStruct((n_out,) + probes.shape, probes.dtype),
        ),
        in_specs=[pl.BlockSpec(memory_space=pltpu.VMEM)] * 3,
        out_specs=(pl.BlockSpec(memory_space=pltpu.VMEM),) * 3,
        scratch_shapes=[
            pltpu.SemaphoreType.DMA((n_out,)),
            pltpu.SemaphoreType.DMA((n_out,)),
            pltpu.SemaphoreType.DMA(()),
        ],
        compiler_params=pltpu.CompilerParams(
            collective_id=cid, has_side_effects=True, vmem_limit_bytes=60 * 1024 * 1024
        ),
    )(markov, keeper, probes)


def backward_panel(mt, sketch, cols):
    m_width = mt.shape[1]
    sk = sketch.shape[2]
    return pl.pallas_call(
        backward_kernel,
        out_shape=jax.ShapeDtypeStruct((cols, m_width, sk), jnp.float32),
        in_specs=[pl.BlockSpec(memory_space=pltpu.VMEM)] * 2,
        out_specs=pl.BlockSpec(memory_space=pltpu.VMEM),
        compiler_params=pltpu.CompilerParams(vmem_limit_bytes=60 * 1024 * 1024),
    )(mt, sketch)


def exchange_kernel(axis, n, stride, gather, x_ref, y_ref, send_sem, recv_sem, local_sem):
    me = lax.axis_index(axis)
    pos = lax.rem(me // stride, n)
    base = me - pos * stride

    def member(k):
        return base + k * stride

    barrier = pltpu.get_barrier_semaphore()
    for d in range(1, n):
        peer = lax.rem(pos + d, n)
        pl.semaphore_signal(barrier, inc=1, device_id={axis: member(peer)}, device_id_type=MESH)
    pl.semaphore_wait(barrier, n - 1)

    own_src = x_ref if gather else x_ref.at[pos]
    local = pltpu.make_async_copy(own_src, y_ref.at[pos], local_sem)
    local.start()
    copies = []
    for d in range(1, n):
        peer = lax.rem(pos + d, n)
        src = x_ref if gather else x_ref.at[peer]
        copy = pltpu.make_async_remote_copy(
            src_ref=src,
            dst_ref=y_ref.at[pos],
            send_sem=send_sem.at[d],
            recv_sem=recv_sem.at[d],
            device_id={axis: member(peer)},
            device_id_type=MESH,
        )
        copy.start()
        copies.append(copy)
    local.wait()
    for copy in copies:
        copy.wait()


def exchange(x, axis, n, stride, gather, cid):
    out_shape = (n,) + (x.shape if gather else x.shape[1:])
    return pl.pallas_call(
        functools.partial(exchange_kernel, axis, n, stride, gather),
        out_shape=jax.ShapeDtypeStruct(out_shape, x.dtype),
        in_specs=[pl.BlockSpec(memory_space=pl.ANY)],
        out_specs=pl.BlockSpec(memory_space=pl.ANY),
        scratch_shapes=[
            pltpu.SemaphoreType.DMA((n,)),
            pltpu.SemaphoreType.DMA((n,)),
            pltpu.SemaphoreType.DMA(()),
        ],
        compiler_params=pltpu.CompilerParams(collective_id=cid, has_side_effects=True),
    )(x)


def sketch_sum_kernel(
    n_chips, raw_ref, out_ref, half_send, core_buf, chip_send, chip_recv, core_sems, rs_send, rs_recv, ag_send, ag_recv
):
    me = lax.axis_index("in")
    core = lax.rem(me, 2)
    chip = me // 2
    partner = me + 1 - 2 * core
    rows = raw_ref.shape[0]
    half = rows // 2
    piece = half // n_chips
    my_half = core * half

    def chip_dev(k):
        return k * 2 + core

    barrier = pltpu.get_barrier_semaphore()
    pl.semaphore_signal(barrier, inc=1, device_id={"in": partner}, device_id_type=MESH)
    for d in range(1, n_chips):
        peer = lax.rem(chip + d, n_chips)
        pl.semaphore_signal(barrier, inc=1, device_id={"in": chip_dev(peer)}, device_id_type=MESH)
    pl.semaphore_wait(barrier, n_chips)

    other_half = (1 - core) * half

    def to_send(r, carry):
        half_send[r] = raw_ref[other_half + r].astype(half_send.dtype)
        return carry

    lax.fori_loop(0, half, to_send, 0)
    core_copy = pltpu.make_async_remote_copy(
        src_ref=half_send,
        dst_ref=core_buf,
        send_sem=core_sems.at[0],
        recv_sem=core_sems.at[1],
        device_id={"in": partner},
        device_id_type=MESH,
    )
    core_copy.start()
    core_copy.wait()

    def add_core(r, carry):
        chip_send[r] = (raw_ref[my_half + r] + core_buf[r].astype(jnp.float32)).astype(chip_send.dtype)
        return carry

    lax.fori_loop(0, half, add_core, 0)
    scatter = []
    for d in range(1, n_chips):
        peer = lax.rem(chip + d, n_chips)
        copy = pltpu.make_async_remote_copy(
            src_ref=chip_send.at[pl.ds(peer * piece, piece)],
            dst_ref=chip_recv.at[chip],
            send_sem=rs_send.at[d],
            recv_sem=rs_recv.at[d],
            device_id={"in": chip_dev(peer)},
            device_id_type=MESH,
        )
        copy.start()
        scatter.append(copy)
    for copy in scatter:
        copy.wait()

    base_row = my_half + chip * piece
    for q in range(piece):
        acc = chip_send[chip * piece + q].astype(jnp.float32)
        for d in range(1, n_chips):
            acc = acc + chip_recv[lax.rem(chip + d, n_chips), q].astype(jnp.float32)
        out_ref[base_row + q] = acc.astype(out_ref.dtype)

    gather = []
    for d in range(1, n_chips):
        peer = lax.rem(chip + d, n_chips)
        copy = pltpu.make_async_remote_copy(
            src_ref=out_ref.at[pl.ds(base_row, piece)],
            dst_ref=out_ref.at[pl.ds(base_row, piece)],
            send_sem=ag_send.at[d],
            recv_sem=ag_recv.at[d],
            device_id={"in": chip_dev(peer)},
            device_id_type=MESH,
        )
        copy.start()
        gather.append(copy)
    for copy in gather:
        copy.wait()
    core_back = pltpu.make_async_remote_copy(
        src_ref=out_ref.at[pl.ds(my_half, half)],
        dst_ref=out_ref.at[pl.ds(my_half, half)],
        send_sem=core_sems.at[2],
        recv_sem=core_sems.at[3],
        device_id={"in": partner},
        device_id_type=MESH,
    )
    core_back.start()
    core_back.wait()


def sketch_sum(raw, n_in, cid):
    rows, width, sk = raw.shape
    n_chips = n_in // 2
    half = rows // 2
    return pl.pallas_call(
        functools.partial(sketch_sum_kernel, n_chips),
        out_shape=jax.ShapeDtypeStruct(raw.shape, jnp.bfloat16),
        in_specs=[pl.BlockSpec(memory_space=pltpu.VMEM)],
        out_specs=pl.BlockSpec(memory_space=pltpu.VMEM),
        scratch_shapes=[
            pltpu.VMEM((half, width, sk), jnp.bfloat16),
            pltpu.VMEM((half, width, sk), jnp.bfloat16),
            pltpu.VMEM((half, width, sk), jnp.bfloat16),
            pltpu.VMEM((n_chips, half // n_chips, width, sk), jnp.bfloat16),
            pltpu.SemaphoreType.DMA((4,)),
            pltpu.SemaphoreType.DMA((n_chips,)),
            pltpu.SemaphoreType.DMA((n_chips,)),
            pltpu.SemaphoreType.DMA((n_chips,)),
            pltpu.SemaphoreType.DMA((n_chips,)),
        ],
        compiler_params=pltpu.CompilerParams(
            collective_id=cid, has_side_effects=True, vmem_limit_bytes=60 * 1024 * 1024
        ),
    )(raw)


def forward_rows(m_ref, probe_ref, i0, block):
    width, m_width = m_ref.shape[1], m_ref.shape[2]
    sk = probe_ref.shape[2]
    acc = jnp.zeros((block * width, sk), jnp.float32)
    for t in range(probe_ref.shape[0]):
        lo = m_ref[pl.ds(i0 + 2 * t, block)].reshape(block * width, m_width)
        hi = m_ref[pl.ds(i0 + 2 * t + 1, block)].reshape(block * width, m_width)
        lhs = jnp.concatenate([lo, hi], axis=1)
        acc = acc + jnp.dot(lhs, probe_ref[t], preferred_element_type=jnp.float32)
    return acc.reshape(block, width, sk)


def sketch_kernel(
    n_chips, m_ref, probe_ref, out_ref, half_send, core_buf, chip_send, chip_recv,
    core_send, core_recv, rs_send, rs_recv, ag_send, ag_recv, back_sems, back_recv,
):
    me = lax.axis_index("in")
    core = lax.rem(me, 2)
    chip = me // 2
    partner = me + 1 - 2 * core
    rows = out_ref.shape[0]
    half = rows // 2
    piece = half // n_chips
    my_half = core * half
    other_half = (1 - core) * half

    def chip_dev(k):
        return k * 2 + core

    def chunk_of(step):
        return lax.rem(chip + step + 1, n_chips)

    def core_copy(step):
        c = chunk_of(step)
        return pltpu.make_async_remote_copy(
            src_ref=half_send.at[pl.ds(c * piece, piece)],
            dst_ref=core_buf.at[pl.ds(c * piece, piece)],
            send_sem=core_send.at[step],
            recv_sem=core_recv.at[step],
            device_id={"in": partner},
            device_id_type=MESH,
        )

    def rs_copy(step):
        c = chunk_of(step)
        return pltpu.make_async_remote_copy(
            src_ref=chip_send.at[pl.ds(c * piece, piece)],
            dst_ref=chip_recv.at[chip],
            send_sem=rs_send.at[step],
            recv_sem=rs_recv.at[step],
            device_id={"in": chip_dev(c)},
            device_id_type=MESH,
        )

    barrier = pltpu.get_barrier_semaphore()
    pl.semaphore_signal(barrier, inc=1, device_id={"in": partner}, device_id_type=MESH)
    for d in range(1, n_chips):
        pl.semaphore_signal(barrier, inc=1, device_id={"in": chip_dev(lax.rem(chip + d, n_chips))}, device_id_type=MESH)
    pl.semaphore_wait(barrier, n_chips)

    def partner_rows(step, carry):
        c = chunk_of(step)
        half_send[pl.ds(c * piece, piece)] = forward_rows(m_ref, probe_ref, other_half + c * piece, piece).astype(
            half_send.dtype
        )
        core_copy(step).start()
        return carry

    lax.fori_loop(0, n_chips, partner_rows, 0)

    def own_rows(step):
        c = chunk_of(step)
        mine = forward_rows(m_ref, probe_ref, my_half + c * piece, piece)
        core_copy(step).wait_recv()
        chip_send[pl.ds(c * piece, piece)] = (mine + core_buf[pl.ds(c * piece, piece)].astype(jnp.float32)).astype(
            chip_send.dtype
        )

    def chip_rows(step, carry):
        own_rows(step)
        rs_copy(step).start()
        return carry

    lax.fori_loop(0, n_chips - 1, chip_rows, 0)
    own_rows(n_chips - 1)

    for step in range(n_chips - 1):
        rs_copy(step).wait_recv()
    base_row = my_half + chip * piece
    for q in range(piece):
        acc = chip_send[chip * piece + q].astype(jnp.float32)
        for d in range(1, n_chips):
            acc = acc + chip_recv[lax.rem(chip + d, n_chips), q].astype(jnp.float32)
        out_ref[base_row + q] = acc.astype(out_ref.dtype)

    def ag_copy(d):
        return pltpu.make_async_remote_copy(
            src_ref=out_ref.at[pl.ds(base_row, piece)],
            dst_ref=out_ref.at[pl.ds(base_row, piece)],
            send_sem=ag_send.at[d],
            recv_sem=ag_recv.at[d],
            device_id={"in": chip_dev(lax.rem(chip + d, n_chips))},
            device_id_type=MESH,
        )

    def forward_copy(d):
        start = my_half + lax.rem(chip + n_chips - d, n_chips) * piece
        return pltpu.make_async_remote_copy(
            src_ref=out_ref.at[pl.ds(start, piece)],
            dst_ref=out_ref.at[pl.ds(start, piece)],
            send_sem=back_sems.at[d],
            recv_sem=back_recv.at[d],
            device_id={"in": partner},
            device_id_type=MESH,
        )

    forward_copy(0).start()
    for d in range(1, n_chips):
        ag_copy(d).start()
    for d in range(1, n_chips):
        ag_copy(d).wait_recv()
        forward_copy(d).start()
    for step in range(n_chips):
        core_copy(step).wait_send()
    for step in range(n_chips - 1):
        rs_copy(step).wait_send()
    for d in range(1, n_chips):
        ag_copy(d).wait_send()
    for d in range(n_chips):
        forward_copy(d).wait()


def sketch_of(masked, probe_pairs, rows, n_in, cid):
    width = masked.shape[1]
    sk = probe_pairs.shape[2]
    n_chips = n_in // 2
    half = rows // 2
    return pl.pallas_call(
        functools.partial(sketch_kernel, n_chips),
        out_shape=jax.ShapeDtypeStruct((rows, width, sk), jnp.bfloat16),
        in_specs=[pl.BlockSpec(memory_space=pltpu.VMEM)] * 2,
        out_specs=pl.BlockSpec(memory_space=pltpu.VMEM),
        scratch_shapes=[
            pltpu.VMEM((half, width, sk), jnp.bfloat16),
            pltpu.VMEM((half, width, sk), jnp.bfloat16),
            pltpu.VMEM((half, width, sk), jnp.bfloat16),
            pltpu.VMEM((n_chips, half // n_chips, width, sk), jnp.bfloat16),
            pltpu.SemaphoreType.DMA((n_chips,)),
            pltpu.SemaphoreType.DMA((n_chips,)),
            pltpu.SemaphoreType.DMA((n_chips,)),
            pltpu.SemaphoreType.DMA((n_chips,)),
            pltpu.SemaphoreType.DMA((n_chips,)),
            pltpu.SemaphoreType.DMA((n_chips,)),
            pltpu.SemaphoreType.DMA((n_chips,)),
            pltpu.SemaphoreType.DMA((n_chips,)),
        ],
        compiler_params=pltpu.CompilerParams(
            collective_id=cid, has_side_effects=True, vmem_limit_bytes=60 * 1024 * 1024
        ),
    )(masked, probe_pairs)


def corange_kernel(
    n_out, scale, mt_ref, sketch_ref, co_out, gram_out, recv_ref, gram_recv, gram_ref, send_buf,
    co_send, co_recv, gram_send, gram_in, local_sems
):
    me = lax.axis_index("out")
    cols_all = send_buf.shape[1]
    m_width = mt_ref.shape[1]
    sk = sketch_ref.shape[2]
    rows = sketch_ref.shape[0]
    block = 4
    n_blocks = cols_all // (block * m_width)
    span = block * m_width
    per = sk // n_out

    barrier = pltpu.get_barrier_semaphore()
    for d in range(1, n_out):
        pl.semaphore_signal(barrier, inc=1, device_id={"out": lax.rem(me + d, n_out)}, device_id_type=MESH)
    pl.semaphore_wait(barrier, n_out - 1)

    def gram_copy(d):
        return pltpu.make_async_remote_copy(
            src_ref=gram_ref,
            dst_ref=gram_recv.at[me],
            send_sem=gram_send.at[d],
            recv_sem=gram_in.at[d],
            device_id={"out": lax.rem(me + d, n_out)},
            device_id_type=MESH,
        )

    def gram_rows(i, acc):
        value = sketch_ref[i]
        return acc + lax.dot_general(
            value, value, (((0,), (0,)), ((), ())), preferred_element_type=jnp.float32
        )

    gram_ref[...] = lax.fori_loop(0, rows, gram_rows, jnp.zeros((sk, sk), jnp.float32)).astype(gram_ref.dtype)
    gram_local = pltpu.make_async_copy(gram_ref, gram_recv.at[me], local_sems.at[n_blocks])
    gram_local.start()
    for d in range(1, n_out):
        gram_copy(d).start()

    def co_copy(d, b):
        k = lax.rem(me + d, n_out)
        return pltpu.make_async_remote_copy(
            src_ref=send_buf.at[pl.ds(pl.multiple_of(k * per, per), per), pl.ds(pl.multiple_of(b * span, span), span)],
            dst_ref=recv_ref.at[me, :, pl.ds(pl.multiple_of(b * span, span), span)],
            send_sem=co_send.at[d, b],
            recv_sem=co_recv.at[d, b],
            device_id={"out": k},
            device_id_type=MESH,
        )

    def local_copy(b):
        return pltpu.make_async_copy(
            send_buf.at[pl.ds(pl.multiple_of(me * per, per), per), pl.ds(pl.multiple_of(b * span, span), span)],
            recv_ref.at[me, :, pl.ds(pl.multiple_of(b * span, span), span)],
            local_sems.at[b],
        )

    def body(b, carry):
        j0 = b * block
        acc = jnp.zeros((span, sk), jnp.float32)
        for i in range(rows):
            lhs = mt_ref[pl.ds(j0 + i, block)].reshape(span, mt_ref.shape[2])
            acc = acc + jnp.dot(lhs, sketch_ref[i], preferred_element_type=jnp.float32)
        send_buf[:, pl.ds(pl.multiple_of(b * span, span), span)] = acc.T.astype(send_buf.dtype)
        local_copy(b).start()
        for d in range(1, n_out):
            co_copy(d, b).start()
        return carry

    lax.fori_loop(0, n_blocks, body, 0)

    def drain(b, carry):
        local_copy(b).wait()
        for d in range(1, n_out):
            co_copy(d, b).wait()
        return carry

    lax.fori_loop(0, n_blocks, drain, 0)
    gram_local.wait()
    for d in range(1, n_out):
        gram_copy(d).wait()
    co_total = recv_ref[0].astype(jnp.float32)
    gram_total = gram_recv[0].astype(jnp.float32)
    for k in range(1, n_out):
        co_total = co_total + recv_ref[k].astype(jnp.float32)
        gram_total = gram_total + gram_recv[k].astype(jnp.float32)
    co_out[...] = co_total
    gram_out[...] = gram_total * scale


def corange_of(mt, sketch, cols, n_out, cid):
    m_width = mt.shape[1]
    sk = sketch.shape[2]
    n_blocks = cols // 4
    return pl.pallas_call(
        functools.partial(corange_kernel, n_out, 1.0 / (R * OUTPUT_CHANNELS)),
        out_shape=(
            jax.ShapeDtypeStruct((sk // n_out, cols * m_width), jnp.float32),
            jax.ShapeDtypeStruct((sk, sk), jnp.float32),
        ),
        in_specs=[pl.BlockSpec(memory_space=pltpu.VMEM)] * 2,
        out_specs=(pl.BlockSpec(memory_space=pltpu.VMEM),) * 2,
        scratch_shapes=[
            pltpu.VMEM((n_out, sk // n_out, cols * m_width), jnp.bfloat16),
            pltpu.VMEM((n_out, sk, sk), jnp.bfloat16),
            pltpu.VMEM((sk, sk), jnp.bfloat16),
            pltpu.VMEM((sk, cols * m_width), jnp.bfloat16),
            pltpu.SemaphoreType.DMA((n_out, n_blocks)),
            pltpu.SemaphoreType.DMA((n_out, n_blocks)),
            pltpu.SemaphoreType.DMA((n_out,)),
            pltpu.SemaphoreType.DMA((n_out,)),
            pltpu.SemaphoreType.DMA((n_blocks + 1,)),
        ],
        compiler_params=pltpu.CompilerParams(
            collective_id=cid, has_side_effects=True, vmem_limit_bytes=60 * 1024 * 1024
        ),
    )(mt, sketch)


def shards(n_out, n_in, markov, probes, pattern):
    keeper = jnp.repeat(jnp.repeat(pattern, BO, axis=0), BI, axis=1).astype(jnp.bfloat16)
    masked, mt, gathered = prep(markov, keeper, probes, n_out, 0)
    panel = gathered.reshape((-1,) + probes.shape[1:])
    s_all, cols, m_width = panel.shape
    probe_pairs = jnp.swapaxes(panel.reshape(s_all, cols // 2, 2 * m_width), 0, 1).swapaxes(1, 2)
    sketch = sketch_of(masked, probe_pairs, R, n_in, 1)
    rows, width, sk = sketch.shape
    co_sum, gram_matrix = corange_of(mt, sketch, cols, n_out, 4)
    corange = co_sum.reshape(s_all // n_out, cols, m_width)
    return (sketch, corange, gram_matrix)


def solution(mesh):
    return jax.shard_map(
        functools.partial(shards, mesh.shape["out"], mesh.shape["in"]),
        mesh=mesh,
        in_specs=(P(None, "out", "in"), P("out", None, "in"), P("out", "in")),
        out_specs=(P(None, "out", None), P("out", None, "in"), P()),
        check_vma=False,
    )
```

```python
import functools

import jax
import jax.numpy as jnp
from jax import lax
from jax.experimental import pallas as pl
from jax.experimental.pallas import tpu as pltpu
from jax.sharding import PartitionSpec as P

OUTPUT_CHANNELS = 2048
BO = 64
BI = 128
R = 32
C = 32

MESH = pl.DeviceIdType.MESH


def forward_kernel(m_ref, probe_ref, out_ref):
    rows, width, sk = out_ref.shape
    steps = probe_ref.shape[0]
    m_width = m_ref.shape[2]
    block = 2

    def body(b, carry):
        i0 = b * block
        acc = jnp.zeros((block * width, sk), jnp.float32)
        for t in range(steps):
            lo = m_ref[pl.ds(i0 + 2 * t, block)].reshape(block * width, m_width)
            hi = m_ref[pl.ds(i0 + 2 * t + 1, block)].reshape(block * width, m_width)
            lhs = jnp.concatenate([lo, hi], axis=1)
            acc = acc + jnp.dot(lhs, probe_ref[t], preferred_element_type=jnp.float32)
        out_ref[pl.ds(i0, block)] = acc.reshape(block, width, sk)
        return carry

    lax.fori_loop(0, rows // block, body, 0)


def forward_panel(pair, probe_pairs, rows):
    width = pair.shape[1]
    sk = probe_pairs.shape[2]
    return pl.pallas_call(
        forward_kernel,
        out_shape=jax.ShapeDtypeStruct((rows, width, sk), jnp.float32),
        in_specs=[pl.BlockSpec(memory_space=pltpu.VMEM)] * 2,
        out_specs=pl.BlockSpec(memory_space=pltpu.VMEM),
        compiler_params=pltpu.CompilerParams(vmem_limit_bytes=60 * 1024 * 1024),
    )(pair, probe_pairs)


def backward_kernel(mt_ref, sketch_ref, out_ref):
    cols, m_width, sk = out_ref.shape
    rows = sketch_ref.shape[0]
    block = 4

    def body(b, carry):
        j0 = b * block
        acc = jnp.zeros((block * m_width, sk), jnp.float32)
        for i in range(rows):
            lhs = mt_ref[pl.ds(j0 + i, block)].reshape(block * m_width, mt_ref.shape[2])
            acc = acc + jnp.dot(lhs, sketch_ref[i], preferred_element_type=jnp.float32)
        out_ref[pl.ds(j0, block)] = acc.reshape(block, m_width, sk)
        return carry

    lax.fori_loop(0, cols // block, body, 0)


def prep_kernel(n_out, markov_ref, keeper_ref, probes_ref, masked_ref, mt_ref, gathered_ref, send_sem, recv_sem, local_sem):
    me = lax.axis_index("out")
    barrier = pltpu.get_barrier_semaphore()
    for d in range(1, n_out):
        pl.semaphore_signal(barrier, inc=1, device_id={"out": lax.rem(me + d, n_out)}, device_id_type=MESH)
    pl.semaphore_wait(barrier, n_out - 1)
    local = pltpu.make_async_copy(probes_ref, gathered_ref.at[me], local_sem)
    local.start()
    copies = []
    for d in range(1, n_out):
        copy = pltpu.make_async_remote_copy(
            src_ref=probes_ref,
            dst_ref=gathered_ref.at[me],
            send_sem=send_sem.at[d],
            recv_sem=recv_sem.at[d],
            device_id={"out": lax.rem(me + d, n_out)},
            device_id_type=MESH,
        )
        copy.start()
        copies.append(copy)

    keeper = keeper_ref[...]

    def body(k, carry):
        value = markov_ref[k] * keeper
        masked_ref[k] = value
        mt_ref[k] = value.astype(jnp.float32).T.astype(mt_ref.dtype)
        return carry

    lax.fori_loop(0, markov_ref.shape[0], body, 0)
    local.wait()
    for copy in copies:
        copy.wait()


def prep(markov, keeper, probes, n_out, cid):
    lags, width, m_width = markov.shape
    return pl.pallas_call(
        functools.partial(prep_kernel, n_out),
        out_shape=(
            jax.ShapeDtypeStruct((lags, width, m_width), markov.dtype),
            jax.ShapeDtypeStruct((lags, m_width, width), markov.dtype),
            jax.ShapeDtypeStruct((n_out,) + probes.shape, probes.dtype),
        ),
        in_specs=[pl.BlockSpec(memory_space=pltpu.VMEM)] * 3,
        out_specs=(pl.BlockSpec(memory_space=pltpu.VMEM),) * 3,
        scratch_shapes=[
            pltpu.SemaphoreType.DMA((n_out,)),
            pltpu.SemaphoreType.DMA((n_out,)),
            pltpu.SemaphoreType.DMA(()),
        ],
        compiler_params=pltpu.CompilerParams(
            collective_id=cid, has_side_effects=True, vmem_limit_bytes=60 * 1024 * 1024
        ),
    )(markov, keeper, probes)


def backward_panel(mt, sketch, cols):
    m_width = mt.shape[1]
    sk = sketch.shape[2]
    return pl.pallas_call(
        backward_kernel,
        out_shape=jax.ShapeDtypeStruct((cols, m_width, sk), jnp.float32),
        in_specs=[pl.BlockSpec(memory_space=pltpu.VMEM)] * 2,
        out_specs=pl.BlockSpec(memory_space=pltpu.VMEM),
        compiler_params=pltpu.CompilerParams(vmem_limit_bytes=60 * 1024 * 1024),
    )(mt, sketch)


def exchange_kernel(axis, n, stride, gather, x_ref, y_ref, send_sem, recv_sem, local_sem):
    me = lax.axis_index(axis)
    pos = lax.rem(me // stride, n)
    base = me - pos * stride

    def member(k):
        return base + k * stride

    barrier = pltpu.get_barrier_semaphore()
    for d in range(1, n):
        peer = lax.rem(pos + d, n)
        pl.semaphore_signal(barrier, inc=1, device_id={axis: member(peer)}, device_id_type=MESH)
    pl.semaphore_wait(barrier, n - 1)

    own_src = x_ref if gather else x_ref.at[pos]
    local = pltpu.make_async_copy(own_src, y_ref.at[pos], local_sem)
    local.start()
    copies = []
    for d in range(1, n):
        peer = lax.rem(pos + d, n)
        src = x_ref if gather else x_ref.at[peer]
        copy = pltpu.make_async_remote_copy(
            src_ref=src,
            dst_ref=y_ref.at[pos],
            send_sem=send_sem.at[d],
            recv_sem=recv_sem.at[d],
            device_id={axis: member(peer)},
            device_id_type=MESH,
        )
        copy.start()
        copies.append(copy)
    local.wait()
    for copy in copies:
        copy.wait()


def exchange(x, axis, n, stride, gather, cid):
    out_shape = (n,) + (x.shape if gather else x.shape[1:])
    return pl.pallas_call(
        functools.partial(exchange_kernel, axis, n, stride, gather),
        out_shape=jax.ShapeDtypeStruct(out_shape, x.dtype),
        in_specs=[pl.BlockSpec(memory_space=pl.ANY)],
        out_specs=pl.BlockSpec(memory_space=pl.ANY),
        scratch_shapes=[
            pltpu.SemaphoreType.DMA((n,)),
            pltpu.SemaphoreType.DMA((n,)),
            pltpu.SemaphoreType.DMA(()),
        ],
        compiler_params=pltpu.CompilerParams(collective_id=cid, has_side_effects=True),
    )(x)


def sketch_sum_kernel(
    n_chips, raw_ref, out_ref, half_send, core_buf, chip_send, chip_recv, core_sems, rs_send, rs_recv, ag_send, ag_recv
):
    me = lax.axis_index("in")
    core = lax.rem(me, 2)
    chip = me // 2
    partner = me + 1 - 2 * core
    rows = raw_ref.shape[0]
    half = rows // 2
    piece = half // n_chips
    my_half = core * half

    def chip_dev(k):
        return k * 2 + core

    barrier = pltpu.get_barrier_semaphore()
    pl.semaphore_signal(barrier, inc=1, device_id={"in": partner}, device_id_type=MESH)
    for d in range(1, n_chips):
        peer = lax.rem(chip + d, n_chips)
        pl.semaphore_signal(barrier, inc=1, device_id={"in": chip_dev(peer)}, device_id_type=MESH)
    pl.semaphore_wait(barrier, n_chips)

    other_half = (1 - core) * half

    def to_send(r, carry):
        half_send[r] = raw_ref[other_half + r].astype(half_send.dtype)
        return carry

    lax.fori_loop(0, half, to_send, 0)
    core_copy = pltpu.make_async_remote_copy(
        src_ref=half_send,
        dst_ref=core_buf,
        send_sem=core_sems.at[0],
        recv_sem=core_sems.at[1],
        device_id={"in": partner},
        device_id_type=MESH,
    )
    core_copy.start()
    core_copy.wait()

    def add_core(r, carry):
        chip_send[r] = (raw_ref[my_half + r] + core_buf[r].astype(jnp.float32)).astype(chip_send.dtype)
        return carry

    lax.fori_loop(0, half, add_core, 0)
    scatter = []
    for d in range(1, n_chips):
        peer = lax.rem(chip + d, n_chips)
        copy = pltpu.make_async_remote_copy(
            src_ref=chip_send.at[pl.ds(peer * piece, piece)],
            dst_ref=chip_recv.at[chip],
            send_sem=rs_send.at[d],
            recv_sem=rs_recv.at[d],
            device_id={"in": chip_dev(peer)},
            device_id_type=MESH,
        )
        copy.start()
        scatter.append(copy)
    for copy in scatter:
        copy.wait()

    base_row = my_half + chip * piece
    for q in range(piece):
        acc = chip_send[chip * piece + q].astype(jnp.float32)
        for d in range(1, n_chips):
            acc = acc + chip_recv[lax.rem(chip + d, n_chips), q].astype(jnp.float32)
        out_ref[base_row + q] = acc.astype(out_ref.dtype)

    gather = []
    for d in range(1, n_chips):
        peer = lax.rem(chip + d, n_chips)
        copy = pltpu.make_async_remote_copy(
            src_ref=out_ref.at[pl.ds(base_row, piece)],
            dst_ref=out_ref.at[pl.ds(base_row, piece)],
            send_sem=ag_send.at[d],
            recv_sem=ag_recv.at[d],
            device_id={"in": chip_dev(peer)},
            device_id_type=MESH,
        )
        copy.start()
        gather.append(copy)
    for copy in gather:
        copy.wait()
    core_back = pltpu.make_async_remote_copy(
        src_ref=out_ref.at[pl.ds(my_half, half)],
        dst_ref=out_ref.at[pl.ds(my_half, half)],
        send_sem=core_sems.at[2],
        recv_sem=core_sems.at[3],
        device_id={"in": partner},
        device_id_type=MESH,
    )
    core_back.start()
    core_back.wait()


def sketch_sum(raw, n_in, cid):
    rows, width, sk = raw.shape
    n_chips = n_in // 2
    half = rows // 2
    return pl.pallas_call(
        functools.partial(sketch_sum_kernel, n_chips),
        out_shape=jax.ShapeDtypeStruct(raw.shape, jnp.bfloat16),
        in_specs=[pl.BlockSpec(memory_space=pltpu.VMEM)],
        out_specs=pl.BlockSpec(memory_space=pltpu.VMEM),
        scratch_shapes=[
            pltpu.VMEM((half, width, sk), jnp.bfloat16),
            pltpu.VMEM((half, width, sk), jnp.bfloat16),
            pltpu.VMEM((half, width, sk), jnp.bfloat16),
            pltpu.VMEM((n_chips, half // n_chips, width, sk), jnp.bfloat16),
            pltpu.SemaphoreType.DMA((4,)),
            pltpu.SemaphoreType.DMA((n_chips,)),
            pltpu.SemaphoreType.DMA((n_chips,)),
            pltpu.SemaphoreType.DMA((n_chips,)),
            pltpu.SemaphoreType.DMA((n_chips,)),
        ],
        compiler_params=pltpu.CompilerParams(
            collective_id=cid, has_side_effects=True, vmem_limit_bytes=60 * 1024 * 1024
        ),
    )(raw)


def forward_rows(m_ref, probe_ref, i0, block):
    width, m_width = m_ref.shape[1], m_ref.shape[2]
    sk = probe_ref.shape[2]
    acc = jnp.zeros((block * width, sk), jnp.float32)
    for t in range(probe_ref.shape[0]):
        lo = m_ref[pl.ds(i0 + 2 * t, block)].reshape(block * width, m_width)
        hi = m_ref[pl.ds(i0 + 2 * t + 1, block)].reshape(block * width, m_width)
        lhs = jnp.concatenate([lo, hi], axis=1)
        acc = acc + jnp.dot(lhs, probe_ref[t], preferred_element_type=jnp.float32)
    return acc.reshape(block, width, sk)


def sketch_kernel(
    n_chips, m_ref, probe_ref, out_ref, gram_out, half_send, core_buf, chip_send, chip_recv,
    core_send, core_recv, rs_send, rs_recv, ag_send, ag_recv, back_sems, back_recv, gram_mine, gram_peer, gram_sems,
):
    me = lax.axis_index("in")
    core = lax.rem(me, 2)
    chip = me // 2
    partner = me + 1 - 2 * core
    rows = out_ref.shape[0]
    half = rows // 2
    piece = half // n_chips
    my_half = core * half
    other_half = (1 - core) * half

    def chip_dev(k):
        return k * 2 + core

    def chunk_of(step):
        return lax.rem(chip + step + 1, n_chips)

    def core_copy(step):
        c = chunk_of(step)
        return pltpu.make_async_remote_copy(
            src_ref=half_send.at[pl.ds(c * piece, piece)],
            dst_ref=core_buf.at[pl.ds(c * piece, piece)],
            send_sem=core_send.at[step],
            recv_sem=core_recv.at[step],
            device_id={"in": partner},
            device_id_type=MESH,
        )

    def rs_copy(step):
        c = chunk_of(step)
        return pltpu.make_async_remote_copy(
            src_ref=chip_send.at[pl.ds(c * piece, piece)],
            dst_ref=chip_recv.at[chip],
            send_sem=rs_send.at[step],
            recv_sem=rs_recv.at[step],
            device_id={"in": chip_dev(c)},
            device_id_type=MESH,
        )

    barrier = pltpu.get_barrier_semaphore()
    pl.semaphore_signal(barrier, inc=1, device_id={"in": partner}, device_id_type=MESH)
    for d in range(1, n_chips):
        pl.semaphore_signal(barrier, inc=1, device_id={"in": chip_dev(lax.rem(chip + d, n_chips))}, device_id_type=MESH)
    pl.semaphore_wait(barrier, n_chips)

    def partner_rows(step, carry):
        c = chunk_of(step)
        half_send[pl.ds(c * piece, piece)] = forward_rows(m_ref, probe_ref, other_half + c * piece, piece).astype(
            half_send.dtype
        )
        core_copy(step).start()
        return carry

    lax.fori_loop(0, n_chips, partner_rows, 0)

    def own_rows(step):
        c = chunk_of(step)
        mine = forward_rows(m_ref, probe_ref, my_half + c * piece, piece)
        core_copy(step).wait_recv()
        chip_send[pl.ds(c * piece, piece)] = (mine + core_buf[pl.ds(c * piece, piece)].astype(jnp.float32)).astype(
            chip_send.dtype
        )

    def chip_rows(step, carry):
        own_rows(step)
        rs_copy(step).start()
        return carry

    lax.fori_loop(0, n_chips - 1, chip_rows, 0)
    own_rows(n_chips - 1)

    for step in range(n_chips - 1):
        rs_copy(step).wait_recv()
    base_row = my_half + chip * piece
    for q in range(piece):
        acc = chip_send[chip * piece + q].astype(jnp.float32)
        for d in range(1, n_chips):
            acc = acc + chip_recv[lax.rem(chip + d, n_chips), q].astype(jnp.float32)
        out_ref[base_row + q] = acc.astype(out_ref.dtype)

    def ag_copy(d):
        return pltpu.make_async_remote_copy(
            src_ref=out_ref.at[pl.ds(base_row, piece)],
            dst_ref=out_ref.at[pl.ds(base_row, piece)],
            send_sem=ag_send.at[d],
            recv_sem=ag_recv.at[d],
            device_id={"in": chip_dev(lax.rem(chip + d, n_chips))},
            device_id_type=MESH,
        )

    def forward_copy(d):
        start = my_half + lax.rem(chip + n_chips - d, n_chips) * piece
        return pltpu.make_async_remote_copy(
            src_ref=out_ref.at[pl.ds(start, piece)],
            dst_ref=out_ref.at[pl.ds(start, piece)],
            send_sem=back_sems.at[d],
            recv_sem=back_recv.at[d],
            device_id={"in": partner},
            device_id_type=MESH,
        )

    def gram_of(start, acc):
        for q in range(piece):
            value = out_ref[start + q]
            acc = acc + lax.dot_general(value, value, (((0,), (0,)), ((), ())), preferred_element_type=jnp.float32)
        return acc

    forward_copy(0).start()
    for d in range(1, n_chips):
        ag_copy(d).start()
    sk = out_ref.shape[2]
    gram = gram_of(base_row, jnp.zeros((sk, sk), jnp.float32))
    for d in range(1, n_chips):
        ag_copy(d).wait_recv()
        forward_copy(d).start()
        gram = gram_of(my_half + lax.rem(chip + n_chips - d, n_chips) * piece, gram)
    gram_mine[...] = gram
    gram_copy = pltpu.make_async_remote_copy(
        src_ref=gram_mine,
        dst_ref=gram_peer,
        send_sem=gram_sems.at[0],
        recv_sem=gram_sems.at[1],
        device_id={"in": partner},
        device_id_type=MESH,
    )
    gram_copy.start()
    gram_copy.wait()
    gram_out[...] = gram_mine[...] + gram_peer[...]
    for step in range(n_chips):
        core_copy(step).wait_send()
    for step in range(n_chips - 1):
        rs_copy(step).wait_send()
    for d in range(1, n_chips):
        ag_copy(d).wait_send()
    for d in range(n_chips):
        forward_copy(d).wait()


def sketch_of(masked, probe_pairs, rows, n_in, cid):
    width = masked.shape[1]
    sk = probe_pairs.shape[2]
    n_chips = n_in // 2
    half = rows // 2
    return pl.pallas_call(
        functools.partial(sketch_kernel, n_chips),
        out_shape=(
            jax.ShapeDtypeStruct((rows, width, sk), jnp.bfloat16),
            jax.ShapeDtypeStruct((sk, sk), jnp.float32),
        ),
        in_specs=[pl.BlockSpec(memory_space=pltpu.VMEM)] * 2,
        out_specs=(pl.BlockSpec(memory_space=pltpu.VMEM),) * 2,
        scratch_shapes=[
            pltpu.VMEM((half, width, sk), jnp.bfloat16),
            pltpu.VMEM((half, width, sk), jnp.bfloat16),
            pltpu.VMEM((half, width, sk), jnp.bfloat16),
            pltpu.VMEM((n_chips, half // n_chips, width, sk), jnp.bfloat16),
            pltpu.SemaphoreType.DMA((n_chips,)),
            pltpu.SemaphoreType.DMA((n_chips,)),
            pltpu.SemaphoreType.DMA((n_chips,)),
            pltpu.SemaphoreType.DMA((n_chips,)),
            pltpu.SemaphoreType.DMA((n_chips,)),
            pltpu.SemaphoreType.DMA((n_chips,)),
            pltpu.SemaphoreType.DMA((n_chips,)),
            pltpu.SemaphoreType.DMA((n_chips,)),
            pltpu.VMEM((sk, sk), jnp.float32),
            pltpu.VMEM((sk, sk), jnp.float32),
            pltpu.SemaphoreType.DMA((2,)),
        ],
        compiler_params=pltpu.CompilerParams(
            collective_id=cid, has_side_effects=True, vmem_limit_bytes=60 * 1024 * 1024
        ),
    )(masked, probe_pairs)


def corange_kernel(
    n_out, scale, mt_ref, sketch_ref, gram_ref, co_out, gram_out, recv_ref, gram_recv, send_buf,
    co_send, co_recv, gram_send, gram_in, local_sems
):
    me = lax.axis_index("out")
    cols_all = send_buf.shape[1]
    m_width = mt_ref.shape[1]
    sk = sketch_ref.shape[2]
    rows = sketch_ref.shape[0]
    block = 4
    n_blocks = cols_all // (block * m_width)
    span = block * m_width
    per = sk // n_out

    barrier = pltpu.get_barrier_semaphore()
    for d in range(1, n_out):
        pl.semaphore_signal(barrier, inc=1, device_id={"out": lax.rem(me + d, n_out)}, device_id_type=MESH)
    pl.semaphore_wait(barrier, n_out - 1)

    def gram_copy(d):
        return pltpu.make_async_remote_copy(
            src_ref=gram_ref,
            dst_ref=gram_recv.at[me],
            send_sem=gram_send.at[d],
            recv_sem=gram_in.at[d],
            device_id={"out": lax.rem(me + d, n_out)},
            device_id_type=MESH,
        )

    gram_local = pltpu.make_async_copy(gram_ref, gram_recv.at[me], local_sems.at[n_blocks])
    gram_local.start()
    for d in range(1, n_out):
        gram_copy(d).start()

    def co_copy(d, b):
        k = lax.rem(me + d, n_out)
        return pltpu.make_async_remote_copy(
            src_ref=send_buf.at[pl.ds(pl.multiple_of(k * per, per), per), pl.ds(pl.multiple_of(b * span, span), span)],
            dst_ref=recv_ref.at[me, :, pl.ds(pl.multiple_of(b * span, span), span)],
            send_sem=co_send.at[d, b],
            recv_sem=co_recv.at[d, b],
            device_id={"out": k},
            device_id_type=MESH,
        )

    def local_copy(b):
        return pltpu.make_async_copy(
            send_buf.at[pl.ds(pl.multiple_of(me * per, per), per), pl.ds(pl.multiple_of(b * span, span), span)],
            recv_ref.at[me, :, pl.ds(pl.multiple_of(b * span, span), span)],
            local_sems.at[b],
        )

    def body(b, carry):
        j0 = b * block
        acc = jnp.zeros((span, sk), jnp.float32)
        for i in range(rows):
            lhs = mt_ref[pl.ds(j0 + i, block)].reshape(span, mt_ref.shape[2])
            acc = acc + jnp.dot(lhs, sketch_ref[i], preferred_element_type=jnp.float32)
        send_buf[:, pl.ds(pl.multiple_of(b * span, span), span)] = acc.T.astype(send_buf.dtype)
        local_copy(b).start()
        for d in range(1, n_out):
            co_copy(d, b).start()
        return carry

    lax.fori_loop(0, n_blocks, body, 0)

    def drain(b, carry):
        local_copy(b).wait()
        for d in range(1, n_out):
            co_copy(d, b).wait()
        return carry

    lax.fori_loop(0, n_blocks, drain, 0)
    gram_local.wait()
    for d in range(1, n_out):
        gram_copy(d).wait()
    co_total = recv_ref[0].astype(jnp.float32)
    gram_total = gram_recv[0].astype(jnp.float32)
    for k in range(1, n_out):
        co_total = co_total + recv_ref[k].astype(jnp.float32)
        gram_total = gram_total + gram_recv[k].astype(jnp.float32)
    co_out[...] = co_total
    gram_out[...] = gram_total * scale


def corange_of(mt, sketch, gram_part, cols, n_out, cid):
    m_width = mt.shape[1]
    sk = sketch.shape[2]
    n_blocks = cols // 4
    return pl.pallas_call(
        functools.partial(corange_kernel, n_out, 1.0 / (R * OUTPUT_CHANNELS)),
        out_shape=(
            jax.ShapeDtypeStruct((sk // n_out, cols * m_width), jnp.float32),
            jax.ShapeDtypeStruct(gram_part.shape, jnp.float32),
        ),
        in_specs=[pl.BlockSpec(memory_space=pltpu.VMEM)] * 3,
        out_specs=(pl.BlockSpec(memory_space=pltpu.VMEM),) * 2,
        scratch_shapes=[
            pltpu.VMEM((n_out, sk // n_out, cols * m_width), jnp.bfloat16),
            pltpu.VMEM((n_out,) + gram_part.shape, jnp.bfloat16),
            pltpu.VMEM((sk, cols * m_width), jnp.bfloat16),
            pltpu.SemaphoreType.DMA((n_out, n_blocks)),
            pltpu.SemaphoreType.DMA((n_out, n_blocks)),
            pltpu.SemaphoreType.DMA((n_out,)),
            pltpu.SemaphoreType.DMA((n_out,)),
            pltpu.SemaphoreType.DMA((n_blocks + 1,)),
        ],
        compiler_params=pltpu.CompilerParams(
            collective_id=cid, has_side_effects=True, vmem_limit_bytes=60 * 1024 * 1024
        ),
    )(mt, sketch, gram_part)


def shards(n_out, n_in, markov, probes, pattern):
    keeper = jnp.repeat(jnp.repeat(pattern, BO, axis=0), BI, axis=1).astype(jnp.bfloat16)
    masked, mt, gathered = prep(markov, keeper, probes, n_out, 0)
    panel = gathered.reshape((-1,) + probes.shape[1:])
    s_all, cols, m_width = panel.shape
    probe_pairs = jnp.swapaxes(panel.reshape(s_all, cols // 2, 2 * m_width), 0, 1).swapaxes(1, 2)
    sketch, local_gram = sketch_of(masked, probe_pairs, R, n_in, 1)
    co_sum, gram_matrix = corange_of(mt, sketch, local_gram.astype(jnp.bfloat16), cols, n_out, 4)
    corange = co_sum.reshape(s_all // n_out, cols, m_width)
    return (sketch, corange, gram_matrix)


def solution(mesh):
    return jax.shard_map(
        functools.partial(shards, mesh.shape["out"], mesh.shape["in"]),
        mesh=mesh,
        in_specs=(P(None, "out", "in"), P("out", None, "in"), P("out", "in")),
        out_specs=(P(None, "out", None), P("out", None, "in"), P()),
        check_vma=False,
    )
```

```python
import functools

import jax
import jax.numpy as jnp
from jax import lax
from jax.experimental import pallas as pl
from jax.experimental.pallas import tpu as pltpu
from jax.sharding import PartitionSpec as P

OUTPUT_CHANNELS = 2048
BO = 64
BI = 128
R = 32
C = 32

MESH = pl.DeviceIdType.MESH


def forward_kernel(m_ref, probe_ref, out_ref):
    rows, width, sk = out_ref.shape
    steps = probe_ref.shape[0]
    m_width = m_ref.shape[2]
    block = 2

    def body(b, carry):
        i0 = b * block
        acc = jnp.zeros((block * width, sk), jnp.float32)
        for t in range(steps):
            lo = m_ref[pl.ds(i0 + 2 * t, block)].reshape(block * width, m_width)
            hi = m_ref[pl.ds(i0 + 2 * t + 1, block)].reshape(block * width, m_width)
            lhs = jnp.concatenate([lo, hi], axis=1)
            acc = acc + jnp.dot(lhs, probe_ref[t], preferred_element_type=jnp.float32)
        out_ref[pl.ds(i0, block)] = acc.reshape(block, width, sk)
        return carry

    lax.fori_loop(0, rows // block, body, 0)


def forward_panel(pair, probe_pairs, rows):
    width = pair.shape[1]
    sk = probe_pairs.shape[2]
    return pl.pallas_call(
        forward_kernel,
        out_shape=jax.ShapeDtypeStruct((rows, width, sk), jnp.float32),
        in_specs=[pl.BlockSpec(memory_space=pltpu.VMEM)] * 2,
        out_specs=pl.BlockSpec(memory_space=pltpu.VMEM),
        compiler_params=pltpu.CompilerParams(vmem_limit_bytes=60 * 1024 * 1024),
    )(pair, probe_pairs)


def backward_kernel(mt_ref, sketch_ref, out_ref):
    cols, m_width, sk = out_ref.shape
    rows = sketch_ref.shape[0]
    block = 4

    def body(b, carry):
        j0 = b * block
        acc = jnp.zeros((block * m_width, sk), jnp.float32)
        for i in range(rows):
            lhs = mt_ref[pl.ds(j0 + i, block)].reshape(block * m_width, mt_ref.shape[2])
            acc = acc + jnp.dot(lhs, sketch_ref[i], preferred_element_type=jnp.float32)
        out_ref[pl.ds(j0, block)] = acc.reshape(block, m_width, sk)
        return carry

    lax.fori_loop(0, cols // block, body, 0)


def prep_kernel(n_out, markov_ref, keeper_ref, probes_ref, masked_ref, mt_ref, gathered_ref, send_sem, recv_sem, local_sem):
    me = lax.axis_index("out")
    barrier = pltpu.get_barrier_semaphore()
    for d in range(1, n_out):
        pl.semaphore_signal(barrier, inc=1, device_id={"out": lax.rem(me + d, n_out)}, device_id_type=MESH)
    pl.semaphore_wait(barrier, n_out - 1)
    local = pltpu.make_async_copy(probes_ref, gathered_ref.at[me], local_sem)
    local.start()
    copies = []
    for d in range(1, n_out):
        copy = pltpu.make_async_remote_copy(
            src_ref=probes_ref,
            dst_ref=gathered_ref.at[me],
            send_sem=send_sem.at[d],
            recv_sem=recv_sem.at[d],
            device_id={"out": lax.rem(me + d, n_out)},
            device_id_type=MESH,
        )
        copy.start()
        copies.append(copy)

    keeper = keeper_ref[...]

    def body(k, carry):
        value = markov_ref[k] * keeper
        masked_ref[k] = value
        mt_ref[k] = value.astype(jnp.float32).T.astype(mt_ref.dtype)
        return carry

    lax.fori_loop(0, markov_ref.shape[0], body, 0)
    local.wait()
    for copy in copies:
        copy.wait()


def prep(markov, keeper, probes, n_out, cid):
    lags, width, m_width = markov.shape
    return pl.pallas_call(
        functools.partial(prep_kernel, n_out),
        out_shape=(
            jax.ShapeDtypeStruct((lags, width, m_width), markov.dtype),
            jax.ShapeDtypeStruct((lags, m_width, width), markov.dtype),
            jax.ShapeDtypeStruct((n_out,) + probes.shape, probes.dtype),
        ),
        in_specs=[pl.BlockSpec(memory_space=pltpu.VMEM)] * 3,
        out_specs=(pl.BlockSpec(memory_space=pltpu.VMEM),) * 3,
        scratch_shapes=[
            pltpu.SemaphoreType.DMA((n_out,)),
            pltpu.SemaphoreType.DMA((n_out,)),
            pltpu.SemaphoreType.DMA(()),
        ],
        compiler_params=pltpu.CompilerParams(
            collective_id=cid, has_side_effects=True, vmem_limit_bytes=60 * 1024 * 1024
        ),
    )(markov, keeper, probes)


def backward_panel(mt, sketch, cols):
    m_width = mt.shape[1]
    sk = sketch.shape[2]
    return pl.pallas_call(
        backward_kernel,
        out_shape=jax.ShapeDtypeStruct((cols, m_width, sk), jnp.float32),
        in_specs=[pl.BlockSpec(memory_space=pltpu.VMEM)] * 2,
        out_specs=pl.BlockSpec(memory_space=pltpu.VMEM),
        compiler_params=pltpu.CompilerParams(vmem_limit_bytes=60 * 1024 * 1024),
    )(mt, sketch)


def exchange_kernel(axis, n, stride, gather, x_ref, y_ref, send_sem, recv_sem, local_sem):
    me = lax.axis_index(axis)
    pos = lax.rem(me // stride, n)
    base = me - pos * stride

    def member(k):
        return base + k * stride

    barrier = pltpu.get_barrier_semaphore()
    for d in range(1, n):
        peer = lax.rem(pos + d, n)
        pl.semaphore_signal(barrier, inc=1, device_id={axis: member(peer)}, device_id_type=MESH)
    pl.semaphore_wait(barrier, n - 1)

    own_src = x_ref if gather else x_ref.at[pos]
    local = pltpu.make_async_copy(own_src, y_ref.at[pos], local_sem)
    local.start()
    copies = []
    for d in range(1, n):
        peer = lax.rem(pos + d, n)
        src = x_ref if gather else x_ref.at[peer]
        copy = pltpu.make_async_remote_copy(
            src_ref=src,
            dst_ref=y_ref.at[pos],
            send_sem=send_sem.at[d],
            recv_sem=recv_sem.at[d],
            device_id={axis: member(peer)},
            device_id_type=MESH,
        )
        copy.start()
        copies.append(copy)
    local.wait()
    for copy in copies:
        copy.wait()


def exchange(x, axis, n, stride, gather, cid):
    out_shape = (n,) + (x.shape if gather else x.shape[1:])
    return pl.pallas_call(
        functools.partial(exchange_kernel, axis, n, stride, gather),
        out_shape=jax.ShapeDtypeStruct(out_shape, x.dtype),
        in_specs=[pl.BlockSpec(memory_space=pl.ANY)],
        out_specs=pl.BlockSpec(memory_space=pl.ANY),
        scratch_shapes=[
            pltpu.SemaphoreType.DMA((n,)),
            pltpu.SemaphoreType.DMA((n,)),
            pltpu.SemaphoreType.DMA(()),
        ],
        compiler_params=pltpu.CompilerParams(collective_id=cid, has_side_effects=True),
    )(x)


def sketch_sum_kernel(
    n_chips, raw_ref, out_ref, half_send, core_buf, chip_send, chip_recv, core_sems, rs_send, rs_recv, ag_send, ag_recv
):
    me = lax.axis_index("in")
    core = lax.rem(me, 2)
    chip = me // 2
    partner = me + 1 - 2 * core
    rows = raw_ref.shape[0]
    half = rows // 2
    piece = half // n_chips
    my_half = core * half

    def chip_dev(k):
        return k * 2 + core

    barrier = pltpu.get_barrier_semaphore()
    pl.semaphore_signal(barrier, inc=1, device_id={"in": partner}, device_id_type=MESH)
    for d in range(1, n_chips):
        peer = lax.rem(chip + d, n_chips)
        pl.semaphore_signal(barrier, inc=1, device_id={"in": chip_dev(peer)}, device_id_type=MESH)
    pl.semaphore_wait(barrier, n_chips)

    other_half = (1 - core) * half

    def to_send(r, carry):
        half_send[r] = raw_ref[other_half + r].astype(half_send.dtype)
        return carry

    lax.fori_loop(0, half, to_send, 0)
    core_copy = pltpu.make_async_remote_copy(
        src_ref=half_send,
        dst_ref=core_buf,
        send_sem=core_sems.at[0],
        recv_sem=core_sems.at[1],
        device_id={"in": partner},
        device_id_type=MESH,
    )
    core_copy.start()
    core_copy.wait()

    def add_core(r, carry):
        chip_send[r] = (raw_ref[my_half + r] + core_buf[r].astype(jnp.float32)).astype(chip_send.dtype)
        return carry

    lax.fori_loop(0, half, add_core, 0)
    scatter = []
    for d in range(1, n_chips):
        peer = lax.rem(chip + d, n_chips)
        copy = pltpu.make_async_remote_copy(
            src_ref=chip_send.at[pl.ds(peer * piece, piece)],
            dst_ref=chip_recv.at[chip],
            send_sem=rs_send.at[d],
            recv_sem=rs_recv.at[d],
            device_id={"in": chip_dev(peer)},
            device_id_type=MESH,
        )
        copy.start()
        scatter.append(copy)
    for copy in scatter:
        copy.wait()

    base_row = my_half + chip * piece
    for q in range(piece):
        acc = chip_send[chip * piece + q].astype(jnp.float32)
        for d in range(1, n_chips):
            acc = acc + chip_recv[lax.rem(chip + d, n_chips), q].astype(jnp.float32)
        out_ref[base_row + q] = acc.astype(out_ref.dtype)

    gather = []
    for d in range(1, n_chips):
        peer = lax.rem(chip + d, n_chips)
        copy = pltpu.make_async_remote_copy(
            src_ref=out_ref.at[pl.ds(base_row, piece)],
            dst_ref=out_ref.at[pl.ds(base_row, piece)],
            send_sem=ag_send.at[d],
            recv_sem=ag_recv.at[d],
            device_id={"in": chip_dev(peer)},
            device_id_type=MESH,
        )
        copy.start()
        gather.append(copy)
    for copy in gather:
        copy.wait()
    core_back = pltpu.make_async_remote_copy(
        src_ref=out_ref.at[pl.ds(my_half, half)],
        dst_ref=out_ref.at[pl.ds(my_half, half)],
        send_sem=core_sems.at[2],
        recv_sem=core_sems.at[3],
        device_id={"in": partner},
        device_id_type=MESH,
    )
    core_back.start()
    core_back.wait()


def sketch_sum(raw, n_in, cid):
    rows, width, sk = raw.shape
    n_chips = n_in // 2
    half = rows // 2
    return pl.pallas_call(
        functools.partial(sketch_sum_kernel, n_chips),
        out_shape=jax.ShapeDtypeStruct(raw.shape, jnp.bfloat16),
        in_specs=[pl.BlockSpec(memory_space=pltpu.VMEM)],
        out_specs=pl.BlockSpec(memory_space=pltpu.VMEM),
        scratch_shapes=[
            pltpu.VMEM((half, width, sk), jnp.bfloat16),
            pltpu.VMEM((half, width, sk), jnp.bfloat16),
            pltpu.VMEM((half, width, sk), jnp.bfloat16),
            pltpu.VMEM((n_chips, half // n_chips, width, sk), jnp.bfloat16),
            pltpu.SemaphoreType.DMA((4,)),
            pltpu.SemaphoreType.DMA((n_chips,)),
            pltpu.SemaphoreType.DMA((n_chips,)),
            pltpu.SemaphoreType.DMA((n_chips,)),
            pltpu.SemaphoreType.DMA((n_chips,)),
        ],
        compiler_params=pltpu.CompilerParams(
            collective_id=cid, has_side_effects=True, vmem_limit_bytes=60 * 1024 * 1024
        ),
    )(raw)


def forward_rows(m_ref, probe_ref, i0, block):
    width, m_width = m_ref.shape[1], m_ref.shape[2]
    sk = probe_ref.shape[2]
    acc = jnp.zeros((block * width, sk), jnp.float32)
    for t in range(probe_ref.shape[0]):
        lo = m_ref[pl.ds(i0 + 2 * t, block)].reshape(block * width, m_width)
        hi = m_ref[pl.ds(i0 + 2 * t + 1, block)].reshape(block * width, m_width)
        lhs = jnp.concatenate([lo, hi], axis=1)
        acc = acc + jnp.dot(lhs, probe_ref[t], preferred_element_type=jnp.float32)
    return acc.reshape(block, width, sk)


def sketch_kernel(
    n_chips, m_ref, probe_ref, out_ref, gram_out, half_send, core_buf, chip_send, chip_recv,
    core_send, core_recv, rs_send, rs_recv, ag_send, ag_recv, back_sems, back_recv, gram_mine, gram_peer, gram_sems,
):
    me = lax.axis_index("in")
    core = lax.rem(me, 2)
    chip = me // 2
    partner = me + 1 - 2 * core
    rows = out_ref.shape[0]
    half = rows // 2
    piece = half // n_chips
    my_half = core * half
    other_half = (1 - core) * half

    def chip_dev(k):
        return k * 2 + core

    def chunk_of(step):
        return lax.rem(chip + step + 1, n_chips)

    def core_copy(step):
        c = chunk_of(step)
        return pltpu.make_async_remote_copy(
            src_ref=half_send.at[pl.ds(c * piece, piece)],
            dst_ref=core_buf.at[pl.ds(c * piece, piece)],
            send_sem=core_send.at[step],
            recv_sem=core_recv.at[step],
            device_id={"in": partner},
            device_id_type=MESH,
        )

    def rs_copy(step):
        c = chunk_of(step)
        return pltpu.make_async_remote_copy(
            src_ref=chip_send.at[pl.ds(c * piece, piece)],
            dst_ref=chip_recv.at[chip],
            send_sem=rs_send.at[step],
            recv_sem=rs_recv.at[step],
            device_id={"in": chip_dev(c)},
            device_id_type=MESH,
        )

    barrier = pltpu.get_barrier_semaphore()
    pl.semaphore_signal(barrier, inc=1, device_id={"in": partner}, device_id_type=MESH)
    for d in range(1, n_chips):
        pl.semaphore_signal(barrier, inc=1, device_id={"in": chip_dev(lax.rem(chip + d, n_chips))}, device_id_type=MESH)
    pl.semaphore_wait(barrier, n_chips)

    def partner_rows(step, carry):
        c = chunk_of(step)
        half_send[pl.ds(c * piece, piece)] = forward_rows(m_ref, probe_ref, other_half + c * piece, piece).astype(
            half_send.dtype
        )
        core_copy(step).start()
        return carry

    lax.fori_loop(0, n_chips, partner_rows, 0)

    def own_rows(step):
        c = chunk_of(step)
        mine = forward_rows(m_ref, probe_ref, my_half + c * piece, piece)
        core_copy(step).wait_recv()
        chip_send[pl.ds(c * piece, piece)] = (mine + core_buf[pl.ds(c * piece, piece)].astype(jnp.float32)).astype(
            chip_send.dtype
        )

    def chip_rows(step, carry):
        own_rows(step)
        rs_copy(step).start()
        return carry

    lax.fori_loop(0, n_chips - 1, chip_rows, 0)
    own_rows(n_chips - 1)

    for step in range(n_chips - 1):
        rs_copy(step).wait_recv()
    base_row = my_half + chip * piece
    for q in range(piece):
        acc = chip_send[chip * piece + q].astype(jnp.float32)
        for d in range(1, n_chips):
            acc = acc + chip_recv[lax.rem(chip + d, n_chips), q].astype(jnp.float32)
        out_ref[base_row + q] = acc.astype(out_ref.dtype)

    def ag_copy(d):
        return pltpu.make_async_remote_copy(
            src_ref=out_ref.at[pl.ds(base_row, piece)],
            dst_ref=out_ref.at[pl.ds(base_row, piece)],
            send_sem=ag_send.at[d],
            recv_sem=ag_recv.at[d],
            device_id={"in": chip_dev(lax.rem(chip + d, n_chips))},
            device_id_type=MESH,
        )

    def forward_copy(d):
        start = my_half + lax.rem(chip + n_chips - d, n_chips) * piece
        return pltpu.make_async_remote_copy(
            src_ref=out_ref.at[pl.ds(start, piece)],
            dst_ref=out_ref.at[pl.ds(start, piece)],
            send_sem=back_sems.at[d],
            recv_sem=back_recv.at[d],
            device_id={"in": partner},
            device_id_type=MESH,
        )

    def gram_of(start, acc):
        for q in range(piece):
            value = out_ref[start + q]
            acc = acc + lax.dot_general(value, value, (((0,), (0,)), ((), ())), preferred_element_type=jnp.float32)
        return acc

    forward_copy(0).start()
    for d in range(1, n_chips):
        ag_copy(d).start()
    sk = out_ref.shape[2]
    gram = gram_of(base_row, jnp.zeros((sk, sk), jnp.float32))
    for d in range(1, n_chips):
        ag_copy(d).wait_recv()
        forward_copy(d).start()
        gram = gram_of(my_half + lax.rem(chip + n_chips - d, n_chips) * piece, gram)
    gram_mine[...] = gram
    gram_copy = pltpu.make_async_remote_copy(
        src_ref=gram_mine,
        dst_ref=gram_peer,
        send_sem=gram_sems.at[0],
        recv_sem=gram_sems.at[1],
        device_id={"in": partner},
        device_id_type=MESH,
    )
    gram_copy.start()
    gram_copy.wait()
    gram_out[...] = (gram_mine[...] + gram_peer[...]).astype(gram_out.dtype)
    for step in range(n_chips):
        core_copy(step).wait_send()
    for step in range(n_chips - 1):
        rs_copy(step).wait_send()
    for d in range(1, n_chips):
        ag_copy(d).wait_send()
    for d in range(n_chips):
        forward_copy(d).wait()


def sketch_of(masked, probe_pairs, rows, n_in, cid):
    width = masked.shape[1]
    sk = probe_pairs.shape[2]
    n_chips = n_in // 2
    half = rows // 2
    return pl.pallas_call(
        functools.partial(sketch_kernel, n_chips),
        out_shape=(
            jax.ShapeDtypeStruct((rows, width, sk), jnp.bfloat16),
            jax.ShapeDtypeStruct((sk, sk), jnp.bfloat16),
        ),
        in_specs=[pl.BlockSpec(memory_space=pltpu.VMEM)] * 2,
        out_specs=(pl.BlockSpec(memory_space=pltpu.VMEM),) * 2,
        scratch_shapes=[
            pltpu.VMEM((half, width, sk), jnp.bfloat16),
            pltpu.VMEM((half, width, sk), jnp.bfloat16),
            pltpu.VMEM((half, width, sk), jnp.bfloat16),
            pltpu.VMEM((n_chips, half // n_chips, width, sk), jnp.bfloat16),
            pltpu.SemaphoreType.DMA((n_chips,)),
            pltpu.SemaphoreType.DMA((n_chips,)),
            pltpu.SemaphoreType.DMA((n_chips,)),
            pltpu.SemaphoreType.DMA((n_chips,)),
            pltpu.SemaphoreType.DMA((n_chips,)),
            pltpu.SemaphoreType.DMA((n_chips,)),
            pltpu.SemaphoreType.DMA((n_chips,)),
            pltpu.SemaphoreType.DMA((n_chips,)),
            pltpu.VMEM((sk, sk), jnp.float32),
            pltpu.VMEM((sk, sk), jnp.float32),
            pltpu.SemaphoreType.DMA((2,)),
        ],
        compiler_params=pltpu.CompilerParams(
            collective_id=cid, has_side_effects=True, vmem_limit_bytes=60 * 1024 * 1024
        ),
    )(masked, probe_pairs)


def corange_kernel(
    n_out, scale, mt_ref, sketch_ref, gram_ref, co_out, gram_out, recv_ref, gram_recv, send_buf,
    co_send, co_recv, gram_send, gram_in, local_sems
):
    me = lax.axis_index("out")
    cols_all = send_buf.shape[1]
    m_width = mt_ref.shape[1]
    sk = sketch_ref.shape[2]
    rows = sketch_ref.shape[0]
    block = 4
    n_blocks = cols_all // (block * m_width)
    span = block * m_width
    per = sk // n_out

    barrier = pltpu.get_barrier_semaphore()
    for d in range(1, n_out):
        pl.semaphore_signal(barrier, inc=1, device_id={"out": lax.rem(me + d, n_out)}, device_id_type=MESH)
    pl.semaphore_wait(barrier, n_out - 1)

    def gram_copy(d):
        return pltpu.make_async_remote_copy(
            src_ref=gram_ref,
            dst_ref=gram_recv.at[me],
            send_sem=gram_send.at[d],
            recv_sem=gram_in.at[d],
            device_id={"out": lax.rem(me + d, n_out)},
            device_id_type=MESH,
        )

    gram_local = pltpu.make_async_copy(gram_ref, gram_recv.at[me], local_sems.at[n_blocks])
    gram_local.start()
    for d in range(1, n_out):
        gram_copy(d).start()

    def co_copy(d, b):
        k = lax.rem(me + d, n_out)
        return pltpu.make_async_remote_copy(
            src_ref=send_buf.at[pl.ds(pl.multiple_of(k * per, per), per), pl.ds(pl.multiple_of(b * span, span), span)],
            dst_ref=recv_ref.at[me, :, pl.ds(pl.multiple_of(b * span, span), span)],
            send_sem=co_send.at[d, b],
            recv_sem=co_recv.at[d, b],
            device_id={"out": k},
            device_id_type=MESH,
        )

    def local_copy(b):
        return pltpu.make_async_copy(
            send_buf.at[pl.ds(pl.multiple_of(me * per, per), per), pl.ds(pl.multiple_of(b * span, span), span)],
            recv_ref.at[me, :, pl.ds(pl.multiple_of(b * span, span), span)],
            local_sems.at[b],
        )

    def body(b, carry):
        j0 = b * block
        acc = jnp.zeros((span, sk), jnp.float32)
        for i in range(rows):
            lhs = mt_ref[pl.ds(j0 + i, block)].reshape(span, mt_ref.shape[2])
            acc = acc + jnp.dot(lhs, sketch_ref[i], preferred_element_type=jnp.float32)
        send_buf[:, pl.ds(pl.multiple_of(b * span, span), span)] = acc.T.astype(send_buf.dtype)
        local_copy(b).start()
        for d in range(1, n_out):
            co_copy(d, b).start()
        return carry

    lax.fori_loop(0, n_blocks, body, 0)

    def drain(b, carry):
        local_copy(b).wait()
        for d in range(1, n_out):
            co_copy(d, b).wait()
        return carry

    lax.fori_loop(0, n_blocks, drain, 0)
    gram_local.wait()
    for d in range(1, n_out):
        gram_copy(d).wait()
    co_total = recv_ref[0].astype(jnp.float32)
    gram_total = gram_recv[0].astype(jnp.float32)
    for k in range(1, n_out):
        co_total = co_total + recv_ref[k].astype(jnp.float32)
        gram_total = gram_total + gram_recv[k].astype(jnp.float32)
    co_out[...] = co_total
    gram_out[...] = gram_total * scale


def corange_of(mt, sketch, gram_part, cols, n_out, cid):
    m_width = mt.shape[1]
    sk = sketch.shape[2]
    n_blocks = cols // 4
    return pl.pallas_call(
        functools.partial(corange_kernel, n_out, 1.0 / (R * OUTPUT_CHANNELS)),
        out_shape=(
            jax.ShapeDtypeStruct((sk // n_out, cols * m_width), jnp.float32),
            jax.ShapeDtypeStruct(gram_part.shape, jnp.float32),
        ),
        in_specs=[pl.BlockSpec(memory_space=pltpu.VMEM)] * 3,
        out_specs=(pl.BlockSpec(memory_space=pltpu.VMEM),) * 2,
        scratch_shapes=[
            pltpu.VMEM((n_out, sk // n_out, cols * m_width), jnp.bfloat16),
            pltpu.VMEM((n_out,) + gram_part.shape, jnp.bfloat16),
            pltpu.VMEM((sk, cols * m_width), jnp.bfloat16),
            pltpu.SemaphoreType.DMA((n_out, n_blocks)),
            pltpu.SemaphoreType.DMA((n_out, n_blocks)),
            pltpu.SemaphoreType.DMA((n_out,)),
            pltpu.SemaphoreType.DMA((n_out,)),
            pltpu.SemaphoreType.DMA((n_blocks + 1,)),
        ],
        compiler_params=pltpu.CompilerParams(
            collective_id=cid, has_side_effects=True, vmem_limit_bytes=60 * 1024 * 1024
        ),
    )(mt, sketch, gram_part)


def shards(n_out, n_in, markov, probes, pattern):
    keeper = jnp.repeat(jnp.repeat(pattern, BO, axis=0), BI, axis=1).astype(jnp.bfloat16)
    masked, mt, gathered = prep(markov, keeper, probes, n_out, 0)
    panel = gathered.reshape((-1,) + probes.shape[1:])
    s_all, cols, m_width = panel.shape
    probe_pairs = jnp.swapaxes(panel.reshape(s_all, cols // 2, 2 * m_width), 0, 1).swapaxes(1, 2)
    sketch, local_gram = sketch_of(masked, probe_pairs, R, n_in, 1)
    co_sum, gram_matrix = corange_of(mt, sketch, local_gram, cols, n_out, 4)
    corange = co_sum.reshape(s_all // n_out, cols, m_width)
    return (sketch, corange, gram_matrix)


def solution(mesh):
    return jax.shard_map(
        functools.partial(shards, mesh.shape["out"], mesh.shape["in"]),
        mesh=mesh,
        in_specs=(P(None, "out", "in"), P("out", None, "in"), P("out", "in")),
        out_specs=(P(None, "out", None), P("out", None, "in"), P()),
        check_vma=False,
    )
```

```python
import functools

import jax
import jax.numpy as jnp
from jax import lax
from jax.experimental import pallas as pl
from jax.experimental.pallas import tpu as pltpu
from jax.sharding import PartitionSpec as P

OUTPUT_CHANNELS = 2048
BO = 64
BI = 128
R = 32
C = 32

MESH = pl.DeviceIdType.MESH


def forward_kernel(m_ref, probe_ref, out_ref):
    rows, width, sk = out_ref.shape
    steps = probe_ref.shape[0]
    m_width = m_ref.shape[2]
    block = 2

    def body(b, carry):
        i0 = b * block
        acc = jnp.zeros((block * width, sk), jnp.float32)
        for t in range(steps):
            lo = m_ref[pl.ds(i0 + 2 * t, block)].reshape(block * width, m_width)
            hi = m_ref[pl.ds(i0 + 2 * t + 1, block)].reshape(block * width, m_width)
            lhs = jnp.concatenate([lo, hi], axis=1)
            acc = acc + jnp.dot(lhs, probe_ref[t], preferred_element_type=jnp.float32)
        out_ref[pl.ds(i0, block)] = acc.reshape(block, width, sk)
        return carry

    lax.fori_loop(0, rows // block, body, 0)


def forward_panel(pair, probe_pairs, rows):
    width = pair.shape[1]
    sk = probe_pairs.shape[2]
    return pl.pallas_call(
        forward_kernel,
        out_shape=jax.ShapeDtypeStruct((rows, width, sk), jnp.float32),
        in_specs=[pl.BlockSpec(memory_space=pltpu.VMEM)] * 2,
        out_specs=pl.BlockSpec(memory_space=pltpu.VMEM),
        compiler_params=pltpu.CompilerParams(vmem_limit_bytes=60 * 1024 * 1024),
    )(pair, probe_pairs)


def backward_kernel(mt_ref, sketch_ref, out_ref):
    cols, m_width, sk = out_ref.shape
    rows = sketch_ref.shape[0]
    block = 4

    def body(b, carry):
        j0 = b * block
        acc = jnp.zeros((block * m_width, sk), jnp.float32)
        for i in range(rows):
            lhs = mt_ref[pl.ds(j0 + i, block)].reshape(block * m_width, mt_ref.shape[2])
            acc = acc + jnp.dot(lhs, sketch_ref[i], preferred_element_type=jnp.float32)
        out_ref[pl.ds(j0, block)] = acc.reshape(block, m_width, sk)
        return carry

    lax.fori_loop(0, cols // block, body, 0)


def prep_kernel(n_out, markov_ref, keeper_ref, probes_ref, masked_ref, mt_ref, gathered_ref, send_sem, recv_sem, local_sem):
    me = lax.axis_index("out")
    barrier = pltpu.get_barrier_semaphore()
    for d in range(1, n_out):
        pl.semaphore_signal(barrier, inc=1, device_id={"out": lax.rem(me + d, n_out)}, device_id_type=MESH)
    pl.semaphore_wait(barrier, n_out - 1)
    local = pltpu.make_async_copy(probes_ref, gathered_ref.at[me], local_sem)
    local.start()
    copies = []
    for d in range(1, n_out):
        copy = pltpu.make_async_remote_copy(
            src_ref=probes_ref,
            dst_ref=gathered_ref.at[me],
            send_sem=send_sem.at[d],
            recv_sem=recv_sem.at[d],
            device_id={"out": lax.rem(me + d, n_out)},
            device_id_type=MESH,
        )
        copy.start()
        copies.append(copy)

    keeper = keeper_ref[...]

    def body(k, carry):
        value = markov_ref[k] * keeper
        masked_ref[k] = value
        mt_ref[k] = value.astype(jnp.float32).T.astype(mt_ref.dtype)
        return carry

    lax.fori_loop(0, markov_ref.shape[0], body, 0)
    local.wait()
    for copy in copies:
        copy.wait()


def prep(markov, keeper, probes, n_out, cid):
    lags, width, m_width = markov.shape
    return pl.pallas_call(
        functools.partial(prep_kernel, n_out),
        out_shape=(
            jax.ShapeDtypeStruct((lags, width, m_width), markov.dtype),
            jax.ShapeDtypeStruct((lags, m_width, width), markov.dtype),
            jax.ShapeDtypeStruct((n_out,) + probes.shape, probes.dtype),
        ),
        in_specs=[pl.BlockSpec(memory_space=pltpu.VMEM)] * 3,
        out_specs=(pl.BlockSpec(memory_space=pltpu.VMEM),) * 3,
        scratch_shapes=[
            pltpu.SemaphoreType.DMA((n_out,)),
            pltpu.SemaphoreType.DMA((n_out,)),
            pltpu.SemaphoreType.DMA(()),
        ],
        compiler_params=pltpu.CompilerParams(
            collective_id=cid, has_side_effects=True, vmem_limit_bytes=60 * 1024 * 1024
        ),
    )(markov, keeper, probes)


def backward_panel(mt, sketch, cols):
    m_width = mt.shape[1]
    sk = sketch.shape[2]
    return pl.pallas_call(
        backward_kernel,
        out_shape=jax.ShapeDtypeStruct((cols, m_width, sk), jnp.float32),
        in_specs=[pl.BlockSpec(memory_space=pltpu.VMEM)] * 2,
        out_specs=pl.BlockSpec(memory_space=pltpu.VMEM),
        compiler_params=pltpu.CompilerParams(vmem_limit_bytes=60 * 1024 * 1024),
    )(mt, sketch)


def exchange_kernel(axis, n, stride, gather, x_ref, y_ref, send_sem, recv_sem, local_sem):
    me = lax.axis_index(axis)
    pos = lax.rem(me // stride, n)
    base = me - pos * stride

    def member(k):
        return base + k * stride

    barrier = pltpu.get_barrier_semaphore()
    for d in range(1, n):
        peer = lax.rem(pos + d, n)
        pl.semaphore_signal(barrier, inc=1, device_id={axis: member(peer)}, device_id_type=MESH)
    pl.semaphore_wait(barrier, n - 1)

    own_src = x_ref if gather else x_ref.at[pos]
    local = pltpu.make_async_copy(own_src, y_ref.at[pos], local_sem)
    local.start()
    copies = []
    for d in range(1, n):
        peer = lax.rem(pos + d, n)
        src = x_ref if gather else x_ref.at[peer]
        copy = pltpu.make_async_remote_copy(
            src_ref=src,
            dst_ref=y_ref.at[pos],
            send_sem=send_sem.at[d],
            recv_sem=recv_sem.at[d],
            device_id={axis: member(peer)},
            device_id_type=MESH,
        )
        copy.start()
        copies.append(copy)
    local.wait()
    for copy in copies:
        copy.wait()


def exchange(x, axis, n, stride, gather, cid):
    out_shape = (n,) + (x.shape if gather else x.shape[1:])
    return pl.pallas_call(
        functools.partial(exchange_kernel, axis, n, stride, gather),
        out_shape=jax.ShapeDtypeStruct(out_shape, x.dtype),
        in_specs=[pl.BlockSpec(memory_space=pl.ANY)],
        out_specs=pl.BlockSpec(memory_space=pl.ANY),
        scratch_shapes=[
            pltpu.SemaphoreType.DMA((n,)),
            pltpu.SemaphoreType.DMA((n,)),
            pltpu.SemaphoreType.DMA(()),
        ],
        compiler_params=pltpu.CompilerParams(collective_id=cid, has_side_effects=True),
    )(x)


def sketch_sum_kernel(
    n_chips, raw_ref, out_ref, half_send, core_buf, chip_send, chip_recv, core_sems, rs_send, rs_recv, ag_send, ag_recv
):
    me = lax.axis_index("in")
    core = lax.rem(me, 2)
    chip = me // 2
    partner = me + 1 - 2 * core
    rows = raw_ref.shape[0]
    half = rows // 2
    piece = half // n_chips
    my_half = core * half

    def chip_dev(k):
        return k * 2 + core

    barrier = pltpu.get_barrier_semaphore()
    pl.semaphore_signal(barrier, inc=1, device_id={"in": partner}, device_id_type=MESH)
    for d in range(1, n_chips):
        peer = lax.rem(chip + d, n_chips)
        pl.semaphore_signal(barrier, inc=1, device_id={"in": chip_dev(peer)}, device_id_type=MESH)
    pl.semaphore_wait(barrier, n_chips)

    other_half = (1 - core) * half

    def to_send(r, carry):
        half_send[r] = raw_ref[other_half + r].astype(half_send.dtype)
        return carry

    lax.fori_loop(0, half, to_send, 0)
    core_copy = pltpu.make_async_remote_copy(
        src_ref=half_send,
        dst_ref=core_buf,
        send_sem=core_sems.at[0],
        recv_sem=core_sems.at[1],
        device_id={"in": partner},
        device_id_type=MESH,
    )
    core_copy.start()
    core_copy.wait()

    def add_core(r, carry):
        chip_send[r] = (raw_ref[my_half + r] + core_buf[r].astype(jnp.float32)).astype(chip_send.dtype)
        return carry

    lax.fori_loop(0, half, add_core, 0)
    scatter = []
    for d in range(1, n_chips):
        peer = lax.rem(chip + d, n_chips)
        copy = pltpu.make_async_remote_copy(
            src_ref=chip_send.at[pl.ds(peer * piece, piece)],
            dst_ref=chip_recv.at[chip],
            send_sem=rs_send.at[d],
            recv_sem=rs_recv.at[d],
            device_id={"in": chip_dev(peer)},
            device_id_type=MESH,
        )
        copy.start()
        scatter.append(copy)
    for copy in scatter:
        copy.wait()

    base_row = my_half + chip * piece
    for q in range(piece):
        acc = chip_send[chip * piece + q].astype(jnp.float32)
        for d in range(1, n_chips):
            acc = acc + chip_recv[lax.rem(chip + d, n_chips), q].astype(jnp.float32)
        out_ref[base_row + q] = acc.astype(out_ref.dtype)

    gather = []
    for d in range(1, n_chips):
        peer = lax.rem(chip + d, n_chips)
        copy = pltpu.make_async_remote_copy(
            src_ref=out_ref.at[pl.ds(base_row, piece)],
            dst_ref=out_ref.at[pl.ds(base_row, piece)],
            send_sem=ag_send.at[d],
            recv_sem=ag_recv.at[d],
            device_id={"in": chip_dev(peer)},
            device_id_type=MESH,
        )
        copy.start()
        gather.append(copy)
    for copy in gather:
        copy.wait()
    core_back = pltpu.make_async_remote_copy(
        src_ref=out_ref.at[pl.ds(my_half, half)],
        dst_ref=out_ref.at[pl.ds(my_half, half)],
        send_sem=core_sems.at[2],
        recv_sem=core_sems.at[3],
        device_id={"in": partner},
        device_id_type=MESH,
    )
    core_back.start()
    core_back.wait()


def sketch_sum(raw, n_in, cid):
    rows, width, sk = raw.shape
    n_chips = n_in // 2
    half = rows // 2
    return pl.pallas_call(
        functools.partial(sketch_sum_kernel, n_chips),
        out_shape=jax.ShapeDtypeStruct(raw.shape, jnp.bfloat16),
        in_specs=[pl.BlockSpec(memory_space=pltpu.VMEM)],
        out_specs=pl.BlockSpec(memory_space=pltpu.VMEM),
        scratch_shapes=[
            pltpu.VMEM((half, width, sk), jnp.bfloat16),
            pltpu.VMEM((half, width, sk), jnp.bfloat16),
            pltpu.VMEM((half, width, sk), jnp.bfloat16),
            pltpu.VMEM((n_chips, half // n_chips, width, sk), jnp.bfloat16),
            pltpu.SemaphoreType.DMA((4,)),
            pltpu.SemaphoreType.DMA((n_chips,)),
            pltpu.SemaphoreType.DMA((n_chips,)),
            pltpu.SemaphoreType.DMA((n_chips,)),
            pltpu.SemaphoreType.DMA((n_chips,)),
        ],
        compiler_params=pltpu.CompilerParams(
            collective_id=cid, has_side_effects=True, vmem_limit_bytes=60 * 1024 * 1024
        ),
    )(raw)


def forward_rows(m_ref, probe_ref, i0, block):
    width, m_width = m_ref.shape[1], m_ref.shape[2]
    sk = probe_ref.shape[2]
    acc = jnp.zeros((block * width, sk), jnp.float32)
    for t in range(probe_ref.shape[0]):
        lo = m_ref[pl.ds(i0 + 2 * t, block)].reshape(block * width, m_width)
        hi = m_ref[pl.ds(i0 + 2 * t + 1, block)].reshape(block * width, m_width)
        lhs = jnp.concatenate([lo, hi], axis=1)
        acc = acc + jnp.dot(lhs, probe_ref[t], preferred_element_type=jnp.float32)
    return acc.reshape(block, width, sk)


def sketch_kernel(
    n_chips, m_ref, probe_ref, out_ref, gram_out, half_send, core_buf, chip_send, chip_recv,
    core_send, core_recv, rs_send, rs_recv, ag_send, ag_recv, back_sems, back_recv, gram_mine, gram_peer, gram_sems,
):
    me = lax.axis_index("in")
    core = lax.rem(me, 2)
    chip = me // 2
    partner = me + 1 - 2 * core
    rows = out_ref.shape[0]
    half = rows // 2
    piece = half // n_chips
    my_half = core * half
    other_half = (1 - core) * half

    def chip_dev(k):
        return k * 2 + core

    def chunk_of(step):
        return lax.rem(chip + step + 1, n_chips)

    def core_copy(step):
        c = chunk_of(step)
        return pltpu.make_async_remote_copy(
            src_ref=half_send.at[pl.ds(c * piece, piece)],
            dst_ref=core_buf.at[pl.ds(c * piece, piece)],
            send_sem=core_send.at[step],
            recv_sem=core_recv.at[step],
            device_id={"in": partner},
            device_id_type=MESH,
        )

    def rs_copy(step):
        c = chunk_of(step)
        return pltpu.make_async_remote_copy(
            src_ref=chip_send.at[pl.ds(c * piece, piece)],
            dst_ref=chip_recv.at[chip],
            send_sem=rs_send.at[step],
            recv_sem=rs_recv.at[step],
            device_id={"in": chip_dev(c)},
            device_id_type=MESH,
        )

    barrier = pltpu.get_barrier_semaphore()
    pl.semaphore_signal(barrier, inc=1, device_id={"in": partner}, device_id_type=MESH)
    for d in range(1, n_chips):
        pl.semaphore_signal(barrier, inc=1, device_id={"in": chip_dev(lax.rem(chip + d, n_chips))}, device_id_type=MESH)
    pl.semaphore_wait(barrier, n_chips)

    def partner_rows(step, carry):
        c = chunk_of(step)
        half_send[pl.ds(c * piece, piece)] = forward_rows(m_ref, probe_ref, other_half + c * piece, piece).astype(
            half_send.dtype
        )
        core_copy(step).start()
        return carry

    lax.fori_loop(0, n_chips, partner_rows, 0)

    def own_rows(step):
        c = chunk_of(step)
        mine = forward_rows(m_ref, probe_ref, my_half + c * piece, piece)
        core_copy(step).wait_recv()
        chip_send[pl.ds(c * piece, piece)] = (mine + core_buf[pl.ds(c * piece, piece)].astype(jnp.float32)).astype(
            chip_send.dtype
        )

    def chip_rows(step, carry):
        own_rows(step)
        rs_copy(step).start()
        return carry

    lax.fori_loop(0, n_chips - 1, chip_rows, 0)
    own_rows(n_chips - 1)

    for step in range(n_chips - 1):
        rs_copy(step).wait_recv()
    base_row = my_half + chip * piece
    for q in range(piece):
        acc = chip_send[chip * piece + q].astype(jnp.float32)
        for d in range(1, n_chips):
            acc = acc + chip_recv[lax.rem(chip + d, n_chips), q].astype(jnp.float32)
        out_ref[base_row + q] = acc.astype(out_ref.dtype)

    def ag_copy(d):
        return pltpu.make_async_remote_copy(
            src_ref=out_ref.at[pl.ds(base_row, piece)],
            dst_ref=out_ref.at[pl.ds(base_row, piece)],
            send_sem=ag_send.at[d],
            recv_sem=ag_recv.at[d],
            device_id={"in": chip_dev(lax.rem(chip + d, n_chips))},
            device_id_type=MESH,
        )

    def forward_copy(d):
        start = my_half + lax.rem(chip + n_chips - d, n_chips) * piece
        return pltpu.make_async_remote_copy(
            src_ref=out_ref.at[pl.ds(start, piece)],
            dst_ref=out_ref.at[pl.ds(start, piece)],
            send_sem=back_sems.at[d],
            recv_sem=back_recv.at[d],
            device_id={"in": partner},
            device_id_type=MESH,
        )

    def gram_of(start, acc):
        for q in range(piece):
            value = out_ref[start + q]
            acc = acc + lax.dot_general(value, value, (((0,), (0,)), ((), ())), preferred_element_type=jnp.float32)
        return acc

    forward_copy(0).start()
    for d in range(1, n_chips):
        ag_copy(d).start()
    sk = out_ref.shape[2]
    gram = gram_of(base_row, jnp.zeros((sk, sk), jnp.float32))
    for d in range(1, n_chips):
        ag_copy(d).wait_recv()
        forward_copy(d).start()
        gram = gram_of(my_half + lax.rem(chip + n_chips - d, n_chips) * piece, gram)
    gram_mine[...] = gram
    gram_copy = pltpu.make_async_remote_copy(
        src_ref=gram_mine,
        dst_ref=gram_peer,
        send_sem=gram_sems.at[0],
        recv_sem=gram_sems.at[1],
        device_id={"in": partner},
        device_id_type=MESH,
    )
    gram_copy.start()
    gram_copy.wait()
    gram_out[...] = (gram_mine[...] + gram_peer[...]).astype(gram_out.dtype)
    for step in range(n_chips):
        core_copy(step).wait_send()
    for step in range(n_chips - 1):
        rs_copy(step).wait_send()
    for d in range(1, n_chips):
        ag_copy(d).wait_send()
    for d in range(n_chips):
        forward_copy(d).wait()


def sketch_of(masked, probe_pairs, rows, n_in, cid):
    width = masked.shape[1]
    sk = probe_pairs.shape[2]
    n_chips = n_in // 2
    half = rows // 2
    return pl.pallas_call(
        functools.partial(sketch_kernel, n_chips),
        out_shape=(
            jax.ShapeDtypeStruct((rows, width, sk), jnp.bfloat16),
            jax.ShapeDtypeStruct((sk, sk), jnp.bfloat16),
        ),
        in_specs=[pl.BlockSpec(memory_space=pltpu.VMEM)] * 2,
        out_specs=(pl.BlockSpec(memory_space=pltpu.VMEM),) * 2,
        scratch_shapes=[
            pltpu.VMEM((half, width, sk), jnp.bfloat16),
            pltpu.VMEM((half, width, sk), jnp.bfloat16),
            pltpu.VMEM((half, width, sk), jnp.bfloat16),
            pltpu.VMEM((n_chips, half // n_chips, width, sk), jnp.bfloat16),
            pltpu.SemaphoreType.DMA((n_chips,)),
            pltpu.SemaphoreType.DMA((n_chips,)),
            pltpu.SemaphoreType.DMA((n_chips,)),
            pltpu.SemaphoreType.DMA((n_chips,)),
            pltpu.SemaphoreType.DMA((n_chips,)),
            pltpu.SemaphoreType.DMA((n_chips,)),
            pltpu.SemaphoreType.DMA((n_chips,)),
            pltpu.SemaphoreType.DMA((n_chips,)),
            pltpu.VMEM((sk, sk), jnp.float32),
            pltpu.VMEM((sk, sk), jnp.float32),
            pltpu.SemaphoreType.DMA((2,)),
        ],
        compiler_params=pltpu.CompilerParams(
            collective_id=cid, has_side_effects=True, vmem_limit_bytes=60 * 1024 * 1024
        ),
    )(masked, probe_pairs)


def corange_kernel(
    n_out, scale, mt_ref, sketch_ref, gram_ref, co_out, gram_out, recv_ref, gram_recv, send_buf,
    co_send, co_recv, gram_send, gram_in, local_sems
):
    me = lax.axis_index("out")
    cols_all = send_buf.shape[1]
    m_width = mt_ref.shape[1]
    sk = sketch_ref.shape[2]
    rows = sketch_ref.shape[0]
    block = 4
    n_blocks = cols_all // (block * m_width)
    span = block * m_width
    per = sk // n_out

    barrier = pltpu.get_barrier_semaphore()
    for d in range(1, n_out):
        pl.semaphore_signal(barrier, inc=1, device_id={"out": lax.rem(me + d, n_out)}, device_id_type=MESH)
    pl.semaphore_wait(barrier, n_out - 1)

    def gram_copy(d):
        return pltpu.make_async_remote_copy(
            src_ref=gram_ref,
            dst_ref=gram_recv.at[me],
            send_sem=gram_send.at[d],
            recv_sem=gram_in.at[d],
            device_id={"out": lax.rem(me + d, n_out)},
            device_id_type=MESH,
        )

    gram_local = pltpu.make_async_copy(gram_ref, gram_recv.at[me], local_sems.at[n_blocks])
    gram_local.start()
    for d in range(1, n_out):
        gram_copy(d).start()

    def co_copy(d, b):
        k = lax.rem(me + d, n_out)
        return pltpu.make_async_remote_copy(
            src_ref=send_buf.at[pl.ds(pl.multiple_of(k * per, per), per), pl.ds(pl.multiple_of(b * span, span), span)],
            dst_ref=recv_ref.at[me, :, pl.ds(pl.multiple_of(b * span, span), span)],
            send_sem=co_send.at[d, b],
            recv_sem=co_recv.at[d, b],
            device_id={"out": k},
            device_id_type=MESH,
        )

    def local_copy(b):
        return pltpu.make_async_copy(
            send_buf.at[pl.ds(pl.multiple_of(me * per, per), per), pl.ds(pl.multiple_of(b * span, span), span)],
            recv_ref.at[me, :, pl.ds(pl.multiple_of(b * span, span), span)],
            local_sems.at[b],
        )

    def body(b, carry):
        j0 = b * block
        acc = jnp.zeros((span, sk), jnp.float32)
        for i in range(rows):
            lhs = mt_ref[pl.ds(j0 + i, block)].reshape(span, mt_ref.shape[2])
            acc = acc + jnp.dot(lhs, sketch_ref[i], preferred_element_type=jnp.float32)
        send_buf[:, pl.ds(pl.multiple_of(b * span, span), span)] = acc.T.astype(send_buf.dtype)
        local_copy(b).start()
        for d in range(1, n_out):
            co_copy(d, b).start()
        return carry

    lax.fori_loop(0, n_blocks, body, 0)

    def drain(b, carry):
        local_copy(b).wait()
        for d in range(1, n_out):
            co_copy(d, b).wait()
        return carry

    lax.fori_loop(0, n_blocks, drain, 0)
    gram_local.wait()
    for d in range(1, n_out):
        gram_copy(d).wait()
    gram_total = gram_recv[0].astype(jnp.float32)
    for k in range(1, n_out):
        gram_total = gram_total + gram_recv[k].astype(jnp.float32)
    gram_out[...] = gram_total * scale
    for j in range(co_out.shape[1]):
        lanes = slice(j * m_width, (j + 1) * m_width)
        co_total = recv_ref[0, :, lanes].astype(jnp.float32)
        for k in range(1, n_out):
            co_total = co_total + recv_ref[k, :, lanes].astype(jnp.float32)
        co_out[:, j, :] = co_total


def corange_of(mt, sketch, gram_part, cols, n_out, cid):
    m_width = mt.shape[1]
    sk = sketch.shape[2]
    n_blocks = cols // 4
    return pl.pallas_call(
        functools.partial(corange_kernel, n_out, 1.0 / (R * OUTPUT_CHANNELS)),
        out_shape=(
            jax.ShapeDtypeStruct((sk // n_out, cols, m_width), jnp.float32),
            jax.ShapeDtypeStruct(gram_part.shape, jnp.float32),
        ),
        in_specs=[pl.BlockSpec(memory_space=pltpu.VMEM)] * 3,
        out_specs=(pl.BlockSpec(memory_space=pltpu.VMEM),) * 2,
        scratch_shapes=[
            pltpu.VMEM((n_out, sk // n_out, cols * m_width), jnp.bfloat16),
            pltpu.VMEM((n_out,) + gram_part.shape, jnp.bfloat16),
            pltpu.VMEM((sk, cols * m_width), jnp.bfloat16),
            pltpu.SemaphoreType.DMA((n_out, n_blocks)),
            pltpu.SemaphoreType.DMA((n_out, n_blocks)),
            pltpu.SemaphoreType.DMA((n_out,)),
            pltpu.SemaphoreType.DMA((n_out,)),
            pltpu.SemaphoreType.DMA((n_blocks + 1,)),
        ],
        compiler_params=pltpu.CompilerParams(
            collective_id=cid, has_side_effects=True, vmem_limit_bytes=60 * 1024 * 1024
        ),
    )(mt, sketch, gram_part)


def shards(n_out, n_in, markov, probes, pattern):
    keeper = jnp.repeat(jnp.repeat(pattern, BO, axis=0), BI, axis=1).astype(jnp.bfloat16)
    masked, mt, gathered = prep(markov, keeper, probes, n_out, 0)
    panel = gathered.reshape((-1,) + probes.shape[1:])
    s_all, cols, m_width = panel.shape
    probe_pairs = jnp.swapaxes(panel.reshape(s_all, cols // 2, 2 * m_width), 0, 1).swapaxes(1, 2)
    sketch, local_gram = sketch_of(masked, probe_pairs, R, n_in, 1)
    co_sum, gram_matrix = corange_of(mt, sketch, local_gram, cols, n_out, 4)
    corange = co_sum
    return (sketch, corange, gram_matrix)


def solution(mesh):
    return jax.shard_map(
        functools.partial(shards, mesh.shape["out"], mesh.shape["in"]),
        mesh=mesh,
        in_specs=(P(None, "out", "in"), P("out", None, "in"), P("out", "in")),
        out_specs=(P(None, "out", None), P("out", None, "in"), P()),
        check_vma=False,
    )
```

```python
import functools

import jax
import jax.numpy as jnp
from jax import lax
from jax.experimental import pallas as pl
from jax.experimental.pallas import tpu as pltpu
from jax.sharding import PartitionSpec as P

OUTPUT_CHANNELS = 2048
BO = 64
BI = 128
R = 32
C = 32

MESH = pl.DeviceIdType.MESH


def forward_kernel(m_ref, probe_ref, out_ref):
    rows, width, sk = out_ref.shape
    steps = probe_ref.shape[0]
    m_width = m_ref.shape[2]
    block = 2

    def body(b, carry):
        i0 = b * block
        acc = jnp.zeros((block * width, sk), jnp.float32)
        for t in range(steps):
            lo = m_ref[pl.ds(i0 + 2 * t, block)].reshape(block * width, m_width)
            hi = m_ref[pl.ds(i0 + 2 * t + 1, block)].reshape(block * width, m_width)
            lhs = jnp.concatenate([lo, hi], axis=1)
            acc = acc + jnp.dot(lhs, probe_ref[t], preferred_element_type=jnp.float32)
        out_ref[pl.ds(i0, block)] = acc.reshape(block, width, sk)
        return carry

    lax.fori_loop(0, rows // block, body, 0)


def forward_panel(pair, probe_pairs, rows):
    width = pair.shape[1]
    sk = probe_pairs.shape[2]
    return pl.pallas_call(
        forward_kernel,
        out_shape=jax.ShapeDtypeStruct((rows, width, sk), jnp.float32),
        in_specs=[pl.BlockSpec(memory_space=pltpu.VMEM)] * 2,
        out_specs=pl.BlockSpec(memory_space=pltpu.VMEM),
        compiler_params=pltpu.CompilerParams(vmem_limit_bytes=60 * 1024 * 1024),
    )(pair, probe_pairs)


def backward_kernel(mt_ref, sketch_ref, out_ref):
    cols, m_width, sk = out_ref.shape
    rows = sketch_ref.shape[0]
    block = 4

    def body(b, carry):
        j0 = b * block
        acc = jnp.zeros((block * m_width, sk), jnp.float32)
        for i in range(rows):
            lhs = mt_ref[pl.ds(j0 + i, block)].reshape(block * m_width, mt_ref.shape[2])
            acc = acc + jnp.dot(lhs, sketch_ref[i], preferred_element_type=jnp.float32)
        out_ref[pl.ds(j0, block)] = acc.reshape(block, m_width, sk)
        return carry

    lax.fori_loop(0, cols // block, body, 0)


def prep_kernel(n_out, markov_ref, keeper_ref, probes_ref, masked_ref, mt_ref, pair_ref, gathered_ref, send_sem, recv_sem, local_sem):
    me = lax.axis_index("out")
    barrier = pltpu.get_barrier_semaphore()
    for d in range(1, n_out):
        pl.semaphore_signal(barrier, inc=1, device_id={"out": lax.rem(me + d, n_out)}, device_id_type=MESH)
    pl.semaphore_wait(barrier, n_out - 1)
    local = pltpu.make_async_copy(probes_ref, gathered_ref.at[me], local_sem)
    local.start()
    copies = []
    for d in range(1, n_out):
        copy = pltpu.make_async_remote_copy(
            src_ref=probes_ref,
            dst_ref=gathered_ref.at[me],
            send_sem=send_sem.at[d],
            recv_sem=recv_sem.at[d],
            device_id={"out": lax.rem(me + d, n_out)},
            device_id_type=MESH,
        )
        copy.start()
        copies.append(copy)

    keeper = keeper_ref[...]

    def body(k, carry):
        value = markov_ref[k] * keeper
        masked_ref[k] = value
        mt_ref[k] = value.astype(jnp.float32).T.astype(mt_ref.dtype)
        return carry

    lax.fori_loop(0, markov_ref.shape[0], body, 0)
    local.wait()
    for copy in copies:
        copy.wait()
    n_lag = gathered_ref.shape[1]
    m_width = gathered_ref.shape[3]
    for j in range(n_lag):
        block = gathered_ref[:, j].reshape(-1, m_width)
        pair_ref[j // 2, (j % 2) * m_width : (j % 2 + 1) * m_width, :] = (
            block.astype(jnp.float32).T.astype(pair_ref.dtype)
        )


def prep(markov, keeper, probes, n_out, cid):
    lags, width, m_width = markov.shape
    lag, per, pm = probes.shape
    return pl.pallas_call(
        functools.partial(prep_kernel, n_out),
        out_shape=(
            jax.ShapeDtypeStruct((lags, width, m_width), markov.dtype),
            jax.ShapeDtypeStruct((lags, m_width, width), markov.dtype),
            jax.ShapeDtypeStruct((lag // 2, 2 * pm, n_out * per), probes.dtype),
        ),
        in_specs=[pl.BlockSpec(memory_space=pltpu.VMEM)] * 3,
        out_specs=(pl.BlockSpec(memory_space=pltpu.VMEM),) * 3,
        scratch_shapes=[
            pltpu.VMEM((n_out,) + probes.shape, probes.dtype),
            pltpu.SemaphoreType.DMA((n_out,)),
            pltpu.SemaphoreType.DMA((n_out,)),
            pltpu.SemaphoreType.DMA(()),
        ],
        compiler_params=pltpu.CompilerParams(
            collective_id=cid, has_side_effects=True, vmem_limit_bytes=60 * 1024 * 1024
        ),
    )(markov, keeper, probes)


def backward_panel(mt, sketch, cols):
    m_width = mt.shape[1]
    sk = sketch.shape[2]
    return pl.pallas_call(
        backward_kernel,
        out_shape=jax.ShapeDtypeStruct((cols, m_width, sk), jnp.float32),
        in_specs=[pl.BlockSpec(memory_space=pltpu.VMEM)] * 2,
        out_specs=pl.BlockSpec(memory_space=pltpu.VMEM),
        compiler_params=pltpu.CompilerParams(vmem_limit_bytes=60 * 1024 * 1024),
    )(mt, sketch)


def exchange_kernel(axis, n, stride, gather, x_ref, y_ref, send_sem, recv_sem, local_sem):
    me = lax.axis_index(axis)
    pos = lax.rem(me // stride, n)
    base = me - pos * stride

    def member(k):
        return base + k * stride

    barrier = pltpu.get_barrier_semaphore()
    for d in range(1, n):
        peer = lax.rem(pos + d, n)
        pl.semaphore_signal(barrier, inc=1, device_id={axis: member(peer)}, device_id_type=MESH)
    pl.semaphore_wait(barrier, n - 1)

    own_src = x_ref if gather else x_ref.at[pos]
    local = pltpu.make_async_copy(own_src, y_ref.at[pos], local_sem)
    local.start()
    copies = []
    for d in range(1, n):
        peer = lax.rem(pos + d, n)
        src = x_ref if gather else x_ref.at[peer]
        copy = pltpu.make_async_remote_copy(
            src_ref=src,
            dst_ref=y_ref.at[pos],
            send_sem=send_sem.at[d],
            recv_sem=recv_sem.at[d],
            device_id={axis: member(peer)},
            device_id_type=MESH,
        )
        copy.start()
        copies.append(copy)
    local.wait()
    for copy in copies:
        copy.wait()


def exchange(x, axis, n, stride, gather, cid):
    out_shape = (n,) + (x.shape if gather else x.shape[1:])
    return pl.pallas_call(
        functools.partial(exchange_kernel, axis, n, stride, gather),
        out_shape=jax.ShapeDtypeStruct(out_shape, x.dtype),
        in_specs=[pl.BlockSpec(memory_space=pl.ANY)],
        out_specs=pl.BlockSpec(memory_space=pl.ANY),
        scratch_shapes=[
            pltpu.SemaphoreType.DMA((n,)),
            pltpu.SemaphoreType.DMA((n,)),
            pltpu.SemaphoreType.DMA(()),
        ],
        compiler_params=pltpu.CompilerParams(collective_id=cid, has_side_effects=True),
    )(x)


def sketch_sum_kernel(
    n_chips, raw_ref, out_ref, half_send, core_buf, chip_send, chip_recv, core_sems, rs_send, rs_recv, ag_send, ag_recv
):
    me = lax.axis_index("in")
    core = lax.rem(me, 2)
    chip = me // 2
    partner = me + 1 - 2 * core
    rows = raw_ref.shape[0]
    half = rows // 2
    piece = half // n_chips
    my_half = core * half

    def chip_dev(k):
        return k * 2 + core

    barrier = pltpu.get_barrier_semaphore()
    pl.semaphore_signal(barrier, inc=1, device_id={"in": partner}, device_id_type=MESH)
    for d in range(1, n_chips):
        peer = lax.rem(chip + d, n_chips)
        pl.semaphore_signal(barrier, inc=1, device_id={"in": chip_dev(peer)}, device_id_type=MESH)
    pl.semaphore_wait(barrier, n_chips)

    other_half = (1 - core) * half

    def to_send(r, carry):
        half_send[r] = raw_ref[other_half + r].astype(half_send.dtype)
        return carry

    lax.fori_loop(0, half, to_send, 0)
    core_copy = pltpu.make_async_remote_copy(
        src_ref=half_send,
        dst_ref=core_buf,
        send_sem=core_sems.at[0],
        recv_sem=core_sems.at[1],
        device_id={"in": partner},
        device_id_type=MESH,
    )
    core_copy.start()
    core_copy.wait()

    def add_core(r, carry):
        chip_send[r] = (raw_ref[my_half + r] + core_buf[r].astype(jnp.float32)).astype(chip_send.dtype)
        return carry

    lax.fori_loop(0, half, add_core, 0)
    scatter = []
    for d in range(1, n_chips):
        peer = lax.rem(chip + d, n_chips)
        copy = pltpu.make_async_remote_copy(
            src_ref=chip_send.at[pl.ds(peer * piece, piece)],
            dst_ref=chip_recv.at[chip],
            send_sem=rs_send.at[d],
            recv_sem=rs_recv.at[d],
            device_id={"in": chip_dev(peer)},
            device_id_type=MESH,
        )
        copy.start()
        scatter.append(copy)
    for copy in scatter:
        copy.wait()

    base_row = my_half + chip * piece
    for q in range(piece):
        acc = chip_send[chip * piece + q].astype(jnp.float32)
        for d in range(1, n_chips):
            acc = acc + chip_recv[lax.rem(chip + d, n_chips), q].astype(jnp.float32)
        out_ref[base_row + q] = acc.astype(out_ref.dtype)

    gather = []
    for d in range(1, n_chips):
        peer = lax.rem(chip + d, n_chips)
        copy = pltpu.make_async_remote_copy(
            src_ref=out_ref.at[pl.ds(base_row, piece)],
            dst_ref=out_ref.at[pl.ds(base_row, piece)],
            send_sem=ag_send.at[d],
            recv_sem=ag_recv.at[d],
            device_id={"in": chip_dev(peer)},
            device_id_type=MESH,
        )
        copy.start()
        gather.append(copy)
    for copy in gather:
        copy.wait()
    core_back = pltpu.make_async_remote_copy(
        src_ref=out_ref.at[pl.ds(my_half, half)],
        dst_ref=out_ref.at[pl.ds(my_half, half)],
        send_sem=core_sems.at[2],
        recv_sem=core_sems.at[3],
        device_id={"in": partner},
        device_id_type=MESH,
    )
    core_back.start()
    core_back.wait()


def sketch_sum(raw, n_in, cid):
    rows, width, sk = raw.shape
    n_chips = n_in // 2
    half = rows // 2
    return pl.pallas_call(
        functools.partial(sketch_sum_kernel, n_chips),
        out_shape=jax.ShapeDtypeStruct(raw.shape, jnp.bfloat16),
        in_specs=[pl.BlockSpec(memory_space=pltpu.VMEM)],
        out_specs=pl.BlockSpec(memory_space=pltpu.VMEM),
        scratch_shapes=[
            pltpu.VMEM((half, width, sk), jnp.bfloat16),
            pltpu.VMEM((half, width, sk), jnp.bfloat16),
            pltpu.VMEM((half, width, sk), jnp.bfloat16),
            pltpu.VMEM((n_chips, half // n_chips, width, sk), jnp.bfloat16),
            pltpu.SemaphoreType.DMA((4,)),
            pltpu.SemaphoreType.DMA((n_chips,)),
            pltpu.SemaphoreType.DMA((n_chips,)),
            pltpu.SemaphoreType.DMA((n_chips,)),
            pltpu.SemaphoreType.DMA((n_chips,)),
        ],
        compiler_params=pltpu.CompilerParams(
            collective_id=cid, has_side_effects=True, vmem_limit_bytes=60 * 1024 * 1024
        ),
    )(raw)


def forward_rows(m_ref, probe_ref, i0, block):
    width, m_width = m_ref.shape[1], m_ref.shape[2]
    sk = probe_ref.shape[2]
    acc = jnp.zeros((block * width, sk), jnp.float32)
    for t in range(probe_ref.shape[0]):
        lo = m_ref[pl.ds(i0 + 2 * t, block)].reshape(block * width, m_width)
        hi = m_ref[pl.ds(i0 + 2 * t + 1, block)].reshape(block * width, m_width)
        lhs = jnp.concatenate([lo, hi], axis=1)
        acc = acc + jnp.dot(lhs, probe_ref[t], preferred_element_type=jnp.float32)
    return acc.reshape(block, width, sk)


def sketch_kernel(
    n_chips, m_ref, probe_ref, out_ref, gram_out, half_send, core_buf, chip_send, chip_recv,
    core_send, core_recv, rs_send, rs_recv, ag_send, ag_recv, back_sems, back_recv, gram_mine, gram_peer, gram_sems,
):
    me = lax.axis_index("in")
    core = lax.rem(me, 2)
    chip = me // 2
    partner = me + 1 - 2 * core
    rows = out_ref.shape[0]
    half = rows // 2
    piece = half // n_chips
    my_half = core * half
    other_half = (1 - core) * half

    def chip_dev(k):
        return k * 2 + core

    def chunk_of(step):
        return lax.rem(chip + step + 1, n_chips)

    def core_copy(step):
        c = chunk_of(step)
        return pltpu.make_async_remote_copy(
            src_ref=half_send.at[pl.ds(c * piece, piece)],
            dst_ref=core_buf.at[pl.ds(c * piece, piece)],
            send_sem=core_send.at[step],
            recv_sem=core_recv.at[step],
            device_id={"in": partner},
            device_id_type=MESH,
        )

    def rs_copy(step):
        c = chunk_of(step)
        return pltpu.make_async_remote_copy(
            src_ref=chip_send.at[pl.ds(c * piece, piece)],
            dst_ref=chip_recv.at[chip],
            send_sem=rs_send.at[step],
            recv_sem=rs_recv.at[step],
            device_id={"in": chip_dev(c)},
            device_id_type=MESH,
        )

    barrier = pltpu.get_barrier_semaphore()
    pl.semaphore_signal(barrier, inc=1, device_id={"in": partner}, device_id_type=MESH)
    for d in range(1, n_chips):
        pl.semaphore_signal(barrier, inc=1, device_id={"in": chip_dev(lax.rem(chip + d, n_chips))}, device_id_type=MESH)
    pl.semaphore_wait(barrier, n_chips)

    def partner_rows(step, carry):
        c = chunk_of(step)
        half_send[pl.ds(c * piece, piece)] = forward_rows(m_ref, probe_ref, other_half + c * piece, piece).astype(
            half_send.dtype
        )
        core_copy(step).start()
        return carry

    lax.fori_loop(0, n_chips, partner_rows, 0)

    def own_rows(step):
        c = chunk_of(step)
        mine = forward_rows(m_ref, probe_ref, my_half + c * piece, piece)
        core_copy(step).wait_recv()
        chip_send[pl.ds(c * piece, piece)] = (mine + core_buf[pl.ds(c * piece, piece)].astype(jnp.float32)).astype(
            chip_send.dtype
        )

    def chip_rows(step, carry):
        own_rows(step)
        rs_copy(step).start()
        return carry

    lax.fori_loop(0, n_chips - 1, chip_rows, 0)
    own_rows(n_chips - 1)

    for step in range(n_chips - 1):
        rs_copy(step).wait_recv()
    base_row = my_half + chip * piece
    for q in range(piece):
        acc = chip_send[chip * piece + q].astype(jnp.float32)
        for d in range(1, n_chips):
            acc = acc + chip_recv[lax.rem(chip + d, n_chips), q].astype(jnp.float32)
        out_ref[base_row + q] = acc.astype(out_ref.dtype)

    def ag_copy(d):
        return pltpu.make_async_remote_copy(
            src_ref=out_ref.at[pl.ds(base_row, piece)],
            dst_ref=out_ref.at[pl.ds(base_row, piece)],
            send_sem=ag_send.at[d],
            recv_sem=ag_recv.at[d],
            device_id={"in": chip_dev(lax.rem(chip + d, n_chips))},
            device_id_type=MESH,
        )

    def forward_copy(d):
        start = my_half + lax.rem(chip + n_chips - d, n_chips) * piece
        return pltpu.make_async_remote_copy(
            src_ref=out_ref.at[pl.ds(start, piece)],
            dst_ref=out_ref.at[pl.ds(start, piece)],
            send_sem=back_sems.at[d],
            recv_sem=back_recv.at[d],
            device_id={"in": partner},
            device_id_type=MESH,
        )

    def gram_of(start, acc):
        for q in range(piece):
            value = out_ref[start + q]
            acc = acc + lax.dot_general(value, value, (((0,), (0,)), ((), ())), preferred_element_type=jnp.float32)
        return acc

    forward_copy(0).start()
    for d in range(1, n_chips):
        ag_copy(d).start()
    sk = out_ref.shape[2]
    gram = gram_of(base_row, jnp.zeros((sk, sk), jnp.float32))
    for d in range(1, n_chips):
        ag_copy(d).wait_recv()
        forward_copy(d).start()
        gram = gram_of(my_half + lax.rem(chip + n_chips - d, n_chips) * piece, gram)
    gram_mine[...] = gram
    gram_copy = pltpu.make_async_remote_copy(
        src_ref=gram_mine,
        dst_ref=gram_peer,
        send_sem=gram_sems.at[0],
        recv_sem=gram_sems.at[1],
        device_id={"in": partner},
        device_id_type=MESH,
    )
    gram_copy.start()
    gram_copy.wait()
    gram_out[...] = (gram_mine[...] + gram_peer[...]).astype(gram_out.dtype)
    for step in range(n_chips):
        core_copy(step).wait_send()
    for step in range(n_chips - 1):
        rs_copy(step).wait_send()
    for d in range(1, n_chips):
        ag_copy(d).wait_send()
    for d in range(n_chips):
        forward_copy(d).wait()


def sketch_of(masked, probe_pairs, rows, n_in, cid):
    width = masked.shape[1]
    sk = probe_pairs.shape[2]
    n_chips = n_in // 2
    half = rows // 2
    return pl.pallas_call(
        functools.partial(sketch_kernel, n_chips),
        out_shape=(
            jax.ShapeDtypeStruct((rows, width, sk), jnp.bfloat16),
            jax.ShapeDtypeStruct((sk, sk), jnp.bfloat16),
        ),
        in_specs=[pl.BlockSpec(memory_space=pltpu.VMEM)] * 2,
        out_specs=(pl.BlockSpec(memory_space=pltpu.VMEM),) * 2,
        scratch_shapes=[
            pltpu.VMEM((half, width, sk), jnp.bfloat16),
            pltpu.VMEM((half, width, sk), jnp.bfloat16),
            pltpu.VMEM((half, width, sk), jnp.bfloat16),
            pltpu.VMEM((n_chips, half // n_chips, width, sk), jnp.bfloat16),
            pltpu.SemaphoreType.DMA((n_chips,)),
            pltpu.SemaphoreType.DMA((n_chips,)),
            pltpu.SemaphoreType.DMA((n_chips,)),
            pltpu.SemaphoreType.DMA((n_chips,)),
            pltpu.SemaphoreType.DMA((n_chips,)),
            pltpu.SemaphoreType.DMA((n_chips,)),
            pltpu.SemaphoreType.DMA((n_chips,)),
            pltpu.SemaphoreType.DMA((n_chips,)),
            pltpu.VMEM((sk, sk), jnp.float32),
            pltpu.VMEM((sk, sk), jnp.float32),
            pltpu.SemaphoreType.DMA((2,)),
        ],
        compiler_params=pltpu.CompilerParams(
            collective_id=cid, has_side_effects=True, vmem_limit_bytes=60 * 1024 * 1024
        ),
    )(masked, probe_pairs)


def corange_kernel(
    n_out, scale, mt_ref, sketch_ref, gram_ref, co_out, gram_out, recv_ref, gram_recv, send_buf,
    co_send, co_recv, gram_send, gram_in, local_sems
):
    me = lax.axis_index("out")
    cols_all = send_buf.shape[1]
    m_width = mt_ref.shape[1]
    sk = sketch_ref.shape[2]
    rows = sketch_ref.shape[0]
    block = 4
    n_blocks = cols_all // (block * m_width)
    span = block * m_width
    per = sk // n_out

    barrier = pltpu.get_barrier_semaphore()
    for d in range(1, n_out):
        pl.semaphore_signal(barrier, inc=1, device_id={"out": lax.rem(me + d, n_out)}, device_id_type=MESH)
    pl.semaphore_wait(barrier, n_out - 1)

    def gram_copy(d):
        return pltpu.make_async_remote_copy(
            src_ref=gram_ref,
            dst_ref=gram_recv.at[me],
            send_sem=gram_send.at[d],
            recv_sem=gram_in.at[d],
            device_id={"out": lax.rem(me + d, n_out)},
            device_id_type=MESH,
        )

    gram_local = pltpu.make_async_copy(gram_ref, gram_recv.at[me], local_sems.at[n_blocks])
    gram_local.start()
    for d in range(1, n_out):
        gram_copy(d).start()

    def co_copy(d, b):
        k = lax.rem(me + d, n_out)
        return pltpu.make_async_remote_copy(
            src_ref=send_buf.at[pl.ds(pl.multiple_of(k * per, per), per), pl.ds(pl.multiple_of(b * span, span), span)],
            dst_ref=recv_ref.at[me, :, pl.ds(pl.multiple_of(b * span, span), span)],
            send_sem=co_send.at[d, b],
            recv_sem=co_recv.at[d, b],
            device_id={"out": k},
            device_id_type=MESH,
        )

    def local_copy(b):
        return pltpu.make_async_copy(
            send_buf.at[pl.ds(pl.multiple_of(me * per, per), per), pl.ds(pl.multiple_of(b * span, span), span)],
            recv_ref.at[me, :, pl.ds(pl.multiple_of(b * span, span), span)],
            local_sems.at[b],
        )

    def body(b, carry):
        j0 = b * block
        acc = jnp.zeros((span, sk), jnp.float32)
        for i in range(rows):
            lhs = mt_ref[pl.ds(j0 + i, block)].reshape(span, mt_ref.shape[2])
            acc = acc + jnp.dot(lhs, sketch_ref[i], preferred_element_type=jnp.float32)
        send_buf[:, pl.ds(pl.multiple_of(b * span, span), span)] = acc.T.astype(send_buf.dtype)
        local_copy(b).start()
        for d in range(1, n_out):
            co_copy(d, b).start()
        return carry

    lax.fori_loop(0, n_blocks, body, 0)

    def drain(b, carry):
        local_copy(b).wait()
        for d in range(1, n_out):
            co_copy(d, b).wait()
        return carry

    lax.fori_loop(0, n_blocks, drain, 0)
    gram_local.wait()
    for d in range(1, n_out):
        gram_copy(d).wait()
    gram_total = gram_recv[0].astype(jnp.float32)
    for k in range(1, n_out):
        gram_total = gram_total + gram_recv[k].astype(jnp.float32)
    gram_out[...] = gram_total * scale
    for j in range(co_out.shape[1]):
        lanes = slice(j * m_width, (j + 1) * m_width)
        co_total = recv_ref[0, :, lanes].astype(jnp.float32)
        for k in range(1, n_out):
            co_total = co_total + recv_ref[k, :, lanes].astype(jnp.float32)
        co_out[:, j, :] = co_total


def corange_of(mt, sketch, gram_part, cols, n_out, cid):
    m_width = mt.shape[1]
    sk = sketch.shape[2]
    n_blocks = cols // 4
    return pl.pallas_call(
        functools.partial(corange_kernel, n_out, 1.0 / (R * OUTPUT_CHANNELS)),
        out_shape=(
            jax.ShapeDtypeStruct((sk // n_out, cols, m_width), jnp.float32),
            jax.ShapeDtypeStruct(gram_part.shape, jnp.float32),
        ),
        in_specs=[pl.BlockSpec(memory_space=pltpu.VMEM)] * 3,
        out_specs=(pl.BlockSpec(memory_space=pltpu.VMEM),) * 2,
        scratch_shapes=[
            pltpu.VMEM((n_out, sk // n_out, cols * m_width), jnp.bfloat16),
            pltpu.VMEM((n_out,) + gram_part.shape, jnp.bfloat16),
            pltpu.VMEM((sk, cols * m_width), jnp.bfloat16),
            pltpu.SemaphoreType.DMA((n_out, n_blocks)),
            pltpu.SemaphoreType.DMA((n_out, n_blocks)),
            pltpu.SemaphoreType.DMA((n_out,)),
            pltpu.SemaphoreType.DMA((n_out,)),
            pltpu.SemaphoreType.DMA((n_blocks + 1,)),
        ],
        compiler_params=pltpu.CompilerParams(
            collective_id=cid, has_side_effects=True, vmem_limit_bytes=60 * 1024 * 1024
        ),
    )(mt, sketch, gram_part)


def shards(n_out, n_in, markov, probes, pattern):
    keeper = jnp.repeat(jnp.repeat(pattern, BO, axis=0), BI, axis=1).astype(jnp.bfloat16)
    s_local, cols, m_width = probes.shape
    masked, mt, probe_pairs = prep(markov, keeper, jnp.swapaxes(probes, 0, 1), n_out, 0)
    sketch, local_gram = sketch_of(masked, probe_pairs, R, n_in, 1)
    co_sum, gram_matrix = corange_of(mt, sketch, local_gram, cols, n_out, 4)
    corange = co_sum
    return (sketch, corange, gram_matrix)


def solution(mesh):
    return jax.shard_map(
        functools.partial(shards, mesh.shape["out"], mesh.shape["in"]),
        mesh=mesh,
        in_specs=(P(None, "out", "in"), P("out", None, "in"), P("out", "in")),
        out_specs=(P(None, "out", None), P("out", None, "in"), P()),
        check_vma=False,
    )
```

```python
import functools

import jax
import jax.numpy as jnp
from jax import lax
from jax.experimental import pallas as pl
from jax.experimental.pallas import tpu as pltpu
from jax.sharding import PartitionSpec as P

OUTPUT_CHANNELS = 2048
BO = 64
BI = 128
R = 32
C = 32

MESH = pl.DeviceIdType.MESH


def forward_kernel(m_ref, probe_ref, out_ref):
    rows, width, sk = out_ref.shape
    steps = probe_ref.shape[0]
    m_width = m_ref.shape[2]
    block = 2

    def body(b, carry):
        i0 = b * block
        acc = jnp.zeros((block * width, sk), jnp.float32)
        for t in range(steps):
            lo = m_ref[pl.ds(i0 + 2 * t, block)].reshape(block * width, m_width)
            hi = m_ref[pl.ds(i0 + 2 * t + 1, block)].reshape(block * width, m_width)
            lhs = jnp.concatenate([lo, hi], axis=1)
            acc = acc + jnp.dot(lhs, probe_ref[t], preferred_element_type=jnp.float32)
        out_ref[pl.ds(i0, block)] = acc.reshape(block, width, sk)
        return carry

    lax.fori_loop(0, rows // block, body, 0)


def forward_panel(pair, probe_pairs, rows):
    width = pair.shape[1]
    sk = probe_pairs.shape[2]
    return pl.pallas_call(
        forward_kernel,
        out_shape=jax.ShapeDtypeStruct((rows, width, sk), jnp.float32),
        in_specs=[pl.BlockSpec(memory_space=pltpu.VMEM)] * 2,
        out_specs=pl.BlockSpec(memory_space=pltpu.VMEM),
        compiler_params=pltpu.CompilerParams(vmem_limit_bytes=60 * 1024 * 1024),
    )(pair, probe_pairs)


def backward_kernel(mt_ref, sketch_ref, out_ref):
    cols, m_width, sk = out_ref.shape
    rows = sketch_ref.shape[0]
    block = 4

    def body(b, carry):
        j0 = b * block
        acc = jnp.zeros((block * m_width, sk), jnp.float32)
        for i in range(rows):
            lhs = mt_ref[pl.ds(j0 + i, block)].reshape(block * m_width, mt_ref.shape[2])
            acc = acc + jnp.dot(lhs, sketch_ref[i], preferred_element_type=jnp.float32)
        out_ref[pl.ds(j0, block)] = acc.reshape(block, m_width, sk)
        return carry

    lax.fori_loop(0, cols // block, body, 0)


def prep_kernel(n_out, markov_ref, pattern_ref, probes_ref, masked_ref, mt_ref, pair_ref, gathered_ref, local_t, send_sem, recv_sem, local_sem):
    me = lax.axis_index("out")
    barrier = pltpu.get_barrier_semaphore()
    for d in range(1, n_out):
        pl.semaphore_signal(barrier, inc=1, device_id={"out": lax.rem(me + d, n_out)}, device_id_type=MESH)
    pl.semaphore_wait(barrier, n_out - 1)
    for j in range(local_t.shape[0]):
        local_t[j] = probes_ref[:, j, :]
    local = pltpu.make_async_copy(local_t, gathered_ref.at[me], local_sem)
    local.start()
    copies = []
    for d in range(1, n_out):
        copy = pltpu.make_async_remote_copy(
            src_ref=local_t,
            dst_ref=gathered_ref.at[me],
            send_sem=send_sem.at[d],
            recv_sem=recv_sem.at[d],
            device_id={"out": lax.rem(me + d, n_out)},
            device_id_type=MESH,
        )
        copy.start()
        copies.append(copy)

    width, m_width = markov_ref.shape[1], markov_ref.shape[2]
    rows_per = width // pattern_ref.shape[0]
    keeper = jnp.concatenate(
        [jnp.full((rows_per, m_width), pattern_ref[q, 0].astype(jnp.float32), jnp.float32) for q in range(pattern_ref.shape[0])],
        axis=0,
    ).astype(markov_ref.dtype)

    def body(k, carry):
        value = markov_ref[k] * keeper
        masked_ref[k] = value
        mt_ref[k] = value.astype(jnp.float32).T.astype(mt_ref.dtype)
        return carry

    lax.fori_loop(0, markov_ref.shape[0], body, 0)
    local.wait()
    for copy in copies:
        copy.wait()
    n_lag = gathered_ref.shape[1]
    m_width = gathered_ref.shape[3]
    for j in range(n_lag):
        block = gathered_ref[:, j].reshape(-1, m_width)
        pair_ref[j // 2, (j % 2) * m_width : (j % 2 + 1) * m_width, :] = (
            block.astype(jnp.float32).T.astype(pair_ref.dtype)
        )


def prep(markov, pattern, probes, n_out, cid):
    lags, width, m_width = markov.shape
    per, lag, pm = probes.shape
    return pl.pallas_call(
        functools.partial(prep_kernel, n_out),
        out_shape=(
            jax.ShapeDtypeStruct((lags, width, m_width), markov.dtype),
            jax.ShapeDtypeStruct((lags, m_width, width), markov.dtype),
            jax.ShapeDtypeStruct((lag // 2, 2 * pm, n_out * per), probes.dtype),
        ),
        in_specs=[
            pl.BlockSpec(memory_space=pltpu.VMEM),
            pl.BlockSpec(memory_space=pltpu.SMEM),
            pl.BlockSpec(memory_space=pltpu.VMEM),
        ],
        out_specs=(pl.BlockSpec(memory_space=pltpu.VMEM),) * 3,
        scratch_shapes=[
            pltpu.VMEM((n_out, lag, per, pm), probes.dtype),
            pltpu.VMEM((lag, per, pm), probes.dtype),
            pltpu.SemaphoreType.DMA((n_out,)),
            pltpu.SemaphoreType.DMA((n_out,)),
            pltpu.SemaphoreType.DMA(()),
        ],
        compiler_params=pltpu.CompilerParams(
            collective_id=cid, has_side_effects=True, vmem_limit_bytes=60 * 1024 * 1024
        ),
    )(markov, pattern, probes)


def backward_panel(mt, sketch, cols):
    m_width = mt.shape[1]
    sk = sketch.shape[2]
    return pl.pallas_call(
        backward_kernel,
        out_shape=jax.ShapeDtypeStruct((cols, m_width, sk), jnp.float32),
        in_specs=[pl.BlockSpec(memory_space=pltpu.VMEM)] * 2,
        out_specs=pl.BlockSpec(memory_space=pltpu.VMEM),
        compiler_params=pltpu.CompilerParams(vmem_limit_bytes=60 * 1024 * 1024),
    )(mt, sketch)


def exchange_kernel(axis, n, stride, gather, x_ref, y_ref, send_sem, recv_sem, local_sem):
    me = lax.axis_index(axis)
    pos = lax.rem(me // stride, n)
    base = me - pos * stride

    def member(k):
        return base + k * stride

    barrier = pltpu.get_barrier_semaphore()
    for d in range(1, n):
        peer = lax.rem(pos + d, n)
        pl.semaphore_signal(barrier, inc=1, device_id={axis: member(peer)}, device_id_type=MESH)
    pl.semaphore_wait(barrier, n - 1)

    own_src = x_ref if gather else x_ref.at[pos]
    local = pltpu.make_async_copy(own_src, y_ref.at[pos], local_sem)
    local.start()
    copies = []
    for d in range(1, n):
        peer = lax.rem(pos + d, n)
        src = x_ref if gather else x_ref.at[peer]
        copy = pltpu.make_async_remote_copy(
            src_ref=src,
            dst_ref=y_ref.at[pos],
            send_sem=send_sem.at[d],
            recv_sem=recv_sem.at[d],
            device_id={axis: member(peer)},
            device_id_type=MESH,
        )
        copy.start()
        copies.append(copy)
    local.wait()
    for copy in copies:
        copy.wait()


def exchange(x, axis, n, stride, gather, cid):
    out_shape = (n,) + (x.shape if gather else x.shape[1:])
    return pl.pallas_call(
        functools.partial(exchange_kernel, axis, n, stride, gather),
        out_shape=jax.ShapeDtypeStruct(out_shape, x.dtype),
        in_specs=[pl.BlockSpec(memory_space=pl.ANY)],
        out_specs=pl.BlockSpec(memory_space=pl.ANY),
        scratch_shapes=[
            pltpu.SemaphoreType.DMA((n,)),
            pltpu.SemaphoreType.DMA((n,)),
            pltpu.SemaphoreType.DMA(()),
        ],
        compiler_params=pltpu.CompilerParams(collective_id=cid, has_side_effects=True),
    )(x)


def sketch_sum_kernel(
    n_chips, raw_ref, out_ref, half_send, core_buf, chip_send, chip_recv, core_sems, rs_send, rs_recv, ag_send, ag_recv
):
    me = lax.axis_index("in")
    core = lax.rem(me, 2)
    chip = me // 2
    partner = me + 1 - 2 * core
    rows = raw_ref.shape[0]
    half = rows // 2
    piece = half // n_chips
    my_half = core * half

    def chip_dev(k):
        return k * 2 + core

    barrier = pltpu.get_barrier_semaphore()
    pl.semaphore_signal(barrier, inc=1, device_id={"in": partner}, device_id_type=MESH)
    for d in range(1, n_chips):
        peer = lax.rem(chip + d, n_chips)
        pl.semaphore_signal(barrier, inc=1, device_id={"in": chip_dev(peer)}, device_id_type=MESH)
    pl.semaphore_wait(barrier, n_chips)

    other_half = (1 - core) * half

    def to_send(r, carry):
        half_send[r] = raw_ref[other_half + r].astype(half_send.dtype)
        return carry

    lax.fori_loop(0, half, to_send, 0)
    core_copy = pltpu.make_async_remote_copy(
        src_ref=half_send,
        dst_ref=core_buf,
        send_sem=core_sems.at[0],
        recv_sem=core_sems.at[1],
        device_id={"in": partner},
        device_id_type=MESH,
    )
    core_copy.start()
    core_copy.wait()

    def add_core(r, carry):
        chip_send[r] = (raw_ref[my_half + r] + core_buf[r].astype(jnp.float32)).astype(chip_send.dtype)
        return carry

    lax.fori_loop(0, half, add_core, 0)
    scatter = []
    for d in range(1, n_chips):
        peer = lax.rem(chip + d, n_chips)
        copy = pltpu.make_async_remote_copy(
            src_ref=chip_send.at[pl.ds(peer * piece, piece)],
            dst_ref=chip_recv.at[chip],
            send_sem=rs_send.at[d],
            recv_sem=rs_recv.at[d],
            device_id={"in": chip_dev(peer)},
            device_id_type=MESH,
        )
        copy.start()
        scatter.append(copy)
    for copy in scatter:
        copy.wait()

    base_row = my_half + chip * piece
    for q in range(piece):
        acc = chip_send[chip * piece + q].astype(jnp.float32)
        for d in range(1, n_chips):
            acc = acc + chip_recv[lax.rem(chip + d, n_chips), q].astype(jnp.float32)
        out_ref[base_row + q] = acc.astype(out_ref.dtype)

    gather = []
    for d in range(1, n_chips):
        peer = lax.rem(chip + d, n_chips)
        copy = pltpu.make_async_remote_copy(
            src_ref=out_ref.at[pl.ds(base_row, piece)],
            dst_ref=out_ref.at[pl.ds(base_row, piece)],
            send_sem=ag_send.at[d],
            recv_sem=ag_recv.at[d],
            device_id={"in": chip_dev(peer)},
            device_id_type=MESH,
        )
        copy.start()
        gather.append(copy)
    for copy in gather:
        copy.wait()
    core_back = pltpu.make_async_remote_copy(
        src_ref=out_ref.at[pl.ds(my_half, half)],
        dst_ref=out_ref.at[pl.ds(my_half, half)],
        send_sem=core_sems.at[2],
        recv_sem=core_sems.at[3],
        device_id={"in": partner},
        device_id_type=MESH,
    )
    core_back.start()
    core_back.wait()


def sketch_sum(raw, n_in, cid):
    rows, width, sk = raw.shape
    n_chips = n_in // 2
    half = rows // 2
    return pl.pallas_call(
        functools.partial(sketch_sum_kernel, n_chips),
        out_shape=jax.ShapeDtypeStruct(raw.shape, jnp.bfloat16),
        in_specs=[pl.BlockSpec(memory_space=pltpu.VMEM)],
        out_specs=pl.BlockSpec(memory_space=pltpu.VMEM),
        scratch_shapes=[
            pltpu.VMEM((half, width, sk), jnp.bfloat16),
            pltpu.VMEM((half, width, sk), jnp.bfloat16),
            pltpu.VMEM((half, width, sk), jnp.bfloat16),
            pltpu.VMEM((n_chips, half // n_chips, width, sk), jnp.bfloat16),
            pltpu.SemaphoreType.DMA((4,)),
            pltpu.SemaphoreType.DMA((n_chips,)),
            pltpu.SemaphoreType.DMA((n_chips,)),
            pltpu.SemaphoreType.DMA((n_chips,)),
            pltpu.SemaphoreType.DMA((n_chips,)),
        ],
        compiler_params=pltpu.CompilerParams(
            collective_id=cid, has_side_effects=True, vmem_limit_bytes=60 * 1024 * 1024
        ),
    )(raw)


def forward_rows(m_ref, probe_ref, i0, block):
    width, m_width = m_ref.shape[1], m_ref.shape[2]
    sk = probe_ref.shape[2]
    acc = jnp.zeros((block * width, sk), jnp.float32)
    for t in range(probe_ref.shape[0]):
        lo = m_ref[pl.ds(i0 + 2 * t, block)].reshape(block * width, m_width)
        hi = m_ref[pl.ds(i0 + 2 * t + 1, block)].reshape(block * width, m_width)
        lhs = jnp.concatenate([lo, hi], axis=1)
        acc = acc + jnp.dot(lhs, probe_ref[t], preferred_element_type=jnp.float32)
    return acc.reshape(block, width, sk)


def sketch_kernel(
    n_chips, m_ref, probe_ref, out_ref, gram_out, half_send, core_buf, chip_send, chip_recv,
    core_send, core_recv, rs_send, rs_recv, ag_send, ag_recv, back_sems, back_recv, gram_mine, gram_peer, gram_sems,
):
    me = lax.axis_index("in")
    core = lax.rem(me, 2)
    chip = me // 2
    partner = me + 1 - 2 * core
    rows = out_ref.shape[0]
    half = rows // 2
    piece = half // n_chips
    my_half = core * half
    other_half = (1 - core) * half

    def chip_dev(k):
        return k * 2 + core

    def chunk_of(step):
        return lax.rem(chip + step + 1, n_chips)

    def core_copy(step):
        c = chunk_of(step)
        return pltpu.make_async_remote_copy(
            src_ref=half_send.at[pl.ds(c * piece, piece)],
            dst_ref=core_buf.at[pl.ds(c * piece, piece)],
            send_sem=core_send.at[step],
            recv_sem=core_recv.at[step],
            device_id={"in": partner},
            device_id_type=MESH,
        )

    def rs_copy(step):
        c = chunk_of(step)
        return pltpu.make_async_remote_copy(
            src_ref=chip_send.at[pl.ds(c * piece, piece)],
            dst_ref=chip_recv.at[chip],
            send_sem=rs_send.at[step],
            recv_sem=rs_recv.at[step],
            device_id={"in": chip_dev(c)},
            device_id_type=MESH,
        )

    barrier = pltpu.get_barrier_semaphore()
    pl.semaphore_signal(barrier, inc=1, device_id={"in": partner}, device_id_type=MESH)
    for d in range(1, n_chips):
        pl.semaphore_signal(barrier, inc=1, device_id={"in": chip_dev(lax.rem(chip + d, n_chips))}, device_id_type=MESH)
    pl.semaphore_wait(barrier, n_chips)

    def partner_rows(step, carry):
        c = chunk_of(step)
        half_send[pl.ds(c * piece, piece)] = forward_rows(m_ref, probe_ref, other_half + c * piece, piece).astype(
            half_send.dtype
        )
        core_copy(step).start()
        return carry

    lax.fori_loop(0, n_chips, partner_rows, 0)

    def own_rows(step):
        c = chunk_of(step)
        mine = forward_rows(m_ref, probe_ref, my_half + c * piece, piece)
        core_copy(step).wait_recv()
        chip_send[pl.ds(c * piece, piece)] = (mine + core_buf[pl.ds(c * piece, piece)].astype(jnp.float32)).astype(
            chip_send.dtype
        )

    def chip_rows(step, carry):
        own_rows(step)
        rs_copy(step).start()
        return carry

    lax.fori_loop(0, n_chips - 1, chip_rows, 0)
    own_rows(n_chips - 1)

    for step in range(n_chips - 1):
        rs_copy(step).wait_recv()
    base_row = my_half + chip * piece
    for q in range(piece):
        acc = chip_send[chip * piece + q].astype(jnp.float32)
        for d in range(1, n_chips):
            acc = acc + chip_recv[lax.rem(chip + d, n_chips), q].astype(jnp.float32)
        out_ref[base_row + q] = acc.astype(out_ref.dtype)

    def ag_copy(d):
        return pltpu.make_async_remote_copy(
            src_ref=out_ref.at[pl.ds(base_row, piece)],
            dst_ref=out_ref.at[pl.ds(base_row, piece)],
            send_sem=ag_send.at[d],
            recv_sem=ag_recv.at[d],
            device_id={"in": chip_dev(lax.rem(chip + d, n_chips))},
            device_id_type=MESH,
        )

    def forward_copy(d):
        start = my_half + lax.rem(chip + n_chips - d, n_chips) * piece
        return pltpu.make_async_remote_copy(
            src_ref=out_ref.at[pl.ds(start, piece)],
            dst_ref=out_ref.at[pl.ds(start, piece)],
            send_sem=back_sems.at[d],
            recv_sem=back_recv.at[d],
            device_id={"in": partner},
            device_id_type=MESH,
        )

    def gram_of(start, acc):
        for q in range(piece):
            value = out_ref[start + q]
            acc = acc + lax.dot_general(value, value, (((0,), (0,)), ((), ())), preferred_element_type=jnp.float32)
        return acc

    forward_copy(0).start()
    for d in range(1, n_chips):
        ag_copy(d).start()
    sk = out_ref.shape[2]
    gram = gram_of(base_row, jnp.zeros((sk, sk), jnp.float32))
    for d in range(1, n_chips):
        ag_copy(d).wait_recv()
        forward_copy(d).start()
        gram = gram_of(my_half + lax.rem(chip + n_chips - d, n_chips) * piece, gram)
    gram_mine[...] = gram
    gram_copy = pltpu.make_async_remote_copy(
        src_ref=gram_mine,
        dst_ref=gram_peer,
        send_sem=gram_sems.at[0],
        recv_sem=gram_sems.at[1],
        device_id={"in": partner},
        device_id_type=MESH,
    )
    gram_copy.start()
    gram_copy.wait()
    gram_out[...] = (gram_mine[...] + gram_peer[...]).astype(gram_out.dtype)
    for step in range(n_chips):
        core_copy(step).wait_send()
    for step in range(n_chips - 1):
        rs_copy(step).wait_send()
    for d in range(1, n_chips):
        ag_copy(d).wait_send()
    for d in range(n_chips):
        forward_copy(d).wait()


def sketch_of(masked, probe_pairs, rows, n_in, cid):
    width = masked.shape[1]
    sk = probe_pairs.shape[2]
    n_chips = n_in // 2
    half = rows // 2
    return pl.pallas_call(
        functools.partial(sketch_kernel, n_chips),
        out_shape=(
            jax.ShapeDtypeStruct((rows, width, sk), jnp.bfloat16),
            jax.ShapeDtypeStruct((sk, sk), jnp.bfloat16),
        ),
        in_specs=[pl.BlockSpec(memory_space=pltpu.VMEM)] * 2,
        out_specs=(pl.BlockSpec(memory_space=pltpu.VMEM),) * 2,
        scratch_shapes=[
            pltpu.VMEM((half, width, sk), jnp.bfloat16),
            pltpu.VMEM((half, width, sk), jnp.bfloat16),
            pltpu.VMEM((half, width, sk), jnp.bfloat16),
            pltpu.VMEM((n_chips, half // n_chips, width, sk), jnp.bfloat16),
            pltpu.SemaphoreType.DMA((n_chips,)),
            pltpu.SemaphoreType.DMA((n_chips,)),
            pltpu.SemaphoreType.DMA((n_chips,)),
            pltpu.SemaphoreType.DMA((n_chips,)),
            pltpu.SemaphoreType.DMA((n_chips,)),
            pltpu.SemaphoreType.DMA((n_chips,)),
            pltpu.SemaphoreType.DMA((n_chips,)),
            pltpu.SemaphoreType.DMA((n_chips,)),
            pltpu.VMEM((sk, sk), jnp.float32),
            pltpu.VMEM((sk, sk), jnp.float32),
            pltpu.SemaphoreType.DMA((2,)),
        ],
        compiler_params=pltpu.CompilerParams(
            collective_id=cid, has_side_effects=True, vmem_limit_bytes=60 * 1024 * 1024
        ),
    )(masked, probe_pairs)


def corange_kernel(
    n_out, scale, mt_ref, sketch_ref, gram_ref, co_out, gram_out, recv_ref, gram_recv, send_buf,
    co_send, co_recv, gram_send, gram_in, local_sems
):
    me = lax.axis_index("out")
    cols_all = send_buf.shape[1]
    m_width = mt_ref.shape[1]
    sk = sketch_ref.shape[2]
    rows = sketch_ref.shape[0]
    block = 4
    n_blocks = cols_all // (block * m_width)
    span = block * m_width
    per = sk // n_out

    barrier = pltpu.get_barrier_semaphore()
    for d in range(1, n_out):
        pl.semaphore_signal(barrier, inc=1, device_id={"out": lax.rem(me + d, n_out)}, device_id_type=MESH)
    pl.semaphore_wait(barrier, n_out - 1)

    def gram_copy(d):
        return pltpu.make_async_remote_copy(
            src_ref=gram_ref,
            dst_ref=gram_recv.at[me],
            send_sem=gram_send.at[d],
            recv_sem=gram_in.at[d],
            device_id={"out": lax.rem(me + d, n_out)},
            device_id_type=MESH,
        )

    gram_local = pltpu.make_async_copy(gram_ref, gram_recv.at[me], local_sems.at[n_blocks])
    gram_local.start()
    for d in range(1, n_out):
        gram_copy(d).start()

    def co_copy(d, b):
        k = lax.rem(me + d, n_out)
        return pltpu.make_async_remote_copy(
            src_ref=send_buf.at[pl.ds(pl.multiple_of(k * per, per), per), pl.ds(pl.multiple_of(b * span, span), span)],
            dst_ref=recv_ref.at[me, :, pl.ds(pl.multiple_of(b * span, span), span)],
            send_sem=co_send.at[d, b],
            recv_sem=co_recv.at[d, b],
            device_id={"out": k},
            device_id_type=MESH,
        )

    def local_copy(b):
        return pltpu.make_async_copy(
            send_buf.at[pl.ds(pl.multiple_of(me * per, per), per), pl.ds(pl.multiple_of(b * span, span), span)],
            recv_ref.at[me, :, pl.ds(pl.multiple_of(b * span, span), span)],
            local_sems.at[b],
        )

    def body(b, carry):
        j0 = b * block
        acc = jnp.zeros((span, sk), jnp.float32)
        for i in range(rows):
            lhs = mt_ref[pl.ds(j0 + i, block)].reshape(span, mt_ref.shape[2])
            acc = acc + jnp.dot(lhs, sketch_ref[i], preferred_element_type=jnp.float32)
        send_buf[:, pl.ds(pl.multiple_of(b * span, span), span)] = acc.T.astype(send_buf.dtype)
        local_copy(b).start()
        for d in range(1, n_out):
            co_copy(d, b).start()
        return carry

    lax.fori_loop(0, n_blocks, body, 0)

    def drain(b, carry):
        local_copy(b).wait()
        for d in range(1, n_out):
            co_copy(d, b).wait()
        return carry

    lax.fori_loop(0, n_blocks, drain, 0)
    gram_local.wait()
    for d in range(1, n_out):
        gram_copy(d).wait()
    gram_total = gram_recv[0].astype(jnp.float32)
    for k in range(1, n_out):
        gram_total = gram_total + gram_recv[k].astype(jnp.float32)
    gram_out[...] = gram_total * scale
    for j in range(co_out.shape[1]):
        lanes = slice(j * m_width, (j + 1) * m_width)
        co_total = recv_ref[0, :, lanes].astype(jnp.float32)
        for k in range(1, n_out):
            co_total = co_total + recv_ref[k, :, lanes].astype(jnp.float32)
        co_out[:, j, :] = co_total


def corange_of(mt, sketch, gram_part, cols, n_out, cid):
    m_width = mt.shape[1]
    sk = sketch.shape[2]
    n_blocks = cols // 4
    return pl.pallas_call(
        functools.partial(corange_kernel, n_out, 1.0 / (R * OUTPUT_CHANNELS)),
        out_shape=(
            jax.ShapeDtypeStruct((sk // n_out, cols, m_width), jnp.float32),
            jax.ShapeDtypeStruct(gram_part.shape, jnp.float32),
        ),
        in_specs=[pl.BlockSpec(memory_space=pltpu.VMEM)] * 3,
        out_specs=(pl.BlockSpec(memory_space=pltpu.VMEM),) * 2,
        scratch_shapes=[
            pltpu.VMEM((n_out, sk // n_out, cols * m_width), jnp.bfloat16),
            pltpu.VMEM((n_out,) + gram_part.shape, jnp.bfloat16),
            pltpu.VMEM((sk, cols * m_width), jnp.bfloat16),
            pltpu.SemaphoreType.DMA((n_out, n_blocks)),
            pltpu.SemaphoreType.DMA((n_out, n_blocks)),
            pltpu.SemaphoreType.DMA((n_out,)),
            pltpu.SemaphoreType.DMA((n_out,)),
            pltpu.SemaphoreType.DMA((n_blocks + 1,)),
        ],
        compiler_params=pltpu.CompilerParams(
            collective_id=cid, has_side_effects=True, vmem_limit_bytes=60 * 1024 * 1024
        ),
    )(mt, sketch, gram_part)


def shards(n_out, n_in, markov, probes, pattern):
    s_local, cols, m_width = probes.shape
    masked, mt, probe_pairs = prep(markov, pattern, probes, n_out, 0)
    sketch, local_gram = sketch_of(masked, probe_pairs, R, n_in, 1)
    co_sum, gram_matrix = corange_of(mt, sketch, local_gram, cols, n_out, 4)
    corange = co_sum
    return (sketch, corange, gram_matrix)


def solution(mesh):
    return jax.shard_map(
        functools.partial(shards, mesh.shape["out"], mesh.shape["in"]),
        mesh=mesh,
        in_specs=(P(None, "out", "in"), P("out", None, "in"), P("out", "in")),
        out_specs=(P(None, "out", None), P("out", None, "in"), P()),
        check_vma=False,
    )
```

```python
import functools

import jax
import jax.numpy as jnp
from jax import lax
from jax.experimental import pallas as pl
from jax.experimental.pallas import tpu as pltpu
from jax.sharding import PartitionSpec as P

OUTPUT_CHANNELS = 2048
BO = 64
BI = 128
R = 32
C = 32

MESH = pl.DeviceIdType.MESH


def forward_kernel(m_ref, probe_ref, out_ref):
    rows, width, sk = out_ref.shape
    steps = probe_ref.shape[0]
    m_width = m_ref.shape[2]
    block = 2

    def body(b, carry):
        i0 = b * block
        acc = jnp.zeros((block * width, sk), jnp.float32)
        for t in range(steps):
            lo = m_ref[pl.ds(i0 + 2 * t, block)].reshape(block * width, m_width)
            hi = m_ref[pl.ds(i0 + 2 * t + 1, block)].reshape(block * width, m_width)
            lhs = jnp.concatenate([lo, hi], axis=1)
            acc = acc + jnp.dot(lhs, probe_ref[t], preferred_element_type=jnp.float32)
        out_ref[pl.ds(i0, block)] = acc.reshape(block, width, sk)
        return carry

    lax.fori_loop(0, rows // block, body, 0)


def forward_panel(pair, probe_pairs, rows):
    width = pair.shape[1]
    sk = probe_pairs.shape[2]
    return pl.pallas_call(
        forward_kernel,
        out_shape=jax.ShapeDtypeStruct((rows, width, sk), jnp.float32),
        in_specs=[pl.BlockSpec(memory_space=pltpu.VMEM)] * 2,
        out_specs=pl.BlockSpec(memory_space=pltpu.VMEM),
        compiler_params=pltpu.CompilerParams(vmem_limit_bytes=60 * 1024 * 1024),
    )(pair, probe_pairs)


def backward_kernel(mt_ref, sketch_ref, out_ref):
    cols, m_width, sk = out_ref.shape
    rows = sketch_ref.shape[0]
    block = 4

    def body(b, carry):
        j0 = b * block
        acc = jnp.zeros((block * m_width, sk), jnp.float32)
        for i in range(rows):
            lhs = mt_ref[pl.ds(j0 + i, block)].reshape(block * m_width, mt_ref.shape[2])
            acc = acc + jnp.dot(lhs, sketch_ref[i], preferred_element_type=jnp.float32)
        out_ref[pl.ds(j0, block)] = acc.reshape(block, m_width, sk)
        return carry

    lax.fori_loop(0, cols // block, body, 0)


def prep_kernel(n_out, markov_ref, pattern_ref, probes_ref, masked_ref, mt_ref, pair_ref, gathered_ref, local_t, send_sem, recv_sem, local_sem):
    me = lax.axis_index("out")
    barrier = pltpu.get_barrier_semaphore()
    for d in range(1, n_out):
        pl.semaphore_signal(barrier, inc=1, device_id={"out": lax.rem(me + d, n_out)}, device_id_type=MESH)
    for j in range(local_t.shape[0]):
        local_t[j] = probes_ref[:, j, :]
    pl.semaphore_wait(barrier, n_out - 1)
    local = pltpu.make_async_copy(local_t, gathered_ref.at[me], local_sem)
    local.start()
    copies = []
    for d in range(1, n_out):
        copy = pltpu.make_async_remote_copy(
            src_ref=local_t,
            dst_ref=gathered_ref.at[me],
            send_sem=send_sem.at[d],
            recv_sem=recv_sem.at[d],
            device_id={"out": lax.rem(me + d, n_out)},
            device_id_type=MESH,
        )
        copy.start()
        copies.append(copy)

    width, m_width = markov_ref.shape[1], markov_ref.shape[2]
    rows_per = width // pattern_ref.shape[0]
    keeper = jnp.concatenate(
        [jnp.full((rows_per, m_width), pattern_ref[q, 0].astype(jnp.float32), jnp.float32) for q in range(pattern_ref.shape[0])],
        axis=0,
    ).astype(markov_ref.dtype)

    def body(k, carry):
        value = markov_ref[k] * keeper
        masked_ref[k] = value
        mt_ref[k] = value.astype(jnp.float32).T.astype(mt_ref.dtype)
        return carry

    lax.fori_loop(0, markov_ref.shape[0], body, 0)
    local.wait()
    for copy in copies:
        copy.wait()
    n_lag = gathered_ref.shape[1]
    m_width = gathered_ref.shape[3]
    for j in range(n_lag):
        block = gathered_ref[:, j].reshape(-1, m_width)
        pair_ref[j // 2, (j % 2) * m_width : (j % 2 + 1) * m_width, :] = (
            block.astype(jnp.float32).T.astype(pair_ref.dtype)
        )


def prep(markov, pattern, probes, n_out, cid):
    lags, width, m_width = markov.shape
    per, lag, pm = probes.shape
    return pl.pallas_call(
        functools.partial(prep_kernel, n_out),
        out_shape=(
            jax.ShapeDtypeStruct((lags, width, m_width), markov.dtype),
            jax.ShapeDtypeStruct((lags, m_width, width), markov.dtype),
            jax.ShapeDtypeStruct((lag // 2, 2 * pm, n_out * per), probes.dtype),
        ),
        in_specs=[
            pl.BlockSpec(memory_space=pltpu.VMEM),
            pl.BlockSpec(memory_space=pltpu.SMEM),
            pl.BlockSpec(memory_space=pltpu.VMEM),
        ],
        out_specs=(pl.BlockSpec(memory_space=pltpu.VMEM),) * 3,
        scratch_shapes=[
            pltpu.VMEM((n_out, lag, per, pm), probes.dtype),
            pltpu.VMEM((lag, per, pm), probes.dtype),
            pltpu.SemaphoreType.DMA((n_out,)),
            pltpu.SemaphoreType.DMA((n_out,)),
            pltpu.SemaphoreType.DMA(()),
        ],
        compiler_params=pltpu.CompilerParams(
            collective_id=cid, has_side_effects=True, vmem_limit_bytes=60 * 1024 * 1024
        ),
    )(markov, pattern, probes)


def backward_panel(mt, sketch, cols):
    m_width = mt.shape[1]
    sk = sketch.shape[2]
    return pl.pallas_call(
        backward_kernel,
        out_shape=jax.ShapeDtypeStruct((cols, m_width, sk), jnp.float32),
        in_specs=[pl.BlockSpec(memory_space=pltpu.VMEM)] * 2,
        out_specs=pl.BlockSpec(memory_space=pltpu.VMEM),
        compiler_params=pltpu.CompilerParams(vmem_limit_bytes=60 * 1024 * 1024),
    )(mt, sketch)


def exchange_kernel(axis, n, stride, gather, x_ref, y_ref, send_sem, recv_sem, local_sem):
    me = lax.axis_index(axis)
    pos = lax.rem(me // stride, n)
    base = me - pos * stride

    def member(k):
        return base + k * stride

    barrier = pltpu.get_barrier_semaphore()
    for d in range(1, n):
        peer = lax.rem(pos + d, n)
        pl.semaphore_signal(barrier, inc=1, device_id={axis: member(peer)}, device_id_type=MESH)
    pl.semaphore_wait(barrier, n - 1)

    own_src = x_ref if gather else x_ref.at[pos]
    local = pltpu.make_async_copy(own_src, y_ref.at[pos], local_sem)
    local.start()
    copies = []
    for d in range(1, n):
        peer = lax.rem(pos + d, n)
        src = x_ref if gather else x_ref.at[peer]
        copy = pltpu.make_async_remote_copy(
            src_ref=src,
            dst_ref=y_ref.at[pos],
            send_sem=send_sem.at[d],
            recv_sem=recv_sem.at[d],
            device_id={axis: member(peer)},
            device_id_type=MESH,
        )
        copy.start()
        copies.append(copy)
    local.wait()
    for copy in copies:
        copy.wait()


def exchange(x, axis, n, stride, gather, cid):
    out_shape = (n,) + (x.shape if gather else x.shape[1:])
    return pl.pallas_call(
        functools.partial(exchange_kernel, axis, n, stride, gather),
        out_shape=jax.ShapeDtypeStruct(out_shape, x.dtype),
        in_specs=[pl.BlockSpec(memory_space=pl.ANY)],
        out_specs=pl.BlockSpec(memory_space=pl.ANY),
        scratch_shapes=[
            pltpu.SemaphoreType.DMA((n,)),
            pltpu.SemaphoreType.DMA((n,)),
            pltpu.SemaphoreType.DMA(()),
        ],
        compiler_params=pltpu.CompilerParams(collective_id=cid, has_side_effects=True),
    )(x)


def sketch_sum_kernel(
    n_chips, raw_ref, out_ref, half_send, core_buf, chip_send, chip_recv, core_sems, rs_send, rs_recv, ag_send, ag_recv
):
    me = lax.axis_index("in")
    core = lax.rem(me, 2)
    chip = me // 2
    partner = me + 1 - 2 * core
    rows = raw_ref.shape[0]
    half = rows // 2
    piece = half // n_chips
    my_half = core * half

    def chip_dev(k):
        return k * 2 + core

    barrier = pltpu.get_barrier_semaphore()
    pl.semaphore_signal(barrier, inc=1, device_id={"in": partner}, device_id_type=MESH)
    for d in range(1, n_chips):
        peer = lax.rem(chip + d, n_chips)
        pl.semaphore_signal(barrier, inc=1, device_id={"in": chip_dev(peer)}, device_id_type=MESH)
    pl.semaphore_wait(barrier, n_chips)

    other_half = (1 - core) * half

    def to_send(r, carry):
        half_send[r] = raw_ref[other_half + r].astype(half_send.dtype)
        return carry

    lax.fori_loop(0, half, to_send, 0)
    core_copy = pltpu.make_async_remote_copy(
        src_ref=half_send,
        dst_ref=core_buf,
        send_sem=core_sems.at[0],
        recv_sem=core_sems.at[1],
        device_id={"in": partner},
        device_id_type=MESH,
    )
    core_copy.start()
    core_copy.wait()

    def add_core(r, carry):
        chip_send[r] = (raw_ref[my_half + r] + core_buf[r].astype(jnp.float32)).astype(chip_send.dtype)
        return carry

    lax.fori_loop(0, half, add_core, 0)
    scatter = []
    for d in range(1, n_chips):
        peer = lax.rem(chip + d, n_chips)
        copy = pltpu.make_async_remote_copy(
            src_ref=chip_send.at[pl.ds(peer * piece, piece)],
            dst_ref=chip_recv.at[chip],
            send_sem=rs_send.at[d],
            recv_sem=rs_recv.at[d],
            device_id={"in": chip_dev(peer)},
            device_id_type=MESH,
        )
        copy.start()
        scatter.append(copy)
    for copy in scatter:
        copy.wait()

    base_row = my_half + chip * piece
    for q in range(piece):
        acc = chip_send[chip * piece + q].astype(jnp.float32)
        for d in range(1, n_chips):
            acc = acc + chip_recv[lax.rem(chip + d, n_chips), q].astype(jnp.float32)
        out_ref[base_row + q] = acc.astype(out_ref.dtype)

    gather = []
    for d in range(1, n_chips):
        peer = lax.rem(chip + d, n_chips)
        copy = pltpu.make_async_remote_copy(
            src_ref=out_ref.at[pl.ds(base_row, piece)],
            dst_ref=out_ref.at[pl.ds(base_row, piece)],
            send_sem=ag_send.at[d],
            recv_sem=ag_recv.at[d],
            device_id={"in": chip_dev(peer)},
            device_id_type=MESH,
        )
        copy.start()
        gather.append(copy)
    for copy in gather:
        copy.wait()
    core_back = pltpu.make_async_remote_copy(
        src_ref=out_ref.at[pl.ds(my_half, half)],
        dst_ref=out_ref.at[pl.ds(my_half, half)],
        send_sem=core_sems.at[2],
        recv_sem=core_sems.at[3],
        device_id={"in": partner},
        device_id_type=MESH,
    )
    core_back.start()
    core_back.wait()


def sketch_sum(raw, n_in, cid):
    rows, width, sk = raw.shape
    n_chips = n_in // 2
    half = rows // 2
    return pl.pallas_call(
        functools.partial(sketch_sum_kernel, n_chips),
        out_shape=jax.ShapeDtypeStruct(raw.shape, jnp.bfloat16),
        in_specs=[pl.BlockSpec(memory_space=pltpu.VMEM)],
        out_specs=pl.BlockSpec(memory_space=pltpu.VMEM),
        scratch_shapes=[
            pltpu.VMEM((half, width, sk), jnp.bfloat16),
            pltpu.VMEM((half, width, sk), jnp.bfloat16),
            pltpu.VMEM((half, width, sk), jnp.bfloat16),
            pltpu.VMEM((n_chips, half // n_chips, width, sk), jnp.bfloat16),
            pltpu.SemaphoreType.DMA((4,)),
            pltpu.SemaphoreType.DMA((n_chips,)),
            pltpu.SemaphoreType.DMA((n_chips,)),
            pltpu.SemaphoreType.DMA((n_chips,)),
            pltpu.SemaphoreType.DMA((n_chips,)),
        ],
        compiler_params=pltpu.CompilerParams(
            collective_id=cid, has_side_effects=True, vmem_limit_bytes=60 * 1024 * 1024
        ),
    )(raw)


def forward_rows(m_ref, probe_ref, i0, block):
    width, m_width = m_ref.shape[1], m_ref.shape[2]
    sk = probe_ref.shape[2]
    acc = jnp.zeros((block * width, sk), jnp.float32)
    for t in range(probe_ref.shape[0]):
        lo = m_ref[pl.ds(i0 + 2 * t, block)].reshape(block * width, m_width)
        hi = m_ref[pl.ds(i0 + 2 * t + 1, block)].reshape(block * width, m_width)
        lhs = jnp.concatenate([lo, hi], axis=1)
        acc = acc + jnp.dot(lhs, probe_ref[t], preferred_element_type=jnp.float32)
    return acc.reshape(block, width, sk)


def sketch_kernel(
    n_chips, m_ref, probe_ref, out_ref, gram_out, half_send, core_buf, chip_send, chip_recv,
    core_send, core_recv, rs_send, rs_recv, ag_send, ag_recv, back_sems, back_recv, gram_mine, gram_peer, gram_sems,
):
    me = lax.axis_index("in")
    core = lax.rem(me, 2)
    chip = me // 2
    partner = me + 1 - 2 * core
    rows = out_ref.shape[0]
    half = rows // 2
    piece = half // n_chips
    my_half = core * half
    other_half = (1 - core) * half

    def chip_dev(k):
        return k * 2 + core

    def chunk_of(step):
        return lax.rem(chip + step + 1, n_chips)

    def core_copy(step):
        c = chunk_of(step)
        return pltpu.make_async_remote_copy(
            src_ref=half_send.at[pl.ds(c * piece, piece)],
            dst_ref=core_buf.at[pl.ds(c * piece, piece)],
            send_sem=core_send.at[step],
            recv_sem=core_recv.at[step],
            device_id={"in": partner},
            device_id_type=MESH,
        )

    def rs_copy(step):
        c = chunk_of(step)
        return pltpu.make_async_remote_copy(
            src_ref=chip_send.at[pl.ds(c * piece, piece)],
            dst_ref=chip_recv.at[chip],
            send_sem=rs_send.at[step],
            recv_sem=rs_recv.at[step],
            device_id={"in": chip_dev(c)},
            device_id_type=MESH,
        )

    barrier = pltpu.get_barrier_semaphore()
    pl.semaphore_signal(barrier, inc=1, device_id={"in": partner}, device_id_type=MESH)
    for d in range(1, n_chips):
        pl.semaphore_signal(barrier, inc=1, device_id={"in": chip_dev(lax.rem(chip + d, n_chips))}, device_id_type=MESH)
    pl.semaphore_wait(barrier, n_chips)

    def partner_rows(step, carry):
        c = chunk_of(step)
        half_send[pl.ds(c * piece, piece)] = forward_rows(m_ref, probe_ref, other_half + c * piece, piece).astype(
            half_send.dtype
        )
        core_copy(step).start()
        return carry

    lax.fori_loop(0, n_chips, partner_rows, 0)

    def own_rows(step):
        c = chunk_of(step)
        mine = forward_rows(m_ref, probe_ref, my_half + c * piece, piece)
        core_copy(step).wait_recv()
        chip_send[pl.ds(c * piece, piece)] = (mine + core_buf[pl.ds(c * piece, piece)].astype(jnp.float32)).astype(
            chip_send.dtype
        )

    def chip_rows(step, carry):
        own_rows(step)
        rs_copy(step).start()
        return carry

    lax.fori_loop(0, n_chips - 1, chip_rows, 0)
    own_rows(n_chips - 1)

    for step in range(n_chips - 1):
        rs_copy(step).wait_recv()
    base_row = my_half + chip * piece
    for q in range(piece):
        acc = chip_send[chip * piece + q].astype(jnp.float32)
        for d in range(1, n_chips):
            acc = acc + chip_recv[lax.rem(chip + d, n_chips), q].astype(jnp.float32)
        out_ref[base_row + q] = acc.astype(out_ref.dtype)

    def ag_copy(d):
        return pltpu.make_async_remote_copy(
            src_ref=out_ref.at[pl.ds(base_row, piece)],
            dst_ref=out_ref.at[pl.ds(base_row, piece)],
            send_sem=ag_send.at[d],
            recv_sem=ag_recv.at[d],
            device_id={"in": chip_dev(lax.rem(chip + d, n_chips))},
            device_id_type=MESH,
        )

    def forward_copy(d):
        start = my_half + lax.rem(chip + n_chips - d, n_chips) * piece
        return pltpu.make_async_remote_copy(
            src_ref=out_ref.at[pl.ds(start, piece)],
            dst_ref=out_ref.at[pl.ds(start, piece)],
            send_sem=back_sems.at[d],
            recv_sem=back_recv.at[d],
            device_id={"in": partner},
            device_id_type=MESH,
        )

    def gram_of(start, acc):
        for q in range(piece):
            value = out_ref[start + q]
            acc = acc + lax.dot_general(value, value, (((0,), (0,)), ((), ())), preferred_element_type=jnp.float32)
        return acc

    forward_copy(0).start()
    for d in range(1, n_chips):
        ag_copy(d).start()
    sk = out_ref.shape[2]
    gram = gram_of(base_row, jnp.zeros((sk, sk), jnp.float32))
    for d in range(1, n_chips):
        ag_copy(d).wait_recv()
        forward_copy(d).start()
        gram = gram_of(my_half + lax.rem(chip + n_chips - d, n_chips) * piece, gram)
    gram_mine[...] = gram
    gram_copy = pltpu.make_async_remote_copy(
        src_ref=gram_mine,
        dst_ref=gram_peer,
        send_sem=gram_sems.at[0],
        recv_sem=gram_sems.at[1],
        device_id={"in": partner},
        device_id_type=MESH,
    )
    gram_copy.start()
    gram_copy.wait()
    gram_out[...] = (gram_mine[...] + gram_peer[...]).astype(gram_out.dtype)
    for step in range(n_chips):
        core_copy(step).wait_send()
    for step in range(n_chips - 1):
        rs_copy(step).wait_send()
    for d in range(1, n_chips):
        ag_copy(d).wait_send()
    for d in range(n_chips):
        forward_copy(d).wait()


def sketch_of(masked, probe_pairs, rows, n_in, cid):
    width = masked.shape[1]
    sk = probe_pairs.shape[2]
    n_chips = n_in // 2
    half = rows // 2
    return pl.pallas_call(
        functools.partial(sketch_kernel, n_chips),
        out_shape=(
            jax.ShapeDtypeStruct((rows, width, sk), jnp.bfloat16),
            jax.ShapeDtypeStruct((sk, sk), jnp.bfloat16),
        ),
        in_specs=[pl.BlockSpec(memory_space=pltpu.VMEM)] * 2,
        out_specs=(pl.BlockSpec(memory_space=pltpu.VMEM),) * 2,
        scratch_shapes=[
            pltpu.VMEM((half, width, sk), jnp.bfloat16),
            pltpu.VMEM((half, width, sk), jnp.bfloat16),
            pltpu.VMEM((half, width, sk), jnp.bfloat16),
            pltpu.VMEM((n_chips, half // n_chips, width, sk), jnp.bfloat16),
            pltpu.SemaphoreType.DMA((n_chips,)),
            pltpu.SemaphoreType.DMA((n_chips,)),
            pltpu.SemaphoreType.DMA((n_chips,)),
            pltpu.SemaphoreType.DMA((n_chips,)),
            pltpu.SemaphoreType.DMA((n_chips,)),
            pltpu.SemaphoreType.DMA((n_chips,)),
            pltpu.SemaphoreType.DMA((n_chips,)),
            pltpu.SemaphoreType.DMA((n_chips,)),
            pltpu.VMEM((sk, sk), jnp.float32),
            pltpu.VMEM((sk, sk), jnp.float32),
            pltpu.SemaphoreType.DMA((2,)),
        ],
        compiler_params=pltpu.CompilerParams(
            collective_id=cid, has_side_effects=True, vmem_limit_bytes=60 * 1024 * 1024
        ),
    )(masked, probe_pairs)


def corange_kernel(
    n_out, scale, mt_ref, sketch_ref, gram_ref, co_out, gram_out, recv_ref, gram_recv, send_buf,
    co_send, co_recv, gram_send, gram_in, local_sems
):
    me = lax.axis_index("out")
    cols_all = send_buf.shape[1]
    m_width = mt_ref.shape[1]
    sk = sketch_ref.shape[2]
    rows = sketch_ref.shape[0]
    block = 4
    n_blocks = cols_all // (block * m_width)
    span = block * m_width
    per = sk // n_out

    barrier = pltpu.get_barrier_semaphore()
    for d in range(1, n_out):
        pl.semaphore_signal(barrier, inc=1, device_id={"out": lax.rem(me + d, n_out)}, device_id_type=MESH)
    pl.semaphore_wait(barrier, n_out - 1)

    def gram_copy(d):
        return pltpu.make_async_remote_copy(
            src_ref=gram_ref,
            dst_ref=gram_recv.at[me],
            send_sem=gram_send.at[d],
            recv_sem=gram_in.at[d],
            device_id={"out": lax.rem(me + d, n_out)},
            device_id_type=MESH,
        )

    gram_local = pltpu.make_async_copy(gram_ref, gram_recv.at[me], local_sems.at[n_blocks])
    gram_local.start()
    for d in range(1, n_out):
        gram_copy(d).start()

    def co_copy(d, b):
        k = lax.rem(me + d, n_out)
        return pltpu.make_async_remote_copy(
            src_ref=send_buf.at[pl.ds(pl.multiple_of(k * per, per), per), pl.ds(pl.multiple_of(b * span, span), span)],
            dst_ref=recv_ref.at[me, :, pl.ds(pl.multiple_of(b * span, span), span)],
            send_sem=co_send.at[d, b],
            recv_sem=co_recv.at[d, b],
            device_id={"out": k},
            device_id_type=MESH,
        )

    def local_copy(b):
        return pltpu.make_async_copy(
            send_buf.at[pl.ds(pl.multiple_of(me * per, per), per), pl.ds(pl.multiple_of(b * span, span), span)],
            recv_ref.at[me, :, pl.ds(pl.multiple_of(b * span, span), span)],
            local_sems.at[b],
        )

    def body(b, carry):
        j0 = b * block
        acc = jnp.zeros((span, sk), jnp.float32)
        for i in range(rows):
            lhs = mt_ref[pl.ds(j0 + i, block)].reshape(span, mt_ref.shape[2])
            acc = acc + jnp.dot(lhs, sketch_ref[i], preferred_element_type=jnp.float32)
        send_buf[:, pl.ds(pl.multiple_of(b * span, span), span)] = acc.T.astype(send_buf.dtype)
        local_copy(b).start()
        for d in range(1, n_out):
            co_copy(d, b).start()
        return carry

    lax.fori_loop(0, n_blocks, body, 0)

    def drain(b, carry):
        local_copy(b).wait()
        for d in range(1, n_out):
            co_copy(d, b).wait()
        return carry

    lax.fori_loop(0, n_blocks, drain, 0)
    gram_local.wait()
    for d in range(1, n_out):
        gram_copy(d).wait()
    gram_total = gram_recv[0].astype(jnp.float32)
    for k in range(1, n_out):
        gram_total = gram_total + gram_recv[k].astype(jnp.float32)
    gram_out[...] = gram_total * scale
    for j in range(co_out.shape[1]):
        lanes = slice(j * m_width, (j + 1) * m_width)
        co_total = recv_ref[0, :, lanes].astype(jnp.float32)
        for k in range(1, n_out):
            co_total = co_total + recv_ref[k, :, lanes].astype(jnp.float32)
        co_out[:, j, :] = co_total


def corange_of(mt, sketch, gram_part, cols, n_out, cid):
    m_width = mt.shape[1]
    sk = sketch.shape[2]
    n_blocks = cols // 4
    return pl.pallas_call(
        functools.partial(corange_kernel, n_out, 1.0 / (R * OUTPUT_CHANNELS)),
        out_shape=(
            jax.ShapeDtypeStruct((sk // n_out, cols, m_width), jnp.float32),
            jax.ShapeDtypeStruct(gram_part.shape, jnp.float32),
        ),
        in_specs=[pl.BlockSpec(memory_space=pltpu.VMEM)] * 3,
        out_specs=(pl.BlockSpec(memory_space=pltpu.VMEM),) * 2,
        scratch_shapes=[
            pltpu.VMEM((n_out, sk // n_out, cols * m_width), jnp.bfloat16),
            pltpu.VMEM((n_out,) + gram_part.shape, jnp.bfloat16),
            pltpu.VMEM((sk, cols * m_width), jnp.bfloat16),
            pltpu.SemaphoreType.DMA((n_out, n_blocks)),
            pltpu.SemaphoreType.DMA((n_out, n_blocks)),
            pltpu.SemaphoreType.DMA((n_out,)),
            pltpu.SemaphoreType.DMA((n_out,)),
            pltpu.SemaphoreType.DMA((n_blocks + 1,)),
        ],
        compiler_params=pltpu.CompilerParams(
            collective_id=cid, has_side_effects=True, vmem_limit_bytes=60 * 1024 * 1024
        ),
    )(mt, sketch, gram_part)


def shards(n_out, n_in, markov, probes, pattern):
    s_local, cols, m_width = probes.shape
    masked, mt, probe_pairs = prep(markov, pattern, probes, n_out, 0)
    sketch, local_gram = sketch_of(masked, probe_pairs, R, n_in, 1)
    co_sum, gram_matrix = corange_of(mt, sketch, local_gram, cols, n_out, 4)
    corange = co_sum
    return (sketch, corange, gram_matrix)


def solution(mesh):
    return jax.shard_map(
        functools.partial(shards, mesh.shape["out"], mesh.shape["in"]),
        mesh=mesh,
        in_specs=(P(None, "out", "in"), P("out", None, "in"), P("out", "in")),
        out_specs=(P(None, "out", None), P("out", None, "in"), P()),
        check_vma=False,
    )
```

```python
import functools

import jax
import jax.numpy as jnp
from jax import lax
from jax.experimental import pallas as pl
from jax.experimental.pallas import tpu as pltpu
from jax.sharding import PartitionSpec as P

OUTPUT_CHANNELS = 2048
BO = 64
BI = 128
R = 32
C = 32

MESH = pl.DeviceIdType.MESH


def forward_kernel(m_ref, probe_ref, out_ref):
    rows, width, sk = out_ref.shape
    steps = probe_ref.shape[0]
    m_width = m_ref.shape[2]
    block = 2

    def body(b, carry):
        i0 = b * block
        acc = jnp.zeros((block * width, sk), jnp.float32)
        for t in range(steps):
            lo = m_ref[pl.ds(i0 + 2 * t, block)].reshape(block * width, m_width)
            hi = m_ref[pl.ds(i0 + 2 * t + 1, block)].reshape(block * width, m_width)
            lhs = jnp.concatenate([lo, hi], axis=1)
            acc = acc + jnp.dot(lhs, probe_ref[t], preferred_element_type=jnp.float32)
        out_ref[pl.ds(i0, block)] = acc.reshape(block, width, sk)
        return carry

    lax.fori_loop(0, rows // block, body, 0)


def forward_panel(pair, probe_pairs, rows):
    width = pair.shape[1]
    sk = probe_pairs.shape[2]
    return pl.pallas_call(
        forward_kernel,
        out_shape=jax.ShapeDtypeStruct((rows, width, sk), jnp.float32),
        in_specs=[pl.BlockSpec(memory_space=pltpu.VMEM)] * 2,
        out_specs=pl.BlockSpec(memory_space=pltpu.VMEM),
        compiler_params=pltpu.CompilerParams(vmem_limit_bytes=60 * 1024 * 1024),
    )(pair, probe_pairs)


def backward_kernel(mt_ref, sketch_ref, out_ref):
    cols, m_width, sk = out_ref.shape
    rows = sketch_ref.shape[0]
    block = 4

    def body(b, carry):
        j0 = b * block
        acc = jnp.zeros((block * m_width, sk), jnp.float32)
        for i in range(rows):
            lhs = mt_ref[pl.ds(j0 + i, block)].reshape(block * m_width, mt_ref.shape[2])
            acc = acc + jnp.dot(lhs, sketch_ref[i], preferred_element_type=jnp.float32)
        out_ref[pl.ds(j0, block)] = acc.reshape(block, m_width, sk)
        return carry

    lax.fori_loop(0, cols // block, body, 0)


def prep_kernel(n_out, markov_ref, pattern_ref, probes_ref, masked_ref, mt_ref, pair_ref, gathered_ref, local_t, send_sem, recv_sem, local_sem):
    me = lax.axis_index("out")
    barrier = pltpu.get_barrier_semaphore()
    for d in range(1, n_out):
        pl.semaphore_signal(barrier, inc=1, device_id={"out": lax.rem(me + d, n_out)}, device_id_type=MESH)
    for j in range(local_t.shape[0]):
        local_t[j] = probes_ref[:, j, :]
    pl.semaphore_wait(barrier, n_out - 1)
    local = pltpu.make_async_copy(local_t, gathered_ref.at[me], local_sem)
    local.start()
    copies = []
    for d in range(1, n_out):
        copy = pltpu.make_async_remote_copy(
            src_ref=local_t,
            dst_ref=gathered_ref.at[me],
            send_sem=send_sem.at[d],
            recv_sem=recv_sem.at[d],
            device_id={"out": lax.rem(me + d, n_out)},
            device_id_type=MESH,
        )
        copy.start()
        copies.append(copy)

    width, m_width = markov_ref.shape[1], markov_ref.shape[2]
    rows_per = width // pattern_ref.shape[0]
    keeper = jnp.concatenate(
        [jnp.full((rows_per, m_width), pattern_ref[q, 0].astype(jnp.float32), jnp.float32) for q in range(pattern_ref.shape[0])],
        axis=0,
    ).astype(markov_ref.dtype)

    def body(k, carry):
        value = markov_ref[k] * keeper
        masked_ref[k] = value
        mt_ref[k] = value.astype(jnp.float32).T.astype(mt_ref.dtype)
        return carry

    lax.fori_loop(0, markov_ref.shape[0], body, 0)
    local.wait()
    for copy in copies:
        copy.wait()
    n_lag = gathered_ref.shape[1]
    m_width = gathered_ref.shape[3]
    for j in range(n_lag):
        block = gathered_ref[:, j].reshape(-1, m_width)
        pair_ref[j // 2, (j % 2) * m_width : (j % 2 + 1) * m_width, :] = (
            block.astype(jnp.float32).T.astype(pair_ref.dtype)
        )


def prep(markov, pattern, probes, n_out, cid):
    lags, width, m_width = markov.shape
    per, lag, pm = probes.shape
    return pl.pallas_call(
        functools.partial(prep_kernel, n_out),
        out_shape=(
            jax.ShapeDtypeStruct((lags, width, m_width), markov.dtype),
            jax.ShapeDtypeStruct((lags, m_width, width), markov.dtype),
            jax.ShapeDtypeStruct((lag // 2, 2 * pm, n_out * per), probes.dtype),
        ),
        in_specs=[
            pl.BlockSpec(memory_space=pltpu.VMEM),
            pl.BlockSpec(memory_space=pltpu.SMEM),
            pl.BlockSpec(memory_space=pltpu.VMEM),
        ],
        out_specs=(pl.BlockSpec(memory_space=pltpu.VMEM),) * 3,
        scratch_shapes=[
            pltpu.VMEM((n_out, lag, per, pm), probes.dtype),
            pltpu.VMEM((lag, per, pm), probes.dtype),
            pltpu.SemaphoreType.DMA((n_out,)),
            pltpu.SemaphoreType.DMA((n_out,)),
            pltpu.SemaphoreType.DMA(()),
        ],
        compiler_params=pltpu.CompilerParams(
            collective_id=cid, has_side_effects=True, vmem_limit_bytes=60 * 1024 * 1024
        ),
    )(markov, pattern, probes)


def backward_panel(mt, sketch, cols):
    m_width = mt.shape[1]
    sk = sketch.shape[2]
    return pl.pallas_call(
        backward_kernel,
        out_shape=jax.ShapeDtypeStruct((cols, m_width, sk), jnp.float32),
        in_specs=[pl.BlockSpec(memory_space=pltpu.VMEM)] * 2,
        out_specs=pl.BlockSpec(memory_space=pltpu.VMEM),
        compiler_params=pltpu.CompilerParams(vmem_limit_bytes=60 * 1024 * 1024),
    )(mt, sketch)


def exchange_kernel(axis, n, stride, gather, x_ref, y_ref, send_sem, recv_sem, local_sem):
    me = lax.axis_index(axis)
    pos = lax.rem(me // stride, n)
    base = me - pos * stride

    def member(k):
        return base + k * stride

    barrier = pltpu.get_barrier_semaphore()
    for d in range(1, n):
        peer = lax.rem(pos + d, n)
        pl.semaphore_signal(barrier, inc=1, device_id={axis: member(peer)}, device_id_type=MESH)
    pl.semaphore_wait(barrier, n - 1)

    own_src = x_ref if gather else x_ref.at[pos]
    local = pltpu.make_async_copy(own_src, y_ref.at[pos], local_sem)
    local.start()
    copies = []
    for d in range(1, n):
        peer = lax.rem(pos + d, n)
        src = x_ref if gather else x_ref.at[peer]
        copy = pltpu.make_async_remote_copy(
            src_ref=src,
            dst_ref=y_ref.at[pos],
            send_sem=send_sem.at[d],
            recv_sem=recv_sem.at[d],
            device_id={axis: member(peer)},
            device_id_type=MESH,
        )
        copy.start()
        copies.append(copy)
    local.wait()
    for copy in copies:
        copy.wait()


def exchange(x, axis, n, stride, gather, cid):
    out_shape = (n,) + (x.shape if gather else x.shape[1:])
    return pl.pallas_call(
        functools.partial(exchange_kernel, axis, n, stride, gather),
        out_shape=jax.ShapeDtypeStruct(out_shape, x.dtype),
        in_specs=[pl.BlockSpec(memory_space=pl.ANY)],
        out_specs=pl.BlockSpec(memory_space=pl.ANY),
        scratch_shapes=[
            pltpu.SemaphoreType.DMA((n,)),
            pltpu.SemaphoreType.DMA((n,)),
            pltpu.SemaphoreType.DMA(()),
        ],
        compiler_params=pltpu.CompilerParams(collective_id=cid, has_side_effects=True),
    )(x)


def sketch_sum_kernel(
    n_chips, raw_ref, out_ref, half_send, core_buf, chip_send, chip_recv, core_sems, rs_send, rs_recv, ag_send, ag_recv
):
    me = lax.axis_index("in")
    core = lax.rem(me, 2)
    chip = me // 2
    partner = me + 1 - 2 * core
    rows = raw_ref.shape[0]
    half = rows // 2
    piece = half // n_chips
    my_half = core * half

    def chip_dev(k):
        return k * 2 + core

    barrier = pltpu.get_barrier_semaphore()
    pl.semaphore_signal(barrier, inc=1, device_id={"in": partner}, device_id_type=MESH)
    for d in range(1, n_chips):
        peer = lax.rem(chip + d, n_chips)
        pl.semaphore_signal(barrier, inc=1, device_id={"in": chip_dev(peer)}, device_id_type=MESH)
    pl.semaphore_wait(barrier, n_chips)

    other_half = (1 - core) * half

    def to_send(r, carry):
        half_send[r] = raw_ref[other_half + r].astype(half_send.dtype)
        return carry

    lax.fori_loop(0, half, to_send, 0)
    core_copy = pltpu.make_async_remote_copy(
        src_ref=half_send,
        dst_ref=core_buf,
        send_sem=core_sems.at[0],
        recv_sem=core_sems.at[1],
        device_id={"in": partner},
        device_id_type=MESH,
    )
    core_copy.start()
    core_copy.wait()

    def add_core(r, carry):
        chip_send[r] = (raw_ref[my_half + r] + core_buf[r].astype(jnp.float32)).astype(chip_send.dtype)
        return carry

    lax.fori_loop(0, half, add_core, 0)
    scatter = []
    for d in range(1, n_chips):
        peer = lax.rem(chip + d, n_chips)
        copy = pltpu.make_async_remote_copy(
            src_ref=chip_send.at[pl.ds(peer * piece, piece)],
            dst_ref=chip_recv.at[chip],
            send_sem=rs_send.at[d],
            recv_sem=rs_recv.at[d],
            device_id={"in": chip_dev(peer)},
            device_id_type=MESH,
        )
        copy.start()
        scatter.append(copy)
    for copy in scatter:
        copy.wait()

    base_row = my_half + chip * piece
    for q in range(piece):
        acc = chip_send[chip * piece + q].astype(jnp.float32)
        for d in range(1, n_chips):
            acc = acc + chip_recv[lax.rem(chip + d, n_chips), q].astype(jnp.float32)
        out_ref[base_row + q] = acc.astype(out_ref.dtype)

    gather = []
    for d in range(1, n_chips):
        peer = lax.rem(chip + d, n_chips)
        copy = pltpu.make_async_remote_copy(
            src_ref=out_ref.at[pl.ds(base_row, piece)],
            dst_ref=out_ref.at[pl.ds(base_row, piece)],
            send_sem=ag_send.at[d],
            recv_sem=ag_recv.at[d],
            device_id={"in": chip_dev(peer)},
            device_id_type=MESH,
        )
        copy.start()
        gather.append(copy)
    for copy in gather:
        copy.wait()
    core_back = pltpu.make_async_remote_copy(
        src_ref=out_ref.at[pl.ds(my_half, half)],
        dst_ref=out_ref.at[pl.ds(my_half, half)],
        send_sem=core_sems.at[2],
        recv_sem=core_sems.at[3],
        device_id={"in": partner},
        device_id_type=MESH,
    )
    core_back.start()
    core_back.wait()


def sketch_sum(raw, n_in, cid):
    rows, width, sk = raw.shape
    n_chips = n_in // 2
    half = rows // 2
    return pl.pallas_call(
        functools.partial(sketch_sum_kernel, n_chips),
        out_shape=jax.ShapeDtypeStruct(raw.shape, jnp.bfloat16),
        in_specs=[pl.BlockSpec(memory_space=pltpu.VMEM)],
        out_specs=pl.BlockSpec(memory_space=pltpu.VMEM),
        scratch_shapes=[
            pltpu.VMEM((half, width, sk), jnp.bfloat16),
            pltpu.VMEM((half, width, sk), jnp.bfloat16),
            pltpu.VMEM((half, width, sk), jnp.bfloat16),
            pltpu.VMEM((n_chips, half // n_chips, width, sk), jnp.bfloat16),
            pltpu.SemaphoreType.DMA((4,)),
            pltpu.SemaphoreType.DMA((n_chips,)),
            pltpu.SemaphoreType.DMA((n_chips,)),
            pltpu.SemaphoreType.DMA((n_chips,)),
            pltpu.SemaphoreType.DMA((n_chips,)),
        ],
        compiler_params=pltpu.CompilerParams(
            collective_id=cid, has_side_effects=True, vmem_limit_bytes=60 * 1024 * 1024
        ),
    )(raw)


def forward_rows(m_ref, probe_ref, i0, block):
    width, m_width = m_ref.shape[1], m_ref.shape[2]
    sk = probe_ref.shape[2]
    acc = jnp.zeros((block * width, sk), jnp.float32)
    for t in range(probe_ref.shape[0]):
        lo = m_ref[pl.ds(i0 + 2 * t, block)].reshape(block * width, m_width)
        hi = m_ref[pl.ds(i0 + 2 * t + 1, block)].reshape(block * width, m_width)
        lhs = jnp.concatenate([lo, hi], axis=1)
        acc = acc + jnp.dot(lhs, probe_ref[t], preferred_element_type=jnp.float32)
    return acc.reshape(block, width, sk)


def sketch_kernel(
    n_chips, m_ref, probe_ref, out_ref, gram_out, half_send, core_buf, chip_send, chip_recv,
    core_send, core_recv, rs_send, rs_recv, ag_send, ag_recv, back_sems, back_recv, gram_mine, gram_peer, gram_sems,
):
    me = lax.axis_index("in")
    core = lax.rem(me, 2)
    chip = me // 2
    partner = me + 1 - 2 * core
    rows = out_ref.shape[0]
    half = rows // 2
    piece = half // n_chips
    my_half = core * half
    other_half = (1 - core) * half

    def chip_dev(k):
        return k * 2 + core

    def chunk_of(step):
        return lax.rem(chip + step + 1, n_chips)

    def core_copy(step):
        c = chunk_of(step)
        return pltpu.make_async_remote_copy(
            src_ref=half_send.at[pl.ds(c * piece, piece)],
            dst_ref=core_buf.at[pl.ds(c * piece, piece)],
            send_sem=core_send.at[step],
            recv_sem=core_recv.at[step],
            device_id={"in": partner},
            device_id_type=MESH,
        )

    def rs_copy(step):
        c = chunk_of(step)
        return pltpu.make_async_remote_copy(
            src_ref=chip_send.at[pl.ds(c * piece, piece)],
            dst_ref=chip_recv.at[chip],
            send_sem=rs_send.at[step],
            recv_sem=rs_recv.at[step],
            device_id={"in": chip_dev(c)},
            device_id_type=MESH,
        )

    barrier = pltpu.get_barrier_semaphore()
    pl.semaphore_signal(barrier, inc=1, device_id={"in": partner}, device_id_type=MESH)
    for d in range(1, n_chips):
        pl.semaphore_signal(barrier, inc=1, device_id={"in": chip_dev(lax.rem(chip + d, n_chips))}, device_id_type=MESH)
    pl.semaphore_wait(barrier, n_chips)

    def partner_rows(step, carry):
        c = chunk_of(step)
        half_send[pl.ds(c * piece, piece)] = forward_rows(m_ref, probe_ref, other_half + c * piece, piece).astype(
            half_send.dtype
        )
        core_copy(step).start()
        return carry

    partner_rows(0, 0)
    partner_rows(1, 0)

    def own_rows(step):
        c = chunk_of(step)
        mine = forward_rows(m_ref, probe_ref, my_half + c * piece, piece)
        core_copy(step).wait_recv()
        chip_send[pl.ds(c * piece, piece)] = (mine + core_buf[pl.ds(c * piece, piece)].astype(jnp.float32)).astype(
            chip_send.dtype
        )

    def chip_rows(step, carry):
        own_rows(step)
        rs_copy(step).start()
        return carry

    def mixed(step, carry):
        chip_rows(step, carry)
        partner_rows(step + 2, carry)
        return carry

    lax.fori_loop(0, n_chips - 2, mixed, 0)
    chip_rows(n_chips - 2, 0)
    own_rows(n_chips - 1)

    for step in range(n_chips - 1):
        rs_copy(step).wait_recv()
    base_row = my_half + chip * piece
    for q in range(piece):
        acc = chip_send[chip * piece + q].astype(jnp.float32)
        for d in range(1, n_chips):
            acc = acc + chip_recv[lax.rem(chip + d, n_chips), q].astype(jnp.float32)
        out_ref[base_row + q] = acc.astype(out_ref.dtype)

    def ag_copy(d):
        return pltpu.make_async_remote_copy(
            src_ref=out_ref.at[pl.ds(base_row, piece)],
            dst_ref=out_ref.at[pl.ds(base_row, piece)],
            send_sem=ag_send.at[d],
            recv_sem=ag_recv.at[d],
            device_id={"in": chip_dev(lax.rem(chip + d, n_chips))},
            device_id_type=MESH,
        )

    def forward_copy(d):
        start = my_half + lax.rem(chip + n_chips - d, n_chips) * piece
        return pltpu.make_async_remote_copy(
            src_ref=out_ref.at[pl.ds(start, piece)],
            dst_ref=out_ref.at[pl.ds(start, piece)],
            send_sem=back_sems.at[d],
            recv_sem=back_recv.at[d],
            device_id={"in": partner},
            device_id_type=MESH,
        )

    def gram_of(start, acc):
        for q in range(piece):
            value = out_ref[start + q]
            acc = acc + lax.dot_general(value, value, (((0,), (0,)), ((), ())), preferred_element_type=jnp.float32)
        return acc

    forward_copy(0).start()
    for d in range(1, n_chips):
        ag_copy(d).start()
    sk = out_ref.shape[2]
    gram = gram_of(base_row, jnp.zeros((sk, sk), jnp.float32))
    for d in range(1, n_chips):
        ag_copy(d).wait_recv()
        forward_copy(d).start()
        gram = gram_of(my_half + lax.rem(chip + n_chips - d, n_chips) * piece, gram)
    gram_mine[...] = gram
    gram_copy = pltpu.make_async_remote_copy(
        src_ref=gram_mine,
        dst_ref=gram_peer,
        send_sem=gram_sems.at[0],
        recv_sem=gram_sems.at[1],
        device_id={"in": partner},
        device_id_type=MESH,
    )
    gram_copy.start()
    gram_copy.wait()
    gram_out[...] = (gram_mine[...] + gram_peer[...]).astype(gram_out.dtype)
    for step in range(n_chips):
        core_copy(step).wait_send()
    for step in range(n_chips - 1):
        rs_copy(step).wait_send()
    for d in range(1, n_chips):
        ag_copy(d).wait_send()
    for d in range(n_chips):
        forward_copy(d).wait()


def sketch_of(masked, probe_pairs, rows, n_in, cid):
    width = masked.shape[1]
    sk = probe_pairs.shape[2]
    n_chips = n_in // 2
    half = rows // 2
    return pl.pallas_call(
        functools.partial(sketch_kernel, n_chips),
        out_shape=(
            jax.ShapeDtypeStruct((rows, width, sk), jnp.bfloat16),
            jax.ShapeDtypeStruct((sk, sk), jnp.bfloat16),
        ),
        in_specs=[pl.BlockSpec(memory_space=pltpu.VMEM)] * 2,
        out_specs=(pl.BlockSpec(memory_space=pltpu.VMEM),) * 2,
        scratch_shapes=[
            pltpu.VMEM((half, width, sk), jnp.bfloat16),
            pltpu.VMEM((half, width, sk), jnp.bfloat16),
            pltpu.VMEM((half, width, sk), jnp.bfloat16),
            pltpu.VMEM((n_chips, half // n_chips, width, sk), jnp.bfloat16),
            pltpu.SemaphoreType.DMA((n_chips,)),
            pltpu.SemaphoreType.DMA((n_chips,)),
            pltpu.SemaphoreType.DMA((n_chips,)),
            pltpu.SemaphoreType.DMA((n_chips,)),
            pltpu.SemaphoreType.DMA((n_chips,)),
            pltpu.SemaphoreType.DMA((n_chips,)),
            pltpu.SemaphoreType.DMA((n_chips,)),
            pltpu.SemaphoreType.DMA((n_chips,)),
            pltpu.VMEM((sk, sk), jnp.float32),
            pltpu.VMEM((sk, sk), jnp.float32),
            pltpu.SemaphoreType.DMA((2,)),
        ],
        compiler_params=pltpu.CompilerParams(
            collective_id=cid, has_side_effects=True, vmem_limit_bytes=60 * 1024 * 1024
        ),
    )(masked, probe_pairs)


def corange_kernel(
    n_out, scale, mt_ref, sketch_ref, gram_ref, co_out, gram_out, recv_ref, gram_recv, send_buf,
    co_send, co_recv, gram_send, gram_in, local_sems
):
    me = lax.axis_index("out")
    cols_all = send_buf.shape[1]
    m_width = mt_ref.shape[1]
    sk = sketch_ref.shape[2]
    rows = sketch_ref.shape[0]
    block = 4
    n_blocks = cols_all // (block * m_width)
    span = block * m_width
    per = sk // n_out

    barrier = pltpu.get_barrier_semaphore()
    for d in range(1, n_out):
        pl.semaphore_signal(barrier, inc=1, device_id={"out": lax.rem(me + d, n_out)}, device_id_type=MESH)
    pl.semaphore_wait(barrier, n_out - 1)

    def gram_copy(d):
        return pltpu.make_async_remote_copy(
            src_ref=gram_ref,
            dst_ref=gram_recv.at[me],
            send_sem=gram_send.at[d],
            recv_sem=gram_in.at[d],
            device_id={"out": lax.rem(me + d, n_out)},
            device_id_type=MESH,
        )

    gram_local = pltpu.make_async_copy(gram_ref, gram_recv.at[me], local_sems.at[n_blocks])
    gram_local.start()
    for d in range(1, n_out):
        gram_copy(d).start()

    def co_copy(d, b):
        k = lax.rem(me + d, n_out)
        return pltpu.make_async_remote_copy(
            src_ref=send_buf.at[pl.ds(pl.multiple_of(k * per, per), per), pl.ds(pl.multiple_of(b * span, span), span)],
            dst_ref=recv_ref.at[me, :, pl.ds(pl.multiple_of(b * span, span), span)],
            send_sem=co_send.at[d, b],
            recv_sem=co_recv.at[d, b],
            device_id={"out": k},
            device_id_type=MESH,
        )

    def local_copy(b):
        return pltpu.make_async_copy(
            send_buf.at[pl.ds(pl.multiple_of(me * per, per), per), pl.ds(pl.multiple_of(b * span, span), span)],
            recv_ref.at[me, :, pl.ds(pl.multiple_of(b * span, span), span)],
            local_sems.at[b],
        )

    def body(b, carry):
        j0 = b * block
        acc = jnp.zeros((span, sk), jnp.float32)
        for i in range(rows):
            lhs = mt_ref[pl.ds(j0 + i, block)].reshape(span, mt_ref.shape[2])
            acc = acc + jnp.dot(lhs, sketch_ref[i], preferred_element_type=jnp.float32)
        send_buf[:, pl.ds(pl.multiple_of(b * span, span), span)] = acc.T.astype(send_buf.dtype)
        local_copy(b).start()
        for d in range(1, n_out):
            co_copy(d, b).start()
        return carry

    lax.fori_loop(0, n_blocks, body, 0)

    def drain(b, carry):
        local_copy(b).wait()
        for d in range(1, n_out):
            co_copy(d, b).wait()
        return carry

    lax.fori_loop(0, n_blocks, drain, 0)
    gram_local.wait()
    for d in range(1, n_out):
        gram_copy(d).wait()
    gram_total = gram_recv[0].astype(jnp.float32)
    for k in range(1, n_out):
        gram_total = gram_total + gram_recv[k].astype(jnp.float32)
    gram_out[...] = gram_total * scale
    for j in range(co_out.shape[1]):
        lanes = slice(j * m_width, (j + 1) * m_width)
        co_total = recv_ref[0, :, lanes].astype(jnp.float32)
        for k in range(1, n_out):
            co_total = co_total + recv_ref[k, :, lanes].astype(jnp.float32)
        co_out[:, j, :] = co_total


def corange_of(mt, sketch, gram_part, cols, n_out, cid):
    m_width = mt.shape[1]
    sk = sketch.shape[2]
    n_blocks = cols // 4
    return pl.pallas_call(
        functools.partial(corange_kernel, n_out, 1.0 / (R * OUTPUT_CHANNELS)),
        out_shape=(
            jax.ShapeDtypeStruct((sk // n_out, cols, m_width), jnp.float32),
            jax.ShapeDtypeStruct(gram_part.shape, jnp.float32),
        ),
        in_specs=[pl.BlockSpec(memory_space=pltpu.VMEM)] * 3,
        out_specs=(pl.BlockSpec(memory_space=pltpu.VMEM),) * 2,
        scratch_shapes=[
            pltpu.VMEM((n_out, sk // n_out, cols * m_width), jnp.bfloat16),
            pltpu.VMEM((n_out,) + gram_part.shape, jnp.bfloat16),
            pltpu.VMEM((sk, cols * m_width), jnp.bfloat16),
            pltpu.SemaphoreType.DMA((n_out, n_blocks)),
            pltpu.SemaphoreType.DMA((n_out, n_blocks)),
            pltpu.SemaphoreType.DMA((n_out,)),
            pltpu.SemaphoreType.DMA((n_out,)),
            pltpu.SemaphoreType.DMA((n_blocks + 1,)),
        ],
        compiler_params=pltpu.CompilerParams(
            collective_id=cid, has_side_effects=True, vmem_limit_bytes=60 * 1024 * 1024
        ),
    )(mt, sketch, gram_part)


def shards(n_out, n_in, markov, probes, pattern):
    s_local, cols, m_width = probes.shape
    masked, mt, probe_pairs = prep(markov, pattern, probes, n_out, 0)
    sketch, local_gram = sketch_of(masked, probe_pairs, R, n_in, 1)
    co_sum, gram_matrix = corange_of(mt, sketch, local_gram, cols, n_out, 4)
    corange = co_sum
    return (sketch, corange, gram_matrix)


def solution(mesh):
    return jax.shard_map(
        functools.partial(shards, mesh.shape["out"], mesh.shape["in"]),
        mesh=mesh,
        in_specs=(P(None, "out", "in"), P("out", None, "in"), P("out", "in")),
        out_specs=(P(None, "out", None), P("out", None, "in"), P()),
        check_vma=False,
    )
```
